32 devices in a mesh: dp: 8 (over y, x, core), mp: 4 (over z).
Axes of the slice: x: 2, y: 2, z: 4, core: 2. Of those that a mesh axis runs over, the one named last changes fastest.
Arguments:
- tokens: bfloat16 [16384, 768], P(('dp', 'mp')), may hold values from -6 to 6
- segment_ids: int32 [32, 512], P('dp'), may hold values from 0 to 7, never falling along the last dimension, each value on 1 to 128 neighbouring positions
- query_weight: bfloat16 [768, 768], P(None, 'mp'), may hold values from -0.21875 to 0.21875
- query_bias: bfloat16 [768], P('mp'), may hold values from -3 to 3
- key_weight: bfloat16 [768, 768], P(None, 'mp'), may hold values from -0.21875 to 0.21875
- value_weight: bfloat16 [768, 768], P(None, 'mp'), may hold values from -0.21875 to 0.21875
- value_bias: bfloat16 [768], P('mp'), may hold values from -3 to 3
- output_weight: bfloat16 [768, 768], P('mp'), may hold values from -0.875 to 0.875
- output_bias: bfloat16 [768], replicated, may hold values from -3 to 3
- first_gain: bfloat16 [768], replicated, may hold values from 0.25 to 1.75
- first_shift: bfloat16 [768], replicated, may hold values from -3 to 3
- up_weight: bfloat16 [768, 3072], P(None, 'mp'), may hold values from -0.21875 to 0.21875
- up_bias: bfloat16 [3072], P('mp'), may hold values from -3 to 3
- down_weight: bfloat16 [3072, 768], P('mp'), may hold values from -0.21875 to 0.21875
- down_bias: bfloat16 [768], replicated, may hold values from -3 to 3
- second_gain: bfloat16 [768], replicated, may hold values from 0.25 to 1.75
- second_shift: bfloat16 [768], replicated, may hold values from -3 to 3
- cotangent: bfloat16 [16384, 768], P(('dp', 'mp')), may hold values from -6 to 6
Outputs:
- output: bfloat16 [16384, 768], P(('dp', 'mp'))
- input_grad: bfloat16 [16384, 768], P(('dp', 'mp'))
- query_weight_grad: float32 [768, 768], P(None, 'mp')
- query_bias_grad: float32 [768], P('mp')
- key_weight_grad: float32 [768, 768], P(None, 'mp')
- value_weight_grad: float32 [768, 768], P(None, 'mp')
- value_bias_grad: float32 [768], P('mp')
- output_weight_grad: float32 [768, 768], P('mp')
- output_bias_grad: float32 [768], replicated
- first_gain_grad: float32 [768], replicated
- first_shift_grad: float32 [768], replicated
- up_weight_grad: float32 [768, 3072], P(None, 'mp')
- up_bias_grad: float32 [3072], P('mp')
- down_weight_grad: float32 [3072, 768], P('mp')
- down_bias_grad: float32 [768], replicated
- second_gain_grad: float32 [768], replicated
- second_shift_grad: float32 [768], replicated
The draws below stay inside these ranges and needn't reach their ends.
Inputs may be any that keep to these rules, and one draw needn't show every extreme that they name: `segment_ids`: along each row of 512 tokens the ids never fall; each passage holds 1 to 128 tokens, and some passage holds exactly 128.
All inputs are finite; a program needn't handle non-finite values.
Results may differ from the reference program's by a relative error of at most 0.023.
Values may be sent and summed in bfloat16 or wider, within the bound.
No kernel may reach another device: no remote copies, remote signals or barrier semaphores. Data moves between devices by JAX's collectives and lax.ppermute only.
A program may use at most 128 MiB of HBM per device.

```python
import math
import jax
import jax.numpy as jnp
import numpy as np
from jax import lax

D = 768
HEADS = 12
HEAD_DIM = 64
FF = 3072
SEQ = 512
PASSAGES = 8
PASSAGE_MAX = 128
ROWS = 32
TOKENS = 16384


def steps_of(stream_key, extent, shards, low, top_value):
    factor_of, own = 1.0, jax.random.fold_in(stream_key, 6)
    for axis_at, shards_of in shards:
        heights = jnp.exp(jax.random.uniform(jax.random.fold_in(own, axis_at), (shards_of,), jnp.float32, low / len(shards), top_value / len(shards)))
        factor_of = factor_of * jnp.repeat(heights, extent[axis_at] // shards_of).reshape([-1 if axis == axis_at else 1 for axis in range(len(extent))])
    return factor_of


def profile(count, total, bound, lean):
    weights = [(1 << 20) // math.isqrt(standing ** lean) + 1 for standing in range(2, count + 1)]
    spare, given = total - bound - (count - 1), [1] * (count - 1)
    while spare > 0:
        movable = [i for i in range(count - 1) if given[i] < bound]
        whole, budget = sum([weights[i] for i in movable]), spare
        for i in movable:
            extra = min(bound - given[i], max(1, budget * weights[i] // whole), spare)
            given[i] = given[i] + extra
            spare = spare - extra
    return np.array([bound] + given)


def ragged_sizes(rng, count, total, limit, skew):
    if count == 2:
        one = jax.random.randint(rng, (), max(1, total - limit), min(limit, total - 1) + 1)
        return jnp.stack([one, total - one])
    lengths = jnp.asarray(profile(count, total, limit, skew), jnp.int32)
    twos = (count - 1) // 2
    giver, sink = lengths[1:1 + 2 * twos:2], lengths[2:2 + 2 * twos:2]
    slack = jnp.minimum(giver - 1, limit - sink)
    moved = jax.random.randint(jax.random.fold_in(rng, 1), (twos,), 0, 1 << 20) % (slack + 1)
    lengths = lengths.at[1:1 + 2 * twos:2].set(giver - moved).at[2:2 + 2 * twos:2].set(sink + moved)
    return lengths[jax.random.permutation(jax.random.fold_in(rng, 2), count)]


def gaussian(rng, shape, scale, limit, shards=(), kind=jnp.bfloat16):
    values = scale * jax.random.normal(rng, shape, jnp.float32)
    if shards:
        values = values * steps_of(rng, shape, shards, -0.22, 0.18)
    return jnp.clip(values, -limit, limit).astype(kind)


def setup_inputs(seed: int = 0) -> dict:
    arg_keys = jax.random.split(jax.random.key(seed), 19)
    tokens = gaussian(arg_keys[0], (TOKENS, D), 1.0, 6.0, ((0, 32),))
    segment_ids = jax.vmap(lambda own: jnp.searchsorted(jnp.cumsum(ragged_sizes(own, PASSAGES, SEQ, PASSAGE_MAX, 2)), jnp.arange(SEQ), side="right"))(jax.random.split(arg_keys[1], ROWS)).reshape((ROWS, SEQ)).astype(jnp.int32)
    query_weight = gaussian(arg_keys[2], (D, D), D ** -0.5, 0.21875, ((1, 4),))
    query_bias = gaussian(arg_keys[3], (D,), 0.5, 3.0, ((0, 4),))
    key_weight = gaussian(arg_keys[4], (D, D), D ** -0.5, 0.21875, ((1, 4),))
    value_weight = gaussian(arg_keys[5], (D, D), D ** -0.5, 0.21875, ((1, 4),))
    value_bias = gaussian(arg_keys[6], (D,), 0.5, 3.0, ((0, 4),))
    output_weight = gaussian(arg_keys[7], (D, D), (D // 16) ** -0.5, 0.875, ((0, 4),))
    output_bias = gaussian(arg_keys[8], (D,), 0.5, 3.0)
    first_gain = jnp.clip(1.0 + 0.15 * jax.random.normal(arg_keys[9], (D,), jnp.float32), 0.25, 1.75).astype(jnp.bfloat16)
    first_shift = gaussian(arg_keys[10], (D,), 0.5, 3.0)
    up_weight = gaussian(arg_keys[11], (D, FF), D ** -0.5, 0.21875, ((1, 4),))
    up_bias = gaussian(arg_keys[12], (FF,), 0.5, 3.0, ((0, 4),))
    down_weight = gaussian(arg_keys[13], (FF, D), (FF // 4) ** -0.5, 0.21875, ((0, 4),))
    down_bias = gaussian(arg_keys[14], (D,), 0.5, 3.0)
    second_gain = jnp.clip(1.0 + 0.15 * jax.random.normal(arg_keys[15], (D,), jnp.float32), 0.25, 1.75).astype(jnp.bfloat16)
    second_shift = gaussian(arg_keys[16], (D,), 0.5, 3.0)
    cotangent = gaussian(arg_keys[17], (TOKENS, D), 1.0, 6.0, ((0, 32),))
    return dict(tokens=tokens, segment_ids=segment_ids, query_weight=query_weight, query_bias=query_bias, key_weight=key_weight, value_weight=value_weight, value_bias=value_bias, output_weight=output_weight, output_bias=output_bias, first_gain=first_gain, first_shift=first_shift, up_weight=up_weight, up_bias=up_bias, down_weight=down_weight, down_bias=down_bias, second_gain=second_gain, second_shift=second_shift, cotangent=cotangent)


@jax.custom_vjp
def low(v):
    return lax.optimization_barrier(v.astype(jnp.bfloat16)).astype(jnp.float32)

@jax.custom_vjp
def low_back(v):
    return v

def low_keep(v):
    return (low(v), None)

def low_pass(kept, grad):
    return (grad,)

def back_keep(v):
    return (v, None)

def back_low(kept, grad):
    return (low(grad),)
low.defvjp(low_keep, low_pass)
low_back.defvjp(back_keep, back_low)
epsilon = 1e-05
highest = lax.Precision.HIGHEST

def matmul(left, right):
    return jnp.dot(left, right, precision=highest)

def layer_norm(total, norm_gain, norm_shift):
    average = lax.optimization_barrier(jnp.mean(total, axis=-1, keepdims=True))
    centred = total - average
    variance = lax.optimization_barrier(jnp.mean(centred * centred, axis=-1, keepdims=True))
    return centred * lax.rsqrt(variance + epsilon) * norm_gain + norm_shift

def attend_row(pieces):
    queries, key_vecs, values, segment_row = pieces
    scale_factor = 1.0 / math.sqrt(HEAD_DIM)
    scores = jnp.einsum('qhd,khd->hqk', queries, key_vecs, precision=highest) * scale_factor
    scores = low_back(scores)
    allowed = segment_row[:, None] == segment_row[None, :]
    masked = jnp.where(allowed[None], scores, -1e+30)
    weights = low(jax.nn.softmax(masked, axis=-1))
    return jnp.einsum('hqk,khd->qhd', weights, values, precision=highest)

def block_forward(tokens, segment_rows, params):
    query_weight, query_bias, key_weight, value_weight, value_bias, output_weight, output_bias, first_gain, first_shift, up_weight, up_bias, down_weight, down_bias, second_gain, second_shift = params
    row_count = segment_rows.shape[0]
    queries = low(low_back(matmul(tokens, query_weight) + query_bias))
    key_vecs = low(low_back(matmul(tokens, key_weight)))
    values = low(low_back(matmul(tokens, value_weight) + value_bias))

    def by_heads(array):
        return array.reshape(row_count, SEQ, HEADS, HEAD_DIM)
    contexts = lax.map(jax.checkpoint(attend_row), (by_heads(queries), by_heads(key_vecs), by_heads(values), segment_rows))
    contexts = low(low_back(contexts.reshape(row_count * SEQ, D)))
    attended = low_back(matmul(contexts, output_weight) + output_bias)
    normed_one = layer_norm(tokens + attended, first_gain, first_shift)
    hidden = low_back(matmul(low(normed_one), up_weight) + up_bias)
    activated = low(jax.nn.gelu(hidden, approximate=False))
    mixed = low_back(matmul(activated, down_weight) + down_bias)
    return layer_norm(normed_one + mixed, second_gain, second_shift)

def reference(tokens, segment_ids, query_weight, query_bias, key_weight, value_weight, value_bias, output_weight, output_bias, first_gain, first_shift, up_weight, up_bias, down_weight, down_bias, second_gain, second_shift, cotangent):
    params = tuple((array.astype(jnp.float32) for array in (query_weight, query_bias, key_weight, value_weight, value_bias, output_weight, output_bias, first_gain, first_shift, up_weight, up_bias, down_weight, down_bias, second_gain, second_shift)))
    group = math.gcd(ROWS, 8)
    blocks = ROWS // group
    token_blocks = tokens.astype(jnp.float32).reshape(blocks, group * SEQ, D)
    segment_blocks = segment_ids.reshape(blocks, group, SEQ)
    cot_blocks = cotangent.astype(jnp.float32).reshape(blocks, group * SEQ, D)
    zero_grads = tuple((jnp.zeros_like(param) for param in params))

    def one_block(totals, pieces):
        token_block, segment_block, cot_block = pieces
        result, pullback = jax.vjp(lambda token_arg, param_args: block_forward(token_arg, segment_block, param_args), token_block, params)
        grad_tokens, grad_params = pullback(cot_block)
        totals = tuple((total + piece for total, piece in zip(totals, grad_params)))
        return (totals, (result.astype(jnp.bfloat16), grad_tokens.astype(jnp.bfloat16)))
    totals, (outputs, grad_inputs) = lax.scan(one_block, zero_grads, (token_blocks, segment_blocks, cot_blocks))
    return (outputs.reshape(TOKENS, D), grad_inputs.reshape(TOKENS, D), totals[0], totals[1], totals[2], totals[3], totals[4], totals[5], totals[6], totals[7], totals[8], totals[9], totals[10], totals[11], totals[12], totals[13], totals[14])
```

```python
import math

import jax
import jax.numpy as jnp
from jax import lax
from jax.sharding import PartitionSpec as P

HEAD_DIM = 64
GROUP = 8
epsilon = 1e-05
bf16 = jnp.bfloat16
f32 = jnp.float32


def inner_rows(left, right):
    return lax.dot_general(left, right, (((0,), (0,)), ((), ())), preferred_element_type=f32)


def norm_forward(total, norm_gain, norm_shift):
    average = jnp.mean(total, axis=-1, keepdims=True)
    centred = total - average
    inverse = lax.rsqrt(jnp.mean(centred * centred, axis=-1, keepdims=True) + epsilon)
    normal = centred * inverse
    return (normal * norm_gain + norm_shift, normal, inverse)


def norm_backward(grad_out, normal, inverse, norm_gain):
    scaled = grad_out * norm_gain
    return inverse * (
        scaled
        - jnp.mean(scaled, axis=-1, keepdims=True)
        - normal * jnp.mean(scaled * normal, axis=-1, keepdims=True)
    )


def gelu_slope(hidden):
    cumulative = 0.5 * (1.0 + lax.erf(hidden * 0.7071067811865476))
    density = jnp.exp(-0.5 * hidden * hidden) * 0.3989422804014327
    return cumulative + hidden * density


def masked_scores(queries, key_vecs, segment_row):
    scale_factor = 1.0 / math.sqrt(queries.shape[-1])
    scores = (
        jnp.einsum("qhd,khd->hqk", queries, key_vecs, preferred_element_type=f32) * scale_factor
    )
    allowed = segment_row[:, None] == segment_row[None, :]
    return jnp.where(allowed[None], scores, -1e30)


def row_forward(queries, key_vecs, values, segment_row):
    masked = masked_scores(queries, key_vecs, segment_row)
    highest_score = jnp.max(masked, axis=-1, keepdims=True)
    expo = jnp.exp(masked - highest_score)
    denominator = jnp.sum(expo, axis=-1, keepdims=True)
    probs = (expo / denominator).astype(bf16)
    context = jnp.einsum("hqk,khd->qhd", probs, values, preferred_element_type=f32)
    log_total = highest_score[..., 0] + jnp.log(denominator[..., 0])
    return (context.astype(bf16), log_total)


def row_backward(queries, key_vecs, values, segment_row, log_total, grad_context):
    scale_factor = 1.0 / math.sqrt(queries.shape[-1])
    masked = masked_scores(queries, key_vecs, segment_row)
    probs = jnp.exp(masked - log_total[..., None])
    grad_probs = jnp.einsum("qhd,khd->hqk", grad_context, values, preferred_element_type=f32)
    grad_values = jnp.einsum(
        "hqk,qhd->khd", probs.astype(bf16), grad_context, preferred_element_type=f32
    )
    inner = jnp.sum(grad_probs * probs, axis=-1, keepdims=True)
    grad_scores = (probs * (grad_probs - inner)).astype(bf16)
    grad_queries = (
        jnp.einsum("hqk,khd->qhd", grad_scores, key_vecs, preferred_element_type=f32) * scale_factor
    )
    grad_keys = (
        jnp.einsum("hqk,qhd->khd", grad_scores, queries, preferred_element_type=f32) * scale_factor
    )
    return (grad_queries.astype(bf16), grad_keys.astype(bf16), grad_values.astype(bf16))


def solution(mesh):
    n_dp, n_mp = mesh.shape["dp"], mesh.shape["mp"]
    if n_dp % GROUP:
        raise ValueError("dp size")

    def rotate(array, step):
        return lax.ppermute(array, "mp", [(i, (i + step) % n_mp) for i in range(n_mp)])

    def swap(array, bits):
        return lax.ppermute(array, "dp", [(i, i ^ bits) for i in range(n_dp)])

    def plane_gather(array):
        four = jnp.stack([array, swap(array, 2), swap(array, 4), swap(array, 6)])
        other = swap(four, 1)
        return jnp.stack([four, other], axis=1).reshape((GROUP,) + array.shape)

    def gather_weights(quarter, order, extra=None):
        rows = quarter.shape[0] // GROUP
        index = lax.axis_index("dp") % GROUP
        piece = lax.dynamic_slice_in_dim(quarter, index * rows, rows, 0)
        if extra is not None:
            piece = jnp.concatenate([piece, extra])
        got = [rotate(piece, r) for r in range(1, n_mp)]
        slots = plane_gather(jnp.stack([g[:rows] for g in got]))
        slots = slots[order].transpose(1, 0, 2, 3).reshape((n_mp - 1,) + quarter.shape)
        full = jnp.concatenate([quarter[None], slots])
        if extra is None:
            return full
        return full, jnp.stack([extra] + [g[rows:] for g in got])

    def reduce_grads(grads, order):
        quarters, height, width = grads.shape
        rows = height // GROUP
        half = width // 2
        slots = grads.astype(bf16).reshape(quarters, GROUP, rows, width)[:, order]
        slots = slots.reshape(quarters, GROUP // 2, 2, rows, width)
        part = (slots[:, :, 0].astype(f32) + swap(slots[:, :, 1], 1).astype(f32)).astype(bf16)
        left, right = part[..., :half], part[..., half:]
        left_got = swap(left[:, jnp.array([1, 3])], 2)
        right_got = swap(right[:, 2:], 4)
        left = (left[:, jnp.array([0, 2])].astype(f32) + left_got.astype(f32)).astype(bf16)
        right = (right[:, :2].astype(f32) + right_got.astype(f32)).astype(bf16)
        left_got = swap(left[:, 1], 4)
        right_got = swap(right[:, 1], 2)
        left = left[:, 0].astype(f32) + left_got.astype(f32)
        right = right[:, 0].astype(f32) + right_got.astype(f32)
        part = jnp.concatenate([left, right], axis=-1).astype(bf16)
        total = part[0].astype(f32)
        for r in range(1, n_mp):
            total = total + rotate(part[r], -r).astype(f32)
        if n_dp > GROUP:
            total = lax.psum(
                total,
                "dp",
                axis_index_groups=[
                    [i + GROUP * k for k in range(n_dp // GROUP)] for i in range(GROUP)
                ],
            )
        return plane_gather(total.astype(bf16))[order].astype(f32).reshape(height, width)

    def shards(
        tokens,
        segment_ids,
        query_weight,
        query_bias,
        key_weight,
        value_weight,
        value_bias,
        output_weight,
        output_bias,
        first_gain,
        first_shift,
        up_weight,
        up_bias,
        down_weight,
        down_bias,
        second_gain,
        second_shift,
        cotangent,
    ):
        length, width = tokens.shape
        head_width = query_weight.shape[1]
        units = up_weight.shape[1]
        heads = n_mp * head_width // HEAD_DIM
        order = jnp.arange(GROUP) ^ (lax.axis_index("dp") % GROUP)
        place = lax.axis_index("mp")
        row = lax.dynamic_index_in_dim(segment_ids, place, 0, keepdims=False)

        biases = jnp.zeros((8, units), bf16)
        biases = biases.at[0, :head_width].set(query_bias)
        biases = biases.at[0, head_width : 2 * head_width].set(value_bias)
        biases = biases.at[1].set(up_bias)
        att_quarter = jnp.concatenate(
            [query_weight, key_weight, value_weight, output_weight.T], axis=1
        )
        att, biases = gather_weights(att_quarter, order, biases)
        up = gather_weights(up_weight, order)
        down = gather_weights(down_weight, order)

        def columns(array):
            return array.transpose(1, 0, 2).reshape(array.shape[1], -1)

        w = head_width
        query_all, key_all, value_all, output_all = (
            columns(att[:, :, i * w : (i + 1) * w]) for i in range(4)
        )
        up_all, down_all = columns(up), down.reshape(-1, width)
        query_bias_all = biases[:, 0, :w].reshape(-1)
        value_bias_all = biases[:, 0, w : 2 * w].reshape(-1)
        up_bias_all = biases[:, 1].reshape(-1)

        def by_heads(array):
            return array.reshape(length, heads, HEAD_DIM)

        def flat(array):
            return array.reshape(length, heads * HEAD_DIM)

        def mm(left, right):
            return jnp.dot(left, right, preferred_element_type=f32)

        def mmt(left, right):
            return lax.dot_general(left, right, (((1,), (1,)), ((), ())), preferred_element_type=f32)

        queries = by_heads((mm(tokens, query_all) + query_bias_all).astype(bf16))
        key_vecs = by_heads(mm(tokens, key_all).astype(bf16))
        values = by_heads((mm(tokens, value_all) + value_bias_all).astype(bf16))
        contexts, log_total = row_forward(queries, key_vecs, values, row)
        contexts = flat(contexts)
        attended = mmt(contexts, output_all) + output_bias
        gain_one = first_gain.astype(f32)
        gain_two = second_gain.astype(f32)
        normed_one, normal_one, inverse_one = norm_forward(
            tokens.astype(f32) + attended, gain_one, first_shift.astype(f32)
        )
        normed_low = normed_one.astype(bf16)
        hidden = mm(normed_low, up_all) + up_bias_all
        activated = jax.nn.gelu(hidden, approximate=False).astype(bf16)
        mixed = mm(activated, down_all) + down_bias
        result, normal_two, inverse_two = norm_forward(
            normed_one + mixed, gain_two, second_shift.astype(f32)
        )
        grad_out = cotangent.astype(f32)
        grad_second_gain = jnp.sum(grad_out * normal_two, axis=0)
        grad_second_shift = jnp.sum(grad_out, axis=0)
        grad_two = norm_backward(grad_out, normal_two, inverse_two, gain_two)
        grad_mixed = grad_two.astype(bf16)
        grad_down_bias = jnp.sum(grad_mixed.astype(f32), axis=0)

        grad_down = inner_rows(activated, grad_mixed).reshape(n_mp, units, width)
        grad_down = reduce_grads(grad_down, order)
        grad_hidden = (mmt(grad_mixed, down_all) * gelu_slope(hidden)).astype(bf16)
        grad_up_bias = jnp.sum(grad_hidden.astype(f32), axis=0)

        def quarters(array):
            return array.reshape(array.shape[0], n_mp, -1).transpose(1, 0, 2)

        grad_up = reduce_grads(quarters(inner_rows(normed_low, grad_hidden)), order)
        grad_normed = mmt(grad_hidden, up_all) + grad_two
        grad_first_gain = jnp.sum(grad_normed * normal_one, axis=0)
        grad_first_shift = jnp.sum(grad_normed, axis=0)
        grad_one = norm_backward(grad_normed, normal_one, inverse_one, gain_one)
        grad_attended = grad_one.astype(bf16)
        grad_output_bias = jnp.sum(grad_attended.astype(f32), axis=0)
        grad_contexts = mm(grad_attended, output_all).astype(bf16)
        grad_queries, grad_keys, grad_values = map(
            flat,
            row_backward(queries, key_vecs, values, row, log_total, by_heads(grad_contexts)),
        )
        grad_query_bias = jnp.sum(grad_queries.astype(f32), axis=0)
        grad_value_bias = jnp.sum(grad_values.astype(f32), axis=0)
        grad_att = jnp.concatenate(
            [
                quarters(inner_rows(tokens, grad_queries)),
                quarters(inner_rows(tokens, grad_keys)),
                quarters(inner_rows(tokens, grad_values)),
                quarters(inner_rows(grad_attended, contexts)),
            ],
            axis=-1,
        )
        grad_att = reduce_grads(grad_att, order)
        grad_tokens = (
            mmt(grad_queries, query_all)
            + mmt(grad_keys, key_all)
            + mmt(grad_values, value_all)
            + grad_one
        )
        mine = jnp.concatenate(
            [
                grad_query_bias.reshape(n_mp, -1),
                grad_value_bias.reshape(n_mp, -1),
                grad_up_bias.reshape(n_mp, -1),
            ],
            axis=1,
        )
        mine = mine[(place - jnp.arange(n_mp)) % n_mp]
        shared = jnp.stack(
            [
                grad_output_bias,
                grad_first_gain,
                grad_first_shift,
                grad_down_bias,
                grad_second_gain,
                grad_second_shift,
            ]
        )
        mine, shared = lax.psum((mine, shared), ("dp", "mp"))
        mine = lax.dynamic_index_in_dim(mine, place, 0, keepdims=False)
        return (
            result.astype(bf16),
            grad_tokens.astype(bf16),
            grad_att[:, :w],
            mine[:w],
            grad_att[:, w : 2 * w],
            grad_att[:, 2 * w : 3 * w],
            mine[w : 2 * w],
            grad_att[:, 3 * w :].T,
            shared[0],
            shared[1],
            shared[2],
            grad_up,
            mine[2 * w :],
            grad_down,
            shared[3],
            shared[4],
            shared[5],
        )

    in_specs = (
        P(("dp", "mp"), None),
        P("dp", None),
        P(None, "mp"),
        P("mp"),
        P(None, "mp"),
        P(None, "mp"),
        P("mp"),
        P("mp", None),
        P(),
        P(),
        P(),
        P(None, "mp"),
        P("mp"),
        P("mp", None),
        P(),
        P(),
        P(),
        P(("dp", "mp"), None),
    )
    out_specs = (
        P(("dp", "mp"), None),
        P(("dp", "mp"), None),
        P(None, "mp"),
        P("mp"),
        P(None, "mp"),
        P(None, "mp"),
        P("mp"),
        P("mp", None),
        P(),
        P(),
        P(),
        P(None, "mp"),
        P("mp"),
        P("mp", None),
        P(),
        P(),
        P(),
    )
    return jax.shard_map(shards, mesh=mesh, in_specs=in_specs, out_specs=out_specs, check_vma=False)
```

```python
import functools
import math

import jax
import jax.numpy as jnp
from jax import lax
from jax.experimental import pallas as pl
from jax.experimental.pallas import tpu as pltpu
from jax.sharding import PartitionSpec as P

HEAD_DIM = 64
PASSAGE = 128
GROUP = 8
EXTRA = 8
LANES = 128
CHUNK = 64
SCOPED = {
    "first_piece": 60,
    "att_forward": 9,
    "ffn_first": 7,
    "ffn_last": 12,
    "ffn_backward": 18,
    "att_backward": 13,
    "input_backward": 6,
    "finish_down": 6,
    "finish_up": 6,
    "finish_att": 8,
}
epsilon = 1e-05
bf16 = jnp.bfloat16
f32 = jnp.float32


def nn(left, right):
    return lax.dot_general(left, right, (((1,), (0,)), ((), ())), preferred_element_type=f32)


def nt(left, right):
    return lax.dot_general(left, right, (((1,), (1,)), ((), ())), preferred_element_type=f32)


def tn(left, right):
    return lax.dot_general(left, right, (((0,), (0,)), ((), ())), preferred_element_type=f32)


def call(body, name, outs, args, spaces, scratch=(), out_spaces=None):
    def spec(kind):
        if kind == "s":
            return pl.BlockSpec(memory_space=pltpu.SMEM)
        if kind == "h":
            return pl.BlockSpec(memory_space=pltpu.HBM)
        return pl.BlockSpec(memory_space=pltpu.VMEM)

    out_spaces = out_spaces or "v" * len(outs)
    def size(array):
        return math.prod(array.shape) * jnp.dtype(array.dtype).itemsize

    every = list(zip(args, spaces)) + list(zip(outs, out_spaces))
    moved = sum(size(array) for array, kind in every)
    return pl.pallas_call(
        body,
        name=name,
        out_shape=tuple(outs),
        in_specs=[spec(k) for k in spaces],
        out_specs=tuple(spec(k) for k in out_spaces),
        scratch_shapes=list(scratch),
        compiler_params=pltpu.CompilerParams(vmem_limit_bytes=SCOPED[name] << 20),
        cost_estimate=pl.CostEstimate(flops=0, bytes_accessed=moved // 64, transcendentals=0),
    )(*args)


def vector(ref):
    return ref[...].astype(f32).reshape(1, ref.shape[0])


def places_by_axis(index):
    x, y = index & 3, ((index >> 1) & 2) | (index & 1)
    return [x, x ^ 1, x ^ 2, x ^ 3, 4 + y, 4 + (y ^ 1), 4 + (y ^ 2), 4 + (y ^ 3)]


def place_slots(four, other, r, low, rows, places, dest, base, columns):
    for s in range(GROUP):
        at = pl.multiple_of(base + places[s] * rows, rows)
        dest[pl.ds(at, rows), columns] = (other if s % 2 else four)[s // 2, r, low : low + rows]


def put_slots(index, r, rows, low, keep, send):
    size = rows[0].shape[0]
    for odd in range(2):

        @pl.when((index & 1) == odd)
        def _():
            for d in range(GROUP):
                dest = send if (d ^ odd) & 1 else keep
                dest[(index ^ d) >> 1, r, low : low + size] = rows[d]


def normalize(total):
    centred = total - jnp.mean(total, axis=-1, keepdims=True)
    inverse = lax.rsqrt(jnp.mean(centred * centred, axis=-1, keepdims=True) + epsilon)
    return centred * inverse, inverse


def norm_backward(grad_out, normal, inverse, norm_gain):
    scaled = grad_out * norm_gain
    return inverse * (
        scaled
        - jnp.mean(scaled, axis=-1, keepdims=True)
        - normal * jnp.mean(scaled * normal, axis=-1, keepdims=True)
    )


def column_sum(array):
    return jnp.sum(array, axis=0, keepdims=True)


def folded(array):
    return jnp.sum(array.reshape(-1, 8, array.shape[1]), axis=0)


def by_rows(length, body, sums, width):
    def step(i, totals):
        found = body(pl.ds(pl.multiple_of(i * CHUNK, CHUNK), CHUNK))
        return tuple(t + folded(f) for t, f in zip(totals, found))

    zeros = tuple(jnp.zeros((8, width), f32) for _ in range(sums))
    totals = lax.fori_loop(0, length // CHUNK, step, zeros, unroll=2)
    return tuple(column_sum(t) for t in totals)


def band(block, length):
    return max(0, (block - 1) * PASSAGE), min(length, (block + 2) * PASSAGE)


def clear_outside(array, length):
    for b in range(length // PASSAGE):
        lo, hi = band(b, length)
        block = slice(b * PASSAGE, (b + 1) * PASSAGE)
        for low, high in ((0, lo), (hi, length)):
            if high > low:
                shape = (array.shape[0], high - low, PASSAGE)
                array[:, low:high, block] = jnp.zeros(shape, array.dtype)


def fill_bias(bias, seg_row, seg_col, length):
    for b in range(length // PASSAGE):
        lo, hi = band(b, length)
        same = seg_col[lo:hi, :] == seg_row[:, b * PASSAGE : (b + 1) * PASSAGE]
        bias[b, : hi - lo, :] = jnp.where(same, 0.0, -1e30)


def softmax_columns(scores):
    expo = jnp.exp(scores - jnp.max(scores, axis=0, keepdims=True))
    return expo * (1.0 / jnp.sum(expo, axis=0, keepdims=True))


def first_piece(
    index_ref, own_q, own_k, own_v, own_o, query_bias, value_bias, up_bias, out, owns,
    query_row, value_row, up_row, sems,
):
    w = own_q.shape[0]
    rows = w // 2
    small = [
        pltpu.make_async_copy(own, owns.at[pl.ds(m * w, w)], sems.at[3 + m])
        for m, own in enumerate((own_q, own_k, own_v, own_o))
    ]
    small += [
        pltpu.make_async_copy(query_bias, query_row, sems.at[0]),
        pltpu.make_async_copy(value_bias, value_row, sems.at[1]),
        pltpu.make_async_copy(up_bias, up_row, sems.at[2]),
    ]
    for copy in small:
        copy.start()
    for copy in small:
        copy.wait()
    out[:rows, :] = owns[pl.ds(pl.multiple_of(index_ref[0] * rows, rows), rows), :]
    out[rows:, :] = jnp.zeros((EXTRA, out.shape[1]), bf16)
    out[rows : rows + 1, :w] = vector(query_row).astype(bf16)
    out[rows : rows + 1, w : 2 * w] = vector(value_row).astype(bf16)
    out[rows + 1 : rows + 2, :] = vector(up_row).astype(bf16)


def att_forward(
    index_ref, tokens, owns, four, other, bias_0, bias_1, bias_2, bias_3,
    output_bias, seg_row, seg_col,
    queries, keys, values, contexts, normal, inverse, weights, wo,
    bias, probs_t, row, attended,
):
    length, width = tokens.shape
    w = owns.shape[0] // 4
    quarters = width // w
    rows = four.shape[2]
    index = index_ref[0]
    for m in range(3):
        weights[m, :w, :] = owns[m * w : (m + 1) * w, :]
    wo[:w, :] = owns[3 * w :, :]
    for r in range(1, quarters):
        for s in range(GROUP):
            owner = index ^ s
            at = pl.multiple_of(r * w + (owner & 1) * rows, rows)
            source = other if s % 2 else four

            @pl.when(owner < 6)
            def _():
                weights[owner >> 1, pl.ds(at, rows), :] = source[s // 2, r - 1]

            @pl.when(owner >= 6)
            def _():
                wo[pl.ds(at, rows), :] = source[s // 2, r - 1]

    fill_bias(bias, seg_row, seg_col, length)
    clear_outside(probs_t, length)
    for r, source in enumerate((bias_0, bias_1, bias_2, bias_3)):
        for i in range(2):
            piece = source[rows : rows + 1, i * w : (i + 1) * w].astype(f32)
            row[i : i + 1, r * w : (r + 1) * w] = piece
    low = (nt(tokens[...], weights[0]) + row[0:1, :]).astype(bf16)
    queries[...] = (low.astype(f32) * (HEAD_DIM**-0.5)).astype(bf16)
    keys[...] = nt(tokens[...], weights[1]).astype(bf16)
    values[...] = (nt(tokens[...], weights[2]) + row[1:2, :]).astype(bf16)
    first = lax.broadcasted_iota(jnp.int32, (PASSAGE, LANES), 1) < HEAD_DIM
    first_all = lax.broadcasted_iota(jnp.int32, (length, LANES), 1) < HEAD_DIM

    def pair(i, carry):
        at = pl.ds(pl.multiple_of(i * LANES, LANES), LANES)
        for half, mine in enumerate((first, jnp.logical_not(first))):
            for b in range(length // PASSAGE):
                lo, hi = band(b, length)
                block = slice(b * PASSAGE, (b + 1) * PASSAGE)
                q = queries[block, at]
                masked = jnp.where(mine, q, jnp.zeros_like(q))
                scores = nt(keys[lo:hi, at], masked) + bias[b, : hi - lo, :]
                probs_t[half, lo:hi, block] = softmax_columns(scores).astype(bf16)
        found = [tn(probs_t[half], values[:, at]) for half in range(2)]
        contexts[:, at] = jnp.where(first_all, *found).astype(bf16)
        return carry

    lax.fori_loop(0, width // LANES, pair, 0)
    attended[...] = nn(contexts[...], wo[...]) + vector(output_bias)

    def norm(rows):
        n, r = normalize(tokens[rows, :].astype(f32) + attended[rows, :])
        normal[rows, :] = n
        inverse[rows, :] = r
        return ()

    by_rows(length, norm, 0, width)


def gelu_parts(hidden):
    cumulative = 0.5 * (1.0 + lax.erf(hidden * 0.7071067811865476))
    density = jnp.exp(-0.5 * hidden * hidden) * 0.3989422804014327
    return (hidden * cumulative).astype(bf16), (cumulative + hidden * density).astype(bf16)


def ffn_first(
    index_ref, normal, gain, shift, down_bias, bias_0, bias_1, bias_2, own_up, own_down, four, other,
    activated, slope, low_t, mixed, up, down,
):
    units = own_up.shape[1]
    rows = four.shape[2] // 2
    quarters = four.shape[1] + 1
    biases = (bias_0, bias_1, bias_2)
    places = places_by_axis(index_ref[0])
    normed = normal[...] * vector(gain) + vector(shift)
    low = normed.astype(bf16)
    low_t[...] = low.T
    mixed[...] = normed + vector(down_bias)
    for r in range(quarters):
        mine = slice(r * units, (r + 1) * units)
        if r == 0:
            up[:, mine] = own_up[...]
            down[mine, :] = own_down[...]
        else:
            place_slots(four, other, r - 1, 0, rows, places, up, 0, mine)
            place_slots(four, other, r - 1, rows, rows, places, down, r * units, slice(None))
        at = biases[r].shape[0] - EXTRA + 1
        hidden = nn(low, up[:, mine]) + biases[r][at : at + 1, :].astype(f32)
        activated[:, mine], slope[:, mine] = gelu_parts(hidden)
    mixed[...] += nn(activated[...], down[...])


def ffn_last(
    index_ref, normal, cotangent, gain, shift, second_gain, second_shift, bias, activated, mixed,
    four, other,
    output, grad_mixed, grad_two, sums, slope, up, down, keep, send,
    own, total,
):
    length, width = normal.shape
    units = up.shape[1]
    rows = four.shape[2] // 2
    index = index_ref[0]
    places = places_by_axis(index)
    place_slots(four, other, 0, 0, rows, places, up, 0, slice(None))
    place_slots(four, other, 0, rows, rows, places, down, 0, slice(None))
    low = (normal[...] * vector(gain) + vector(shift)).astype(bf16)
    at = bias.shape[0] - EXTRA + 1
    own[...], slope[...] = gelu_parts(nn(low, up[...]) + bias[at : at + 1, :].astype(f32))
    total[...] = mixed[...] + nn(own[...], down[...])
    out_gain, out_shift = vector(second_gain), vector(second_shift)

    def norm(rows):
        n, inverse = normalize(total[rows, :])
        output[rows, :] = (n * out_gain + out_shift).astype(bf16)
        grad_out = cotangent[rows, :].astype(f32)
        two = norm_backward(grad_out, n, inverse, out_gain)
        grad_two[rows, :] = two
        low = two.astype(bf16)
        grad_mixed[rows, :] = low
        return low.astype(f32), grad_out * n, grad_out

    sums[...] = jnp.zeros_like(sums)
    for i, found in enumerate(by_rows(length, norm, 3, width)):
        sums[i : i + 1, :] = found
    quarters = keep.shape[1]
    for r in range(quarters):
        left = own[...] if r == quarters - 1 else activated[:, r * units : (r + 1) * units]
        grad = tn(left, grad_mixed[...]).astype(bf16)
        put_slots(index, r, grad.reshape(GROUP, -1, width), 0, keep, send)


def ffn_backward(
    index_ref, grad_mixed, low_t, slope, slope_last, grad_two, normal, inverse, gain_ref, sums_two,
    up, up_last, down, down_last,
    grad_one, grad_attended, keep, send,
    hidden, total,
):
    length, width = grad_mixed.shape
    units = down_last.shape[0]
    quarters, rows = keep.shape[1], keep.shape[2] - EXTRA
    index = index_ref[0]
    low_sums = []
    for r in range(quarters):
        mine = slice(r * units, (r + 1) * units)
        last = r == quarters - 1
        weight = down_last[...] if last else down[mine, :]
        factor = slope_last[...] if last else slope[:, mine]
        low = (nt(grad_mixed[...], weight) * factor.astype(f32)).astype(bf16)
        hidden[:, mine] = low
        low_sums.append(column_sum(low.astype(f32)))
        grad = nn(low_t[...], low).astype(bf16)
        put_slots(index, r, grad.reshape(GROUP, rows, units), 0, keep, send)
    inner = up.shape[1]
    total[...] = nt(hidden[:, :inner], up[...]) + grad_two[...]
    total[...] += nt(hidden[:, inner:], up_last[...])
    gain = vector(gain_ref)

    def norm(at):
        grad_normed = total[at, :]
        n = normal[at, :]
        one = norm_backward(grad_normed, n, inverse[at, :], gain)
        grad_one[at, :] = one
        low = one.astype(bf16)
        grad_attended[at, :] = low
        return low.astype(f32), grad_normed * n, grad_normed

    shared = list(by_rows(length, norm, 3, width))
    shared += [sums_two[i : i + 1, :] for i in range(3)] + [jnp.zeros_like(gain)]
    for r in range(quarters):
        extra = [
            jnp.broadcast_to(total, (EXTRA, units)).astype(bf16) for total in [low_sums[r]] + shared
        ]
        put_slots(index, r, jnp.stack(extra), rows, keep, send)


def att_backward(
    part, index_ref, queries, keys, values, contexts, grad_attended, tokens, wo, seg_row, seg_col,
    grad_queries, grad_keys, grad_values, keep, send,
    grad_contexts, bias, probs_t, scores_t,
):
    length, width = tokens.shape
    quarters, rows = keep.shape[1], keep.shape[2] - EXTRA
    w = 2 * rows
    across = quarters * w
    index = index_ref[0]
    scale = HEAD_DIM**-0.5
    low = part * across
    fill_bias(bias, seg_row, seg_col, length)
    clear_outside(probs_t, length)
    clear_outside(scores_t, length)
    grad_contexts[...] = nt(grad_attended[...], wo[low : low + across, :]).astype(bf16)
    first = lax.broadcasted_iota(jnp.int32, (PASSAGE, LANES), 1) < HEAD_DIM
    first_all = lax.broadcasted_iota(jnp.int32, (length, LANES), 1) < HEAD_DIM

    def pair(i, carry):
        here = pl.ds(pl.multiple_of(i * LANES, LANES), LANES)
        at = pl.ds(pl.multiple_of(low + i * LANES, LANES), LANES)
        found = []
        for half, mine in enumerate((first, jnp.logical_not(first))):
            for b in range(length // PASSAGE):
                lo, hi = band(b, length)
                block = slice(b * PASSAGE, (b + 1) * PASSAGE)
                q = queries[block, at]
                g = grad_contexts[block, here]
                zero = jnp.zeros_like(q)
                scores = nt(keys[lo:hi, at], jnp.where(mine, q, zero)) + bias[b, : hi - lo, :]
                probs = softmax_columns(scores)
                grad_probs = nt(values[lo:hi, at], jnp.where(mine, g, zero))
                inner = jnp.sum(grad_probs * probs, axis=0, keepdims=True)
                probs_t[half, lo:hi, block] = probs.astype(bf16)
                scores_t[half, lo:hi, block] = (probs * (grad_probs - inner)).astype(bf16)
            found.append(
                (
                    tn(scores_t[half], keys[:, at]),
                    nn(scores_t[half], queries[:, at]),
                    nn(probs_t[half], grad_contexts[:, here]),
                )
            )
        dq, dk, dv = (jnp.where(first_all, a, b) for a, b in zip(*found))
        grad_queries[:, here] = (dq * scale).astype(bf16)
        grad_keys[:, here] = dk.astype(bf16)
        grad_values[:, here] = dv.astype(bf16)
        return carry

    lax.fori_loop(0, across // LANES, pair, 0)
    grads = (
        lambda: tn(grad_queries[...], tokens[...]),
        lambda: tn(grad_keys[...], tokens[...]),
        lambda: tn(grad_values[...], tokens[...]),
        lambda: tn(contexts[:, low : low + across], grad_attended[...]),
    )
    grads = [make().astype(bf16).reshape(quarters, 2, rows, width) for make in grads]
    query_sum = column_sum(grad_queries[...].astype(f32))
    value_sum = column_sum(grad_values[...].astype(f32))
    for r in range(quarters):
        put_slots(index, r, [grads[d // 2][r, d % 2] for d in range(GROUP)], 0, keep, send)
        cols = slice(r * w, (r + 1) * w)
        line = jnp.concatenate(
            [query_sum[:, cols], value_sum[:, cols], jnp.zeros((1, width - 2 * w), f32)], axis=1
        )
        line = jnp.broadcast_to(line, (EXTRA, width)).astype(bf16)
        put_slots(index, r, [line] * GROUP, rows, keep, send)


def input_backward(q0, k0, v0, q1, k1, v1, grad_one, weights, out):
    half = q0.shape[1]
    total = grad_one[...]
    for m, (left, right) in enumerate(((q0, q1), (k0, k1), (v0, v1))):
        total += nn(left[...], weights[m, :half]) + nn(right[...], weights[m, half:])
    out[...] = total.astype(bf16)


def finish_down(index_ref, four, other, out):
    rows = four.shape[1]
    for s in range(GROUP):
        at = pl.multiple_of((index_ref[0] ^ s) * rows, rows)
        out[pl.ds(at, rows), :] = (other if s % 2 else four)[s // 2].astype(f32)


def finish_up(index_ref, four, other, out, sums):
    rows = four.shape[1] - EXTRA
    for s in range(GROUP):
        owner = index_ref[0] ^ s
        slot = (other if s % 2 else four)[s // 2].astype(f32)
        out[pl.ds(pl.multiple_of(owner * rows, rows), rows), :] = slot[:rows]
        sums[pl.ds(pl.multiple_of(owner * EXTRA, EXTRA), EXTRA), :] = slot[rows:]


def finish_att(index_ref, four, other, gq, gk, gv, go, sums, whole):
    rows = four.shape[1] - EXTRA
    w = 2 * rows
    for s in range(GROUP):
        slot = (other if s % 2 else four)[s // 2].astype(f32)
        owner = index_ref[0] ^ s
        whole[pl.ds(pl.multiple_of(owner * rows, rows), rows), :] = slot[:rows]
        sums[pl.ds(pl.multiple_of(owner * EXTRA, EXTRA), EXTRA), :] = slot[rows:]
    for m, out in enumerate((gq, gk, gv, go)):
        out[...] = whole[m * w : (m + 1) * w, :]


def solution(mesh):
    n_dp, n_mp = mesh.shape["dp"], mesh.shape["mp"]
    if n_dp % GROUP or n_mp % 2:
        raise ValueError("mesh")

    def rotate(array, step):
        return lax.ppermute(array, "mp", [(i, (i + step) % n_mp) for i in range(n_mp)])

    def swap(array, bits):
        return lax.ppermute(array, "dp", [(i, i ^ bits) for i in range(n_dp)])

    def plane_swap(array):
        return [array, swap(array, 2), swap(array, 4), swap(array, 6)]

    def add(left, right):
        return (left.astype(f32) + right.astype(f32)).astype(bf16)

    def tie(*arrays):
        return lax.optimization_barrier(arrays)

    def after(array, *others):
        return tie(array, *others)[0]

    def first_axis(bits):
        go = slice(1, None, 2) if bits == 2 else slice(2, None)
        stay = slice(0, None, 2) if bits == 2 else slice(0, 2)
        return go, stay

    def plane_first(keep, got, bits):
        go, stay = first_axis(bits)
        return add(keep[go], got[go]), add(keep[stay], got[stay])

    def line_moves(parts):
        return [parts[0]] + [rotate(parts[r], -r) for r in range(1, n_mp)]

    def line_total(moved):
        moved = [array.astype(f32) for array in moved]
        total = sum(moved[0::2][1:], moved[0]) + sum(moved[1::2][1:], moved[1])
        if n_dp > GROUP:
            groups = [[i + GROUP * k for k in range(n_dp // GROUP)] for i in range(GROUP)]
            total = lax.psum(total, "dp", axis_index_groups=groups)
        return total.astype(bf16)

    def shards(
        tokens,
        segment_ids,
        query_weight,
        query_bias,
        key_weight,
        value_weight,
        value_bias,
        output_weight,
        output_bias,
        first_gain,
        first_shift,
        up_weight,
        up_bias,
        down_weight,
        down_bias,
        second_gain,
        second_shift,
        cotangent,
    ):
        length, width = tokens.shape
        w = query_weight.shape[1]
        units = up_weight.shape[1]
        rows = width // GROUP
        blocks = length // PASSAGE
        half, part = GROUP // 2, units // GROUP
        shape = jax.ShapeDtypeStruct
        place = lax.axis_index("mp")
        within = lax.axis_index("dp") % GROUP
        index = within.astype(jnp.int32).reshape(1)
        seg_row = lax.dynamic_slice_in_dim(segment_ids, place, 1, 0)
        seg_col = seg_row.reshape(length, 1)

        def slot(array, at, size):
            return lax.dynamic_slice_in_dim(array, at * size, size, 0)

        owns = [query_weight.T, key_weight.T, value_weight.T, output_weight]
        piece, owns = call(
            first_piece,
            "first_piece",
            [shape((rows + EXTRA, width), bf16), shape((4 * w, width), bf16)],
            [index, *owns, query_bias, value_bias, up_bias],
            "s" + "h" * 7,
            [
                pltpu.VMEM((w,), bf16),
                pltpu.VMEM((w,), bf16),
                pltpu.VMEM((units,), bf16),
                pltpu.SemaphoreType.DMA((7,)),
            ],
        )
        biases = [piece] + [rotate(piece, r) for r in range(1, n_mp)]
        att_line = jnp.stack([g[:rows] for g in biases[1:]])
        by_x, by_y = within & 3, ((within >> 1) & 2) | (within & 1)
        piece = jnp.concatenate(
            [
                slot(up_weight, by_x, rows),
                slot(down_weight, by_x, part),
                slot(up_weight, 4 + by_y, rows),
                slot(down_weight, 4 + by_y, part),
            ]
        )
        ffn_line = [rotate(piece, r) for r in range(1, n_mp)]

        def plane_by_axis(line):
            cut = line[0].shape[0] // 2
            left = jnp.stack([g[:cut] for g in line])
            right = jnp.stack([g[cut:] for g in line])
            return left, swap(left, 2), right, swap(right, 4)

        att_four = jnp.stack([att_line] + [swap(att_line, b) for b in (2, 4, 6)])
        att_other = swap(att_four, 1)
        ffn_four = plane_by_axis(ffn_line[:-1])

        tok_low = shape((length, width), bf16)
        tok_wide = shape((length, width), f32)
        queries, keys, values, contexts, normal, inverse, weights, wo = call(
            att_forward,
            "att_forward",
            [tok_low] * 4
            + [
                tok_wide,
                shape((length, 1), f32),
                shape((3, n_mp * w, width), bf16),
                shape((n_mp * w, width), bf16),
            ],
            [
                index,
                tokens,
                owns,
                att_four,
                att_other,
                *biases,
                output_bias,
                seg_row,
                seg_col,
            ],
            "s" + "v" * 11,
            [
                pltpu.VMEM((blocks, 3 * PASSAGE, PASSAGE), f32),
                pltpu.VMEM((2, length, length), bf16),
                pltpu.VMEM((8, width), f32),
                pltpu.VMEM((length, width), f32),
            ],
        )
        normal, ffn_four, ffn_line[-1] = tie(normal, ffn_four, ffn_line[-1])
        ffn_four = jnp.stack(ffn_four)
        ffn_other = swap(ffn_four, 1)
        last_four = plane_by_axis(ffn_line[-1:])
        inner = (n_mp - 1) * units
        hidden_low = shape((length, inner), bf16)
        activated, slope, low_t, mixed, up, down = call(
            ffn_first,
            "ffn_first",
            [
                hidden_low,
                hidden_low,
                shape((width, length), bf16),
                tok_wide,
                shape((width, inner), bf16),
                shape((inner, width), bf16),
            ],
            [
                index,
                normal,
                first_gain,
                first_shift,
                down_bias,
                *biases[:-1],
                up_weight,
                down_weight,
                ffn_four,
                ffn_other,
            ],
            "s" + "v" * 11,
        )
        activated, last_four = tie(activated, last_four)
        last_four = jnp.stack(last_four)
        last_other = swap(last_four, 1)
        pieces = shape((half, n_mp, part, width), bf16)
        (
            output,
            grad_mixed,
            grad_two,
            sums_two,
            slope_last,
            up_last,
            down_last,
            keep_down,
            send_down,
        ) = call(
            ffn_last,
            "ffn_last",
            [
                tok_low,
                tok_low,
                tok_wide,
                shape((8, width), f32),
                shape((length, units), bf16),
                shape((width, units), bf16),
                shape((units, width), bf16),
                pieces,
                pieces,
            ],
            [
                index,
                normal,
                cotangent,
                first_gain,
                first_shift,
                second_gain,
                second_shift,
                biases[-1],
                activated,
                mixed,
                last_four,
                last_other,
            ],
            "s" + "v" * 11,
            [pltpu.VMEM((length, units), bf16), pltpu.VMEM((length, width), f32)],
        )
        got_down = swap(send_down, 1)
        pieces = shape((half, n_mp, rows + EXTRA, units), bf16)
        grad_one, grad_attended, keep_up, send_up = call(
            ffn_backward,
            "ffn_backward",
            [tok_wide, tok_low, pieces, pieces],
            [
                index,
                grad_mixed,
                low_t,
                slope,
                slope_last,
                grad_two,
                normal,
                inverse,
                first_gain,
                sums_two,
                up,
                up_last,
                down,
                down_last,
            ],
            "s" + "v" * 13,
            [pltpu.VMEM((length, n_mp * units), bf16), pltpu.VMEM((length, width), f32)],
        )
        grad_attended, got_down = tie(grad_attended, got_down)
        got_up = swap(send_up, 1)
        leave_down, stay_down = plane_first(keep_down, got_down, 2)
        come_down = swap(leave_down, 2)
        leave_up, stay_up = plane_first(keep_up, got_up, 4)
        come_up = swap(leave_up, 4)
        grad_attended, leave_down, leave_up = tie(grad_attended, leave_down, leave_up)

        halves = n_mp // 2
        across = halves * w
        pieces = shape((half, halves, rows + EXTRA, width), bf16)

        def attention(which, grad_attended):
            return call(
                functools.partial(att_backward, which),
                "att_backward",
                [shape((length, across), bf16)] * 3 + [pieces] * 2,
                [
                    index,
                    queries,
                    keys,
                    values,
                    contexts,
                    grad_attended,
                    tokens,
                    wo,
                    seg_row,
                    seg_col,
                ],
                "s" + "v" * 9,
                [
                    pltpu.VMEM((length, across), bf16),
                    pltpu.VMEM((blocks, 3 * PASSAGE, PASSAGE), f32),
                    pltpu.VMEM((2, length, length), bf16),
                    pltpu.VMEM((2, length, length), bf16),
                ],
            )

        q0, k0, v0, keep_left, send_left = attention(0, grad_attended)
        grad_attended, q0, send_left = tie(grad_attended, q0, send_left)
        got_left = swap(send_left, 1)
        q1, k1, v1, keep_right, send_right = attention(1, grad_attended)
        got_left, come_down, come_up = (
            after(array, q1) for array in (got_left, come_down, come_up)
        )
        q1, k1, v1, keep_right, send_right = tie(q1, k1, v1, keep_right, send_right)
        got_right = swap(send_right, 1)
        down_now = add(stay_down, come_down)
        come_down = swap(down_now[1], 4)
        up_now = add(stay_up, come_up)
        come_up = swap(up_now[1], 2)
        (grad_tokens,) = call(
            input_backward,
            "input_backward",
            [tok_low],
            [q0, k0, v0, q1, k1, v1, grad_one, weights],
            "v" * 8,
        )
        leave_left, stay_left = plane_first(keep_left, got_left, 2)
        leave_right, stay_right = plane_first(keep_right, got_right, 4)
        come_down, come_up, grad_tokens, leave_left, leave_right = tie(
            come_down, come_up, grad_tokens, leave_left, leave_right
        )
        down_parts, up_parts = add(down_now[0], come_down), add(up_now[0], come_up)
        down_line = line_moves(down_parts)
        come_left, come_right = swap(leave_left, 2), swap(leave_right, 4)
        down_line, come_left, come_right, up_parts = tie(
            down_line, come_left, come_right, up_parts
        )
        up_line = line_moves(up_parts)
        left_now, right_now = add(stay_left, come_left), add(stay_right, come_right)
        come_left, come_right = swap(left_now[1], 4), swap(right_now[1], 2)
        down_total = line_total(down_line)
        up_line, come_left, come_right, down_total = tie(
            up_line, come_left, come_right, down_total
        )
        left_parts, right_parts = add(left_now[0], come_left), add(right_now[0], come_right)
        att_line = line_moves(
            [left_parts[r] for r in range(halves)] + [right_parts[r] for r in range(halves)]
        )
        down_four = plane_swap(down_total)
        up_four = plane_swap(line_total(up_line))
        att_line, down_four, up_four = tie(att_line, down_four, up_four)
        att_four = plane_swap(line_total(att_line))
        down_four, up_four = jnp.stack(down_four), jnp.stack(up_four)
        (grad_down,) = call(
            finish_down,
            "finish_down",
            [shape((units, width), f32)],
            [index, down_four, swap(down_four, 1)],
            "svv",
        )
        grad_up, sums = call(
            finish_up,
            "finish_up",
            [shape((width, units), f32), shape((GROUP * EXTRA, units), f32)],
            [index, up_four, swap(up_four, 1)],
            "svv",
        )
        att_four, grad_down, grad_up, sums = tie(att_four, grad_down, grad_up, sums)
        att_four = jnp.stack(att_four)
        att_other = swap(att_four, 1)
        grad_query, grad_key, grad_value, grad_output, att_sums = call(
            finish_att,
            "finish_att",
            [shape((w, width), f32)] * 4 + [shape((GROUP * EXTRA, width), f32)],
            [index, att_four, att_other],
            "svv",
            [pltpu.VMEM((4 * w, width), f32)],
        )
        return (
            output,
            grad_tokens,
            grad_query.T,
            att_sums[0, :w],
            grad_key.T,
            grad_value.T,
            att_sums[0, w : 2 * w],
            grad_output,
            sums[EXTRA],
            sums[2 * EXTRA],
            sums[3 * EXTRA],
            grad_up,
            sums[0],
            grad_down,
            sums[4 * EXTRA],
            sums[5 * EXTRA],
            sums[6 * EXTRA],
        )

    everywhere, rows, columns, units = P(), P(("dp", "mp"), None), P(None, "mp"), P("mp")
    in_specs = (
        rows,
        P("dp", None),
        columns,
        units,
        columns,
        columns,
        units,
        P("mp", None),
        everywhere,
        everywhere,
        everywhere,
        columns,
        units,
        P("mp", None),
        everywhere,
        everywhere,
        everywhere,
        rows,
    )
    out_specs = (
        rows,
        rows,
        columns,
        units,
        columns,
        columns,
        units,
        P("mp", None),
        everywhere,
        everywhere,
        everywhere,
        columns,
        units,
        P("mp", None),
        everywhere,
        everywhere,
        everywhere,
    )
    return jax.shard_map(shards, mesh=mesh, in_specs=in_specs, out_specs=out_specs, check_vma=False)
```

```python
import functools
import math

import jax
import jax.numpy as jnp
from jax import lax
from jax.experimental import pallas as pl
from jax.experimental.pallas import tpu as pltpu
from jax.sharding import PartitionSpec as P

HEAD_DIM = 64
PASSAGE = 128
GROUP = 8
EXTRA = 8
LANES = 128
CHUNK = 64
SCOPED = {
    "first_piece": 60,
    "att_forward": 7,
    "ffn_first": 5,
    "ffn_last": 10,
    "ffn_backward": 16,
    "att_backward": 11,
    "input_backward": 4,
    "finish_down": 4,
    "finish_up": 4,
    "finish_att": 6,
}
epsilon = 1e-05
bf16 = jnp.bfloat16
f32 = jnp.float32


def nn(left, right):
    return lax.dot_general(left, right, (((1,), (0,)), ((), ())), preferred_element_type=f32)


def nt(left, right):
    return lax.dot_general(left, right, (((1,), (1,)), ((), ())), preferred_element_type=f32)


def tn(left, right):
    return lax.dot_general(left, right, (((0,), (0,)), ((), ())), preferred_element_type=f32)


def call(body, name, outs, args, spaces, scratch=(), out_spaces=None):
    def spec(kind):
        if kind == "s":
            return pl.BlockSpec(memory_space=pltpu.SMEM)
        if kind == "h":
            return pl.BlockSpec(memory_space=pltpu.HBM)
        return pl.BlockSpec(memory_space=pltpu.VMEM)

    out_spaces = out_spaces or "v" * len(outs)
    def size(array):
        return math.prod(array.shape) * jnp.dtype(array.dtype).itemsize

    every = list(zip(args, spaces)) + list(zip(outs, out_spaces))
    moved = sum(size(array) for array, kind in every)
    return pl.pallas_call(
        body,
        name=name,
        out_shape=tuple(outs),
        in_specs=[spec(k) for k in spaces],
        out_specs=tuple(spec(k) for k in out_spaces),
        scratch_shapes=list(scratch),
        compiler_params=pltpu.CompilerParams(vmem_limit_bytes=SCOPED[name] << 20),
        cost_estimate=pl.CostEstimate(flops=0, bytes_accessed=moved // 64, transcendentals=0),
    )(*args)


def vector(ref):
    return ref[...].astype(f32).reshape(1, ref.shape[0])


def places_by_axis(index):
    x, y = index & 3, ((index >> 1) & 2) | (index & 1)
    return [x, x ^ 1, x ^ 2, x ^ 3, 4 + y, 4 + (y ^ 1), 4 + (y ^ 2), 4 + (y ^ 3)]


def eighths(index):
    return [index ^ s for s in range(GROUP)]


def places_gathered(index):
    places = places_by_axis(index)
    return places[:4] + places[6:] + places[4:6]


def place_slots(four, other, r, low, rows, places, dest, base, columns):
    for s in range(GROUP):
        at = pl.multiple_of(base + places[s] * rows, rows)
        dest[pl.ds(at, rows), columns] = (other if s % 2 else four)[s // 2, r, low : low + rows]


def put_slots(index, r, rows, low, keep, send, by_axis=False):
    size = rows[0].shape[0]
    x, y = index & 3, ((index >> 1) & 2) | (index & 1)
    for odd in range(2):

        @pl.when((index & 1) == odd)
        def _():
            for d in range(GROUP):
                dest = send if (d ^ odd) & 1 else keep
                spot = (index ^ d) >> 1
                if by_axis:
                    spot = (x ^ d) >> 1 if d < 4 else 2 + ((y ^ (d - 4)) >> 1)
                dest[spot, r, low : low + size] = rows[d]


def normalize(total):
    centred = total - jnp.mean(total, axis=-1, keepdims=True)
    inverse = lax.rsqrt(jnp.mean(centred * centred, axis=-1, keepdims=True) + epsilon)
    return centred * inverse, inverse


def norm_backward(grad_out, normal, inverse, norm_gain):
    scaled = grad_out * norm_gain
    return inverse * (
        scaled
        - jnp.mean(scaled, axis=-1, keepdims=True)
        - normal * jnp.mean(scaled * normal, axis=-1, keepdims=True)
    )


def column_sum(array):
    return jnp.sum(array, axis=0, keepdims=True)


def folded(array):
    return jnp.sum(array.reshape(-1, 8, array.shape[1]), axis=0)


def by_rows(length, body, sums, width):
    def step(i, totals):
        found = body(pl.ds(pl.multiple_of(i * CHUNK, CHUNK), CHUNK))
        return tuple(t + folded(f) for t, f in zip(totals, found))

    zeros = tuple(jnp.zeros((8, width), f32) for _ in range(sums))
    totals = lax.fori_loop(0, length // CHUNK, step, zeros, unroll=2)
    return tuple(column_sum(t) for t in totals)


def band(block, length):
    return max(0, (block - 1) * PASSAGE), min(length, (block + 2) * PASSAGE)


def clear_outside(array, length):
    for b in range(length // PASSAGE):
        lo, hi = band(b, length)
        block = slice(b * PASSAGE, (b + 1) * PASSAGE)
        for low, high in ((0, lo), (hi, length)):
            if high > low:
                shape = (array.shape[0], high - low, PASSAGE)
                array[:, low:high, block] = jnp.zeros(shape, array.dtype)


def fill_bias(bias, seg_row, seg_col, length):
    for b in range(length // PASSAGE):
        lo, hi = band(b, length)
        same = seg_col[lo:hi, :] == seg_row[:, b * PASSAGE : (b + 1) * PASSAGE]
        bias[b, : hi - lo, :] = jnp.where(same, 0.0, -1e30)


def softmax_columns(scores):
    expo = jnp.exp(scores - jnp.max(scores, axis=0, keepdims=True))
    return expo * (1.0 / jnp.sum(expo, axis=0, keepdims=True))


def first_piece(
    index_ref, own_q, own_k, own_v, own_o, query_bias, value_bias, up_bias, out, owns,
    query_row, value_row, up_row, sems,
):
    w = own_q.shape[0]
    rows = w // 2
    small = [
        pltpu.make_async_copy(own, owns.at[pl.ds(m * w, w)], sems.at[3 + m])
        for m, own in enumerate((own_q, own_k, own_v, own_o))
    ]
    small += [
        pltpu.make_async_copy(query_bias, query_row, sems.at[0]),
        pltpu.make_async_copy(value_bias, value_row, sems.at[1]),
        pltpu.make_async_copy(up_bias, up_row, sems.at[2]),
    ]
    for copy in small:
        copy.start()
    for copy in small:
        copy.wait()
    out[:rows, :] = owns[pl.ds(pl.multiple_of(index_ref[0] * rows, rows), rows), :]
    out[rows:, :] = jnp.zeros((EXTRA, out.shape[1]), bf16)
    out[rows : rows + 1, :w] = vector(query_row).astype(bf16)
    out[rows : rows + 1, w : 2 * w] = vector(value_row).astype(bf16)
    out[rows + 1 : rows + 2, :] = vector(up_row).astype(bf16)


def att_forward(
    index_ref, tokens, owns, four, other, bias_0, bias_1, bias_2, bias_3,
    output_bias, seg_row, seg_col,
    queries, keys, values, contexts, normal, inverse, weights, wo,
    bias, probs_t, row, attended,
):
    length, width = tokens.shape
    w = owns.shape[0] // 4
    quarters = width // w
    rows = four.shape[2]
    index = index_ref[0]
    for m in range(3):
        weights[m, :w, :] = owns[m * w : (m + 1) * w, :]
    wo[:w, :] = owns[3 * w :, :]
    for r in range(1, quarters):
        for s in range(GROUP):
            owner = index ^ s
            at = pl.multiple_of(r * w + (owner & 1) * rows, rows)
            source = other if s % 2 else four

            @pl.when(owner < 6)
            def _():
                weights[owner >> 1, pl.ds(at, rows), :] = source[s // 2, r - 1]

            @pl.when(owner >= 6)
            def _():
                wo[pl.ds(at, rows), :] = source[s // 2, r - 1]

    fill_bias(bias, seg_row, seg_col, length)
    clear_outside(probs_t, length)
    for r, source in enumerate((bias_0, bias_1, bias_2, bias_3)):
        for i in range(2):
            piece = source[rows : rows + 1, i * w : (i + 1) * w].astype(f32)
            row[i : i + 1, r * w : (r + 1) * w] = piece
    low = (nt(tokens[...], weights[0]) + row[0:1, :]).astype(bf16)
    queries[...] = (low.astype(f32) * (HEAD_DIM**-0.5)).astype(bf16)
    keys[...] = nt(tokens[...], weights[1]).astype(bf16)
    values[...] = (nt(tokens[...], weights[2]) + row[1:2, :]).astype(bf16)
    first = lax.broadcasted_iota(jnp.int32, (PASSAGE, LANES), 1) < HEAD_DIM
    first_all = lax.broadcasted_iota(jnp.int32, (length, LANES), 1) < HEAD_DIM

    def pair(i, carry):
        at = pl.ds(pl.multiple_of(i * LANES, LANES), LANES)
        for half, mine in enumerate((first, jnp.logical_not(first))):
            for b in range(length // PASSAGE):
                lo, hi = band(b, length)
                block = slice(b * PASSAGE, (b + 1) * PASSAGE)
                q = queries[block, at]
                masked = jnp.where(mine, q, jnp.zeros_like(q))
                scores = nt(keys[lo:hi, at], masked) + bias[b, : hi - lo, :]
                probs_t[half, lo:hi, block] = softmax_columns(scores).astype(bf16)
        found = [tn(probs_t[half], values[:, at]) for half in range(2)]
        contexts[:, at] = jnp.where(first_all, *found).astype(bf16)
        return carry

    lax.fori_loop(0, width // LANES, pair, 0)
    attended[...] = nn(contexts[...], wo[...]) + vector(output_bias)

    def norm(rows):
        n, r = normalize(tokens[rows, :].astype(f32) + attended[rows, :])
        normal[rows, :] = n
        inverse[rows, :] = r
        return ()

    by_rows(length, norm, 0, width)


def gelu_parts(hidden):
    cumulative = 0.5 * (1.0 + lax.erf(hidden * 0.7071067811865476))
    density = jnp.exp(-0.5 * hidden * hidden) * 0.3989422804014327
    return (hidden * cumulative).astype(bf16), (cumulative + hidden * density).astype(bf16)


def ffn_first(
    index_ref, normal, gain, shift, down_bias, bias_0, bias_1, bias_2, own_up, own_down, four, other,
    activated, slope, low_t, mixed, up, down,
):
    units = own_up.shape[1]
    rows = four.shape[2] // 2
    quarters = four.shape[1] + 1
    biases = (bias_0, bias_1, bias_2)
    up_places, down_places = eighths(index_ref[0]), places_gathered(index_ref[0])
    normed = normal[...] * vector(gain) + vector(shift)
    low = normed.astype(bf16)
    low_t[...] = low.T
    mixed[...] = normed + vector(down_bias)
    for r in range(quarters):
        mine = slice(r * units, (r + 1) * units)
        if r == 0:
            up[:, mine] = own_up[...]
            down[mine, :] = own_down[...]
        else:
            place_slots(four, other, r - 1, 0, rows, up_places, up, 0, mine)
            place_slots(four, other, r - 1, rows, rows, down_places, down, r * units, slice(None))
        at = biases[r].shape[0] - EXTRA + 1
        hidden = nn(low, up[:, mine]) + biases[r][at : at + 1, :].astype(f32)
        activated[:, mine], slope[:, mine] = gelu_parts(hidden)
    mixed[...] += nn(activated[...], down[...])


def ffn_last(
    index_ref, normal, cotangent, gain, shift, second_gain, second_shift, bias, activated, mixed,
    four, other,
    output, grad_mixed, grad_two, sums, slope, up, down, keep, send,
    own, total,
):
    length, width = normal.shape
    units = up.shape[1]
    rows = four.shape[2] // 2
    index = index_ref[0]
    place_slots(four, other, 0, 0, rows, eighths(index), up, 0, slice(None))
    place_slots(four, other, 0, rows, rows, places_gathered(index), down, 0, slice(None))
    low = (normal[...] * vector(gain) + vector(shift)).astype(bf16)
    at = bias.shape[0] - EXTRA + 1
    own[...], slope[...] = gelu_parts(nn(low, up[...]) + bias[at : at + 1, :].astype(f32))
    total[...] = mixed[...] + nn(own[...], down[...])
    out_gain, out_shift = vector(second_gain), vector(second_shift)

    def norm(rows):
        n, inverse = normalize(total[rows, :])
        output[rows, :] = (n * out_gain + out_shift).astype(bf16)
        grad_out = cotangent[rows, :].astype(f32)
        two = norm_backward(grad_out, n, inverse, out_gain)
        grad_two[rows, :] = two
        low = two.astype(bf16)
        grad_mixed[rows, :] = low
        return low.astype(f32), grad_out * n, grad_out

    sums[...] = jnp.zeros_like(sums)
    for i, found in enumerate(by_rows(length, norm, 3, width)):
        sums[i : i + 1, :] = found
    quarters = keep.shape[1]
    for r in range(quarters):
        left = own[...] if r == quarters - 1 else activated[:, r * units : (r + 1) * units]
        grad = tn(left, grad_mixed[...]).astype(bf16)
        put_slots(index, r, grad.reshape(GROUP, -1, width), 0, keep, send, True)


def ffn_backward(
    index_ref, grad_mixed, low_t, slope, slope_last, grad_two, normal, inverse, gain_ref, sums_two,
    up, up_last, down, down_last,
    grad_one, grad_attended, keep, send,
    hidden, total,
):
    length, width = grad_mixed.shape
    units = down_last.shape[0]
    quarters, rows = keep.shape[1], keep.shape[2] - EXTRA
    index = index_ref[0]
    low_sums = []
    for r in range(quarters):
        mine = slice(r * units, (r + 1) * units)
        last = r == quarters - 1
        weight = down_last[...] if last else down[mine, :]
        factor = slope_last[...] if last else slope[:, mine]
        low = (nt(grad_mixed[...], weight) * factor.astype(f32)).astype(bf16)
        hidden[:, mine] = low
        low_sums.append(column_sum(low.astype(f32)))
        grad = nn(low_t[...], low).astype(bf16)
        put_slots(index, r, grad.reshape(GROUP, rows, units), 0, keep, send)
    inner = up.shape[1]
    total[...] = nt(hidden[:, :inner], up[...]) + grad_two[...]
    total[...] += nt(hidden[:, inner:], up_last[...])
    gain = vector(gain_ref)

    def norm(at):
        grad_normed = total[at, :]
        n = normal[at, :]
        one = norm_backward(grad_normed, n, inverse[at, :], gain)
        grad_one[at, :] = one
        low = one.astype(bf16)
        grad_attended[at, :] = low
        return low.astype(f32), grad_normed * n, grad_normed

    shared = list(by_rows(length, norm, 3, width))
    shared += [sums_two[i : i + 1, :] for i in range(3)] + [jnp.zeros_like(gain)]
    for r in range(quarters):
        extra = [
            jnp.broadcast_to(total, (EXTRA, units)).astype(bf16) for total in [low_sums[r]] + shared
        ]
        put_slots(index, r, jnp.stack(extra), rows, keep, send)


def att_backward(
    part, index_ref, queries, keys, values, contexts, grad_attended, tokens, wo, seg_row, seg_col,
    grad_queries, grad_keys, grad_values, keep, send,
    grad_contexts, bias, probs_t, scores_t,
):
    length, width = tokens.shape
    quarters, rows = keep.shape[1], keep.shape[2] - EXTRA
    w = 2 * rows
    across = quarters * w
    index = index_ref[0]
    scale = HEAD_DIM**-0.5
    low = part * across
    fill_bias(bias, seg_row, seg_col, length)
    clear_outside(probs_t, length)
    clear_outside(scores_t, length)
    grad_contexts[...] = nt(grad_attended[...], wo[low : low + across, :]).astype(bf16)
    first = lax.broadcasted_iota(jnp.int32, (PASSAGE, LANES), 1) < HEAD_DIM
    first_all = lax.broadcasted_iota(jnp.int32, (length, LANES), 1) < HEAD_DIM

    def pair(i, carry):
        here = pl.ds(pl.multiple_of(i * LANES, LANES), LANES)
        at = pl.ds(pl.multiple_of(low + i * LANES, LANES), LANES)
        found = []
        for half, mine in enumerate((first, jnp.logical_not(first))):
            for b in range(length // PASSAGE):
                lo, hi = band(b, length)
                block = slice(b * PASSAGE, (b + 1) * PASSAGE)
                q = queries[block, at]
                g = grad_contexts[block, here]
                zero = jnp.zeros_like(q)
                scores = nt(keys[lo:hi, at], jnp.where(mine, q, zero)) + bias[b, : hi - lo, :]
                probs = softmax_columns(scores)
                grad_probs = nt(values[lo:hi, at], jnp.where(mine, g, zero))
                inner = jnp.sum(grad_probs * probs, axis=0, keepdims=True)
                probs_t[half, lo:hi, block] = probs.astype(bf16)
                scores_t[half, lo:hi, block] = (probs * (grad_probs - inner)).astype(bf16)
            found.append(
                (
                    tn(scores_t[half], keys[:, at]),
                    nn(scores_t[half], queries[:, at]),
                    nn(probs_t[half], grad_contexts[:, here]),
                )
            )
        dq, dk, dv = (jnp.where(first_all, a, b) for a, b in zip(*found))
        grad_queries[:, here] = (dq * scale).astype(bf16)
        grad_keys[:, here] = dk.astype(bf16)
        grad_values[:, here] = dv.astype(bf16)
        return carry

    lax.fori_loop(0, across // LANES, pair, 0)
    grads = (
        lambda: tn(grad_queries[...], tokens[...]),
        lambda: tn(grad_keys[...], tokens[...]),
        lambda: tn(grad_values[...], tokens[...]),
        lambda: tn(contexts[:, low : low + across], grad_attended[...]),
    )
    grads = [make().astype(bf16).reshape(quarters, 2, rows, width) for make in grads]
    query_sum = column_sum(grad_queries[...].astype(f32))
    value_sum = column_sum(grad_values[...].astype(f32))
    for r in range(quarters):
        put_slots(index, r, [grads[d // 2][r, d % 2] for d in range(GROUP)], 0, keep, send)
        cols = slice(r * w, (r + 1) * w)
        line = jnp.concatenate(
            [query_sum[:, cols], value_sum[:, cols], jnp.zeros((1, width - 2 * w), f32)], axis=1
        )
        line = jnp.broadcast_to(line, (EXTRA, width)).astype(bf16)
        put_slots(index, r, [line] * GROUP, rows, keep, send)


def input_backward(q0, k0, v0, q1, k1, v1, grad_one, weights, out):
    half = q0.shape[1]
    total = grad_one[...]
    for m, (left, right) in enumerate(((q0, q1), (k0, k1), (v0, v1))):
        total += nn(left[...], weights[m, :half]) + nn(right[...], weights[m, half:])
    out[...] = total.astype(bf16)


def finish_down(index_ref, four, other, out):
    rows = four.shape[1]
    for s, place in enumerate(places_by_axis(index_ref[0])):
        at = pl.multiple_of(place * rows, rows)
        out[pl.ds(at, rows), :] = (other if s % 2 else four)[s // 2].astype(f32)


def finish_up(index_ref, four, other, out, sums):
    rows = four.shape[1] - EXTRA
    for s in range(GROUP):
        owner = index_ref[0] ^ s
        slot = (other if s % 2 else four)[s // 2].astype(f32)
        out[pl.ds(pl.multiple_of(owner * rows, rows), rows), :] = slot[:rows]
        sums[pl.ds(pl.multiple_of(owner * EXTRA, EXTRA), EXTRA), :] = slot[rows:]


def finish_att(index_ref, four, other, gq, gk, gv, go, sums, whole):
    rows = four.shape[1] - EXTRA
    w = 2 * rows
    for s in range(GROUP):
        slot = (other if s % 2 else four)[s // 2].astype(f32)
        owner = index_ref[0] ^ s
        whole[pl.ds(pl.multiple_of(owner * rows, rows), rows), :] = slot[:rows]
        sums[pl.ds(pl.multiple_of(owner * EXTRA, EXTRA), EXTRA), :] = slot[rows:]
    for m, out in enumerate((gq, gk, gv, go)):
        out[...] = whole[m * w : (m + 1) * w, :]


def solution(mesh):
    n_dp, n_mp = mesh.shape["dp"], mesh.shape["mp"]
    if n_dp % GROUP or n_mp % 2:
        raise ValueError("mesh")

    def rotate(array, step):
        return lax.ppermute(array, "mp", [(i, (i + step) % n_mp) for i in range(n_mp)])

    def swap(array, bits):
        return lax.ppermute(array, "dp", [(i, i ^ bits) for i in range(n_dp)])

    def plane_swap(array):
        return [array, swap(array, 2), swap(array, 4), swap(array, 6)]

    def add(left, right):
        return (left.astype(f32) + right.astype(f32)).astype(bf16)

    def tie(*arrays):
        return lax.optimization_barrier(arrays)

    def after(array, *others):
        return tie(array, *others)[0]

    def first_axis(bits):
        go = slice(1, None, 2) if bits == 2 else slice(2, None)
        stay = slice(0, None, 2) if bits == 2 else slice(0, 2)
        return go, stay

    def plane_first(keep, got, bits):
        go, stay = first_axis(bits)
        return add(keep[go], got[go]), add(keep[stay], got[stay])

    def line_moves(parts, order):
        found = {r: rotate(parts[i], -r) if r else parts[i] for i, r in enumerate(order)}
        return [found[r] for r in range(n_mp)]

    def line_total(moved):
        moved = [array.astype(f32) for array in moved]
        total = sum(moved[0::2][1:], moved[0]) + sum(moved[1::2][1:], moved[1])
        if n_dp > GROUP:
            groups = [[i + GROUP * k for k in range(n_dp // GROUP)] for i in range(GROUP)]
            total = lax.psum(total, "dp", axis_index_groups=groups)
        return total.astype(bf16)

    def shards(
        tokens,
        segment_ids,
        query_weight,
        query_bias,
        key_weight,
        value_weight,
        value_bias,
        output_weight,
        output_bias,
        first_gain,
        first_shift,
        up_weight,
        up_bias,
        down_weight,
        down_bias,
        second_gain,
        second_shift,
        cotangent,
    ):
        length, width = tokens.shape
        w = query_weight.shape[1]
        units = up_weight.shape[1]
        rows = width // GROUP
        blocks = length // PASSAGE
        half, part = GROUP // 2, units // GROUP
        shape = jax.ShapeDtypeStruct
        place = lax.axis_index("mp")
        within = lax.axis_index("dp") % GROUP
        index = within.astype(jnp.int32).reshape(1)
        seg_row = lax.dynamic_slice_in_dim(segment_ids, place, 1, 0)
        seg_col = seg_row.reshape(length, 1)

        def slot(array, at, size):
            return lax.dynamic_slice_in_dim(array, at * size, size, 0)

        owns = [query_weight.T, key_weight.T, value_weight.T, output_weight]
        piece, owns = call(
            first_piece,
            "first_piece",
            [shape((rows + EXTRA, width), bf16), shape((4 * w, width), bf16)],
            [index, *owns, query_bias, value_bias, up_bias],
            "s" + "h" * 7,
            [
                pltpu.VMEM((w,), bf16),
                pltpu.VMEM((w,), bf16),
                pltpu.VMEM((units,), bf16),
                pltpu.SemaphoreType.DMA((7,)),
            ],
        )
        biases = [piece] + [rotate(piece, r) for r in range(1, n_mp)]
        order = [r for r in range(n_mp) if r != n_mp // 2] + [n_mp // 2]
        ffn_biases = [biases[r] for r in order]
        att_line = jnp.stack([g[:rows] for g in biases[1:]])
        by_x, by_y = within & 3, ((within >> 1) & 2) | (within & 1)
        piece = jnp.concatenate(
            [
                slot(down_weight, by_x, part),
                slot(up_weight, within, rows),
                slot(down_weight, 4 + by_y, part),
            ]
        )
        piece, att_line = tie(piece, att_line)
        ffn_line = [rotate(piece, r) for r in order[1:]]

        def plane_mixed(line):
            up_rows = slice(part, part + rows)
            left = jnp.stack([jnp.concatenate([g[up_rows], g[:part]]) for g in line])
            right = jnp.stack([g[part:] for g in line])
            corner = swap(jnp.stack([g[up_rows] for g in line]), 6)
            return left, swap(left, 2), swap(right, 4), corner, right[:, rows:]

        def slots_mixed(pieces):
            left, from_x, from_y, corner, own = pieces
            return jnp.stack([left, from_x, from_y, jnp.concatenate([corner, own], axis=1)])

        att_four = [att_line] + [swap(att_line, b) for b in (2, 4, 6)]
        att_four, ffn_line[:-1] = tie(att_four, ffn_line[:-1])
        att_four = jnp.stack(att_four)
        att_other = swap(att_four, 1)
        ffn_four = plane_mixed(ffn_line[:-1])
        tok_low = shape((length, width), bf16)
        tok_wide = shape((length, width), f32)
        queries, keys, values, contexts, normal, inverse, weights, wo = call(
            att_forward,
            "att_forward",
            [tok_low] * 4
            + [
                tok_wide,
                shape((length, 1), f32),
                shape((3, n_mp * w, width), bf16),
                shape((n_mp * w, width), bf16),
            ],
            [
                index,
                tokens,
                owns,
                att_four,
                att_other,
                *biases,
                output_bias,
                seg_row,
                seg_col,
            ],
            "s" + "v" * 11,
            [
                pltpu.VMEM((blocks, 3 * PASSAGE, PASSAGE), f32),
                pltpu.VMEM((2, length, length), bf16),
                pltpu.VMEM((8, width), f32),
                pltpu.VMEM((length, width), f32),
            ],
        )
        normal, ffn_four, ffn_line[-1] = tie(normal, ffn_four, ffn_line[-1])
        ffn_four = slots_mixed(ffn_four)
        ffn_other = swap(ffn_four, 1)
        last_four = plane_mixed(ffn_line[-1:])
        inner = (n_mp - 1) * units
        hidden_low = shape((length, inner), bf16)
        activated, slope, low_t, mixed, up, down = call(
            ffn_first,
            "ffn_first",
            [
                hidden_low,
                hidden_low,
                shape((width, length), bf16),
                tok_wide,
                shape((width, inner), bf16),
                shape((inner, width), bf16),
            ],
            [
                index,
                normal,
                first_gain,
                first_shift,
                down_bias,
                *ffn_biases[:-1],
                up_weight,
                down_weight,
                ffn_four,
                ffn_other,
            ],
            "s" + "v" * 11,
        )
        activated, last_four = tie(activated, last_four)
        last_four = slots_mixed(last_four)
        last_other = swap(last_four, 1)
        pieces = shape((half, n_mp, part, width), bf16)
        (
            output,
            grad_mixed,
            grad_two,
            sums_two,
            slope_last,
            up_last,
            down_last,
            keep_down,
            send_down,
        ) = call(
            ffn_last,
            "ffn_last",
            [
                tok_low,
                tok_low,
                tok_wide,
                shape((8, width), f32),
                shape((length, units), bf16),
                shape((width, units), bf16),
                shape((units, width), bf16),
                pieces,
                pieces,
            ],
            [
                index,
                normal,
                cotangent,
                first_gain,
                first_shift,
                second_gain,
                second_shift,
                ffn_biases[-1],
                activated,
                mixed,
                last_four,
                last_other,
            ],
            "s" + "v" * 11,
            [pltpu.VMEM((length, units), bf16), pltpu.VMEM((length, width), f32)],
        )
        got_down = swap(send_down, 1)
        pieces = shape((half, n_mp, rows + EXTRA, units), bf16)
        grad_one, grad_attended, keep_up, send_up = call(
            ffn_backward,
            "ffn_backward",
            [tok_wide, tok_low, pieces, pieces],
            [
                index,
                grad_mixed,
                low_t,
                slope,
                slope_last,
                grad_two,
                normal,
                inverse,
                first_gain,
                sums_two,
                up,
                up_last,
                down,
                down_last,
            ],
            "s" + "v" * 13,
            [pltpu.VMEM((length, n_mp * units), bf16), pltpu.VMEM((length, width), f32)],
        )
        grad_attended, keep_up, send_up, got_down = tie(grad_attended, keep_up, send_up, got_down)
        got_up = swap(send_up, 1)
        leave_x, leave_y = add(keep_down[1], got_down[1]), add(keep_down[3], got_down[3])
        stay_x, stay_y = add(keep_down[0], got_down[0]), add(keep_down[2], got_down[2])
        grad_attended, leave_x, leave_y = tie(grad_attended, leave_x, leave_y)
        come_x, come_y = swap(leave_x, 2), swap(leave_y, 4)

        halves = n_mp // 2
        across = halves * w
        pieces = shape((half, halves, rows + EXTRA, width), bf16)

        def attention(which, grad_attended):
            return call(
                functools.partial(att_backward, which),
                "att_backward",
                [shape((length, across), bf16)] * 3 + [pieces] * 2,
                [
                    index,
                    queries,
                    keys,
                    values,
                    contexts,
                    grad_attended,
                    tokens,
                    wo,
                    seg_row,
                    seg_col,
                ],
                "s" + "v" * 9,
                [
                    pltpu.VMEM((length, across), bf16),
                    pltpu.VMEM((blocks, 3 * PASSAGE, PASSAGE), f32),
                    pltpu.VMEM((2, length, length), bf16),
                    pltpu.VMEM((2, length, length), bf16),
                ],
            )

        q0, k0, v0, keep_left, send_left = attention(0, grad_attended)
        got_up, come_x, come_y, q0, k0, v0, keep_left, send_left = tie(
            got_up, come_x, come_y, q0, k0, v0, keep_left, send_left
        )
        got_left = swap(send_left, 1)
        cut = units // 2
        left, right = slice(0, cut), slice(cut, None)
        leave_l = add(keep_up[1::2, ..., left], got_up[1::2, ..., left])
        leave_r = add(keep_up[2:, ..., right], got_up[2:, ..., right])
        stay_l = add(keep_up[0::2, ..., left], got_up[0::2, ..., left])
        stay_r = add(keep_up[:2, ..., right], got_up[:2, ..., right])
        parts_x, parts_y = add(stay_x, come_x), add(stay_y, come_y)
        grad_attended, leave_l, leave_r, parts_x, parts_y, got_left = tie(
            grad_attended, leave_l, leave_r, parts_x, parts_y, got_left
        )
        come_l, come_r = swap(leave_l, 2), swap(leave_r, 4)
        line_x = line_moves(parts_x, order)
        q1, k1, v1, keep_right, send_right = attention(1, grad_attended)
        q1, k1, v1, keep_right, send_right, come_l, come_r, line_x, parts_y = tie(
            q1, k1, v1, keep_right, send_right, come_l, come_r, line_x, parts_y
        )
        got_right = swap(send_right, 1)
        line_y = line_moves(parts_y, order)
        now_l, now_r = add(stay_l, come_l), add(stay_r, come_r)
        come_l, come_r = swap(now_l[1], 4), swap(now_r[1], 2)
        leave_left, stay_left = plane_first(keep_left, got_left, 2)
        leave_right, stay_right = plane_first(keep_right, got_right, 4)
        (grad_tokens,) = call(
            input_backward,
            "input_backward",
            [tok_low],
            [q0, k0, v0, q1, k1, v1, grad_one, weights],
            "v" * 8,
        )
        come_l, come_r, leave_left, leave_right, grad_tokens = tie(
            come_l, come_r, leave_left, leave_right, grad_tokens
        )
        come_left, come_right = swap(leave_left, 2), swap(leave_right, 4)
        up_parts = jnp.concatenate([add(now_l[0], come_l), add(now_r[0], come_r)], axis=-1)
        up_parts, line_y = tie(up_parts, line_y)
        up_line = line_moves(up_parts, order)
        down_x, down_y = line_total(line_x), line_total(line_y)
        come_left, come_right, up_line[1] = tie(come_left, come_right, up_line[1])
        left_now, right_now = add(stay_left, come_left), add(stay_right, come_right)
        come_left, come_right = swap(left_now[1], 4), swap(right_now[1], 2)
        come_x, come_y = swap(down_x, 4), swap(down_y, 2)
        up_line[2:], come_left, come_right, come_x, come_y = tie(
            up_line[2:], come_left, come_right, come_x, come_y
        )
        left_parts, right_parts = add(left_now[0], come_left), add(right_now[0], come_right)
        att_line = line_moves(
            [left_parts[r] for r in range(halves)] + [right_parts[r] for r in range(halves)],
            range(n_mp),
        )
        up_four = plane_swap(line_total(up_line))
        down_x, down_y = add(down_x, come_x), add(down_y, come_y)
        att_line[1], down_x, down_y = tie(att_line[1], down_x, down_y)
        down_four = [down_x, swap(down_x, 2), down_y, swap(down_y, 4)]
        att_line, down_four, up_four = tie(att_line, down_four, up_four)
        att_four = plane_swap(line_total(att_line))
        down_four, up_four = jnp.stack(down_four), jnp.stack(up_four)
        (grad_down,) = call(
            finish_down,
            "finish_down",
            [shape((units, width), f32)],
            [index, down_four, swap(down_four, 1)],
            "svv",
        )
        grad_up, sums = call(
            finish_up,
            "finish_up",
            [shape((width, units), f32), shape((GROUP * EXTRA, units), f32)],
            [index, up_four, swap(up_four, 1)],
            "svv",
        )
        att_four, grad_down, grad_up, sums = tie(att_four, grad_down, grad_up, sums)
        att_four = jnp.stack(att_four)
        att_other = swap(att_four, 1)
        grad_query, grad_key, grad_value, grad_output, att_sums = call(
            finish_att,
            "finish_att",
            [shape((w, width), f32)] * 4 + [shape((GROUP * EXTRA, width), f32)],
            [index, att_four, att_other],
            "svv",
            [pltpu.VMEM((4 * w, width), f32)],
        )
        return (
            output,
            grad_tokens,
            grad_query.T,
            att_sums[0, :w],
            grad_key.T,
            grad_value.T,
            att_sums[0, w : 2 * w],
            grad_output,
            sums[EXTRA],
            sums[2 * EXTRA],
            sums[3 * EXTRA],
            grad_up,
            sums[0],
            grad_down,
            sums[4 * EXTRA],
            sums[5 * EXTRA],
            sums[6 * EXTRA],
        )

    everywhere, rows, columns, units = P(), P(("dp", "mp"), None), P(None, "mp"), P("mp")
    in_specs = (
        rows,
        P("dp", None),
        columns,
        units,
        columns,
        columns,
        units,
        P("mp", None),
        everywhere,
        everywhere,
        everywhere,
        columns,
        units,
        P("mp", None),
        everywhere,
        everywhere,
        everywhere,
        rows,
    )
    out_specs = (
        rows,
        rows,
        columns,
        units,
        columns,
        columns,
        units,
        P("mp", None),
        everywhere,
        everywhere,
        everywhere,
        columns,
        units,
        P("mp", None),
        everywhere,
        everywhere,
        everywhere,
    )
    return jax.shard_map(shards, mesh=mesh, in_specs=in_specs, out_specs=out_specs, check_vma=False)
```

```python
import functools
import math

import jax
import jax.numpy as jnp
from jax import lax
from jax.experimental import pallas as pl
from jax.experimental.pallas import tpu as pltpu
from jax.sharding import PartitionSpec as P

HEAD_DIM = 64
PASSAGE = 128
GROUP = 8
EXTRA = 8
LANES = 128
CHUNK = 64
SCOPED = {
    "first_piece": 60,
    "att_forward": 7,
    "ffn_first": 5,
    "ffn_last": 10,
    "ffn_slopes": 8,
    "ffn_grads": 5,
    "ffn_norm": 7,
    "att_backward": 11,
    "input_backward": 4,
    "finish_down": 4,
    "finish_up": 4,
    "finish_att": 6,
}
epsilon = 1e-05
bf16 = jnp.bfloat16
f32 = jnp.float32


def nn(left, right):
    return lax.dot_general(left, right, (((1,), (0,)), ((), ())), preferred_element_type=f32)


def nt(left, right):
    return lax.dot_general(left, right, (((1,), (1,)), ((), ())), preferred_element_type=f32)


def tn(left, right):
    return lax.dot_general(left, right, (((0,), (0,)), ((), ())), preferred_element_type=f32)


def call(body, name, outs, args, spaces, scratch=(), out_spaces=None):
    def spec(kind):
        if kind == "s":
            return pl.BlockSpec(memory_space=pltpu.SMEM)
        if kind == "h":
            return pl.BlockSpec(memory_space=pltpu.HBM)
        return pl.BlockSpec(memory_space=pltpu.VMEM)

    out_spaces = out_spaces or "v" * len(outs)
    def size(array):
        return math.prod(array.shape) * jnp.dtype(array.dtype).itemsize

    every = list(zip(args, spaces)) + list(zip(outs, out_spaces))
    moved = sum(size(array) for array, kind in every)
    return pl.pallas_call(
        body,
        name=name,
        out_shape=tuple(outs),
        in_specs=[spec(k) for k in spaces],
        out_specs=tuple(spec(k) for k in out_spaces),
        scratch_shapes=list(scratch),
        compiler_params=pltpu.CompilerParams(vmem_limit_bytes=SCOPED[name] << 20),
        cost_estimate=pl.CostEstimate(flops=0, bytes_accessed=moved // 64, transcendentals=0),
    )(*args)


def vector(ref):
    return ref[...].astype(f32).reshape(1, ref.shape[0])


def places_by_axis(index):
    x, y = index & 3, ((index >> 1) & 2) | (index & 1)
    return [x, x ^ 1, x ^ 2, x ^ 3, 4 + y, 4 + (y ^ 1), 4 + (y ^ 2), 4 + (y ^ 3)]


def eighths(index):
    return [index ^ s for s in range(GROUP)]


def places_gathered(index):
    places = places_by_axis(index)
    return places[:4] + places[6:] + places[4:6]


def place_slots(four, other, r, down_rows, rows, places, dest, base, columns):
    for s in range(GROUP):
        low = rows if (s < GROUP // 2) != down_rows else 0
        at = pl.multiple_of(base + places[s] * rows, rows)
        dest[pl.ds(at, rows), columns] = (other if s % 2 else four)[s // 2, r, low : low + rows]


def put_slots(index, r, rows, low, keep, send, by_axis=False):
    size = rows[0].shape[0]
    x, y = index & 3, ((index >> 1) & 2) | (index & 1)
    for odd in range(2):

        @pl.when((index & 1) == odd)
        def _():
            for d in range(GROUP):
                dest = send if (d ^ odd) & 1 else keep
                spot = (index ^ d) >> 1
                if by_axis:
                    spot = (x ^ d) >> 1 if d < 4 else 2 + ((y ^ (d - 4)) >> 1)
                dest[spot, r, low : low + size] = rows[d]


def normalize(total):
    centred = total - jnp.mean(total, axis=-1, keepdims=True)
    inverse = lax.rsqrt(jnp.mean(centred * centred, axis=-1, keepdims=True) + epsilon)
    return centred * inverse, inverse


def norm_backward(grad_out, normal, inverse, norm_gain):
    scaled = grad_out * norm_gain
    return inverse * (
        scaled
        - jnp.mean(scaled, axis=-1, keepdims=True)
        - normal * jnp.mean(scaled * normal, axis=-1, keepdims=True)
    )


def column_sum(array):
    return jnp.sum(array, axis=0, keepdims=True)


def folded(array):
    return jnp.sum(array.reshape(-1, 8, array.shape[1]), axis=0)


def by_rows(length, body, sums, width):
    def step(i, totals):
        found = body(pl.ds(pl.multiple_of(i * CHUNK, CHUNK), CHUNK))
        return tuple(t + folded(f) for t, f in zip(totals, found))

    zeros = tuple(jnp.zeros((8, width), f32) for _ in range(sums))
    totals = lax.fori_loop(0, length // CHUNK, step, zeros, unroll=2)
    return tuple(column_sum(t) for t in totals)


def band(block, length):
    return max(0, (block - 1) * PASSAGE), min(length, (block + 2) * PASSAGE)


def clear_outside(array, length):
    for b in range(length // PASSAGE):
        lo, hi = band(b, length)
        block = slice(b * PASSAGE, (b + 1) * PASSAGE)
        for low, high in ((0, lo), (hi, length)):
            if high > low:
                shape = (array.shape[0], high - low, PASSAGE)
                array[:, low:high, block] = jnp.zeros(shape, array.dtype)


def fill_bias(bias, seg_row, seg_col, length):
    for b in range(length // PASSAGE):
        lo, hi = band(b, length)
        same = seg_col[lo:hi, :] == seg_row[:, b * PASSAGE : (b + 1) * PASSAGE]
        bias[b, : hi - lo, :] = jnp.where(same, 0.0, -1e30)


def softmax_columns(scores):
    expo = jnp.exp(scores - jnp.max(scores, axis=0, keepdims=True))
    return expo * (1.0 / jnp.sum(expo, axis=0, keepdims=True))


def first_piece(
    index_ref, own_q, own_k, own_v, own_o, query_bias, value_bias, up_bias, out, owns,
    query_row, value_row, up_row, sems,
):
    w = own_q.shape[0]
    rows = w // 2
    small = [
        pltpu.make_async_copy(own, owns.at[pl.ds(m * w, w)], sems.at[3 + m])
        for m, own in enumerate((own_q, own_k, own_v, own_o))
    ]
    small += [
        pltpu.make_async_copy(query_bias, query_row, sems.at[0]),
        pltpu.make_async_copy(value_bias, value_row, sems.at[1]),
        pltpu.make_async_copy(up_bias, up_row, sems.at[2]),
    ]
    for copy in small:
        copy.start()
    for copy in small:
        copy.wait()
    out[:rows, :] = owns[pl.ds(pl.multiple_of(index_ref[0] * rows, rows), rows), :]
    out[rows:, :] = jnp.zeros((EXTRA, out.shape[1]), bf16)
    out[rows : rows + 1, :w] = vector(query_row).astype(bf16)
    out[rows : rows + 1, w : 2 * w] = vector(value_row).astype(bf16)
    out[rows + 1 : rows + 2, :] = vector(up_row).astype(bf16)


def att_forward(
    index_ref, tokens, owns, four, other, bias_0, bias_1, bias_2, bias_3,
    output_bias, seg_row, seg_col,
    queries, keys, values, contexts, normal, inverse, weights, wo,
    bias, probs_t, row, attended,
):
    length, width = tokens.shape
    w = owns.shape[0] // 4
    quarters = width // w
    rows = four.shape[2]
    index = index_ref[0]
    for m in range(3):
        weights[m, :w, :] = owns[m * w : (m + 1) * w, :]
    wo[:w, :] = owns[3 * w :, :]
    for r in range(1, quarters):
        for s in range(GROUP):
            owner = index ^ s
            at = pl.multiple_of(r * w + (owner & 1) * rows, rows)
            source = other if s % 2 else four

            @pl.when(owner < 6)
            def _():
                weights[owner >> 1, pl.ds(at, rows), :] = source[s // 2, r - 1]

            @pl.when(owner >= 6)
            def _():
                wo[pl.ds(at, rows), :] = source[s // 2, r - 1]

    fill_bias(bias, seg_row, seg_col, length)
    clear_outside(probs_t, length)
    for r, source in enumerate((bias_0, bias_1, bias_2, bias_3)):
        for i in range(2):
            piece = source[rows : rows + 1, i * w : (i + 1) * w].astype(f32)
            row[i : i + 1, r * w : (r + 1) * w] = piece
    low = (nt(tokens[...], weights[0]) + row[0:1, :]).astype(bf16)
    queries[...] = (low.astype(f32) * (HEAD_DIM**-0.5)).astype(bf16)
    keys[...] = nt(tokens[...], weights[1]).astype(bf16)
    values[...] = (nt(tokens[...], weights[2]) + row[1:2, :]).astype(bf16)
    first = lax.broadcasted_iota(jnp.int32, (PASSAGE, LANES), 1) < HEAD_DIM
    first_all = lax.broadcasted_iota(jnp.int32, (length, LANES), 1) < HEAD_DIM

    def pair(i, carry):
        at = pl.ds(pl.multiple_of(i * LANES, LANES), LANES)
        for half, mine in enumerate((first, jnp.logical_not(first))):
            for b in range(length // PASSAGE):
                lo, hi = band(b, length)
                block = slice(b * PASSAGE, (b + 1) * PASSAGE)
                q = queries[block, at]
                masked = jnp.where(mine, q, jnp.zeros_like(q))
                scores = nt(keys[lo:hi, at], masked) + bias[b, : hi - lo, :]
                probs_t[half, lo:hi, block] = softmax_columns(scores).astype(bf16)
        found = [tn(probs_t[half], values[:, at]) for half in range(2)]
        contexts[:, at] = jnp.where(first_all, *found).astype(bf16)
        return carry

    lax.fori_loop(0, width // LANES, pair, 0)
    attended[...] = nn(contexts[...], wo[...]) + vector(output_bias)

    def norm(rows):
        n, r = normalize(tokens[rows, :].astype(f32) + attended[rows, :])
        normal[rows, :] = n
        inverse[rows, :] = r
        return ()

    by_rows(length, norm, 0, width)


def gelu_parts(hidden):
    cumulative = 0.5 * (1.0 + lax.erf(hidden * 0.7071067811865476))
    density = jnp.exp(-0.5 * hidden * hidden) * 0.3989422804014327
    return (hidden * cumulative).astype(bf16), (cumulative + hidden * density).astype(bf16)


def ffn_first(
    index_ref, normal, gain, shift, down_bias, bias_0, bias_1, bias_2, own_up, own_down, four, other,
    activated, slope, low_t, mixed, up, down,
):
    units = own_up.shape[1]
    rows = four.shape[2] // 2
    quarters = four.shape[1] + 1
    biases = (bias_0, bias_1, bias_2)
    up_places, down_places = eighths(index_ref[0]), places_gathered(index_ref[0])
    normed = normal[...] * vector(gain) + vector(shift)
    low = normed.astype(bf16)
    low_t[...] = low.T
    mixed[...] = normed + vector(down_bias)
    for r in range(quarters):
        mine = slice(r * units, (r + 1) * units)
        if r == 0:
            up[:, mine] = own_up[...]
            down[mine, :] = own_down[...]
        else:
            place_slots(four, other, r - 1, False, rows, up_places, up, 0, mine)
            place_slots(four, other, r - 1, True, rows, down_places, down, r * units, slice(None))
        at = biases[r].shape[0] - EXTRA + 1
        hidden = nn(low, up[:, mine]) + biases[r][at : at + 1, :].astype(f32)
        activated[:, mine], slope[:, mine] = gelu_parts(hidden)
    mixed[...] += nn(activated[...], down[...])


def ffn_last(
    index_ref, normal, cotangent, gain, shift, second_gain, second_shift, bias, activated, mixed,
    four, other,
    output, grad_mixed, grad_two, sums, slope, up, down, keep, send,
    own, total,
):
    length, width = normal.shape
    units = up.shape[1]
    rows = four.shape[2] // 2
    index = index_ref[0]
    place_slots(four, other, 0, False, rows, eighths(index), up, 0, slice(None))
    place_slots(four, other, 0, True, rows, places_gathered(index), down, 0, slice(None))
    low = (normal[...] * vector(gain) + vector(shift)).astype(bf16)
    at = bias.shape[0] - EXTRA + 1
    own[...], slope[...] = gelu_parts(nn(low, up[...]) + bias[at : at + 1, :].astype(f32))
    total[...] = mixed[...] + nn(own[...], down[...])
    out_gain, out_shift = vector(second_gain), vector(second_shift)

    def norm(rows):
        n, inverse = normalize(total[rows, :])
        output[rows, :] = (n * out_gain + out_shift).astype(bf16)
        grad_out = cotangent[rows, :].astype(f32)
        two = norm_backward(grad_out, n, inverse, out_gain)
        grad_two[rows, :] = two
        low = two.astype(bf16)
        grad_mixed[rows, :] = low
        return low.astype(f32), grad_out * n, grad_out

    sums[...] = jnp.zeros_like(sums)
    for i, found in enumerate(by_rows(length, norm, 3, width)):
        sums[i : i + 1, :] = found
    quarters = keep.shape[1]
    for r in range(quarters):
        left = own[...] if r == quarters - 1 else activated[:, r * units : (r + 1) * units]
        grad = tn(left, grad_mixed[...]).astype(bf16)
        put_slots(index, r, grad.reshape(GROUP, -1, width), 0, keep, send, True)


def ffn_slopes(grad_mixed, slope, slope_last, down, down_last, hidden, sums):
    units = down_last.shape[0]
    sums[...] = jnp.zeros_like(sums)
    for r in range(hidden.shape[1] // units):
        mine = slice(r * units, (r + 1) * units)
        last = mine.stop == hidden.shape[1]
        weight = down_last[...] if last else down[mine, :]
        factor = slope_last[...] if last else slope[:, mine]
        low = (nt(grad_mixed[...], weight) * factor.astype(f32)).astype(bf16)
        hidden[:, mine] = low
        sums[r : r + 1, :] = column_sum(low.astype(f32))


def ffn_grads(index_ref, hidden, low_t, keep, send):
    units = keep.shape[3]
    for r in range(keep.shape[1]):
        grad = nn(low_t[...], hidden[:, r * units : (r + 1) * units]).astype(bf16)
        put_slots(index_ref[0], r, grad.reshape(GROUP, -1, units), 0, keep, send)


def ffn_norm(
    hidden, grad_two, normal, inverse, gain_ref, up, up_last,
    grad_one, grad_attended, sums,
    total,
):
    length, width = normal.shape
    inner = up.shape[1]
    total[...] = nt(hidden[:, :inner], up[...]) + grad_two[...]
    total[...] += nt(hidden[:, inner:], up_last[...])
    gain = vector(gain_ref)

    def norm(at):
        grad_normed = total[at, :]
        n = normal[at, :]
        one = norm_backward(grad_normed, n, inverse[at, :], gain)
        grad_one[at, :] = one
        low = one.astype(bf16)
        grad_attended[at, :] = low
        return low.astype(f32), grad_normed * n, grad_normed

    sums[...] = jnp.zeros_like(sums)
    for i, found in enumerate(by_rows(length, norm, 3, width)):
        sums[i : i + 1, :] = found


def att_backward(
    part, places, index_ref, queries, keys, values, contexts, grad_attended, tokens, wo,
    seg_row, seg_col, unit_sums, sums_one, sums_two,
    grad_queries, grad_keys, grad_values, keep, send,
    grad_contexts, bias, probs_t, scores_t,
):
    length, width = tokens.shape
    quarters, rows = keep.shape[1], keep.shape[2] - EXTRA
    w = 2 * rows
    across = quarters * w
    index = index_ref[0]
    scale = HEAD_DIM**-0.5
    fill_bias(bias, seg_row, seg_col, length)
    clear_outside(probs_t, length)
    clear_outside(scores_t, length)
    low = part * across
    grad_contexts[...] = nt(grad_attended[...], wo[low : low + across, :]).astype(bf16)
    first = lax.broadcasted_iota(jnp.int32, (PASSAGE, LANES), 1) < HEAD_DIM
    first_all = lax.broadcasted_iota(jnp.int32, (length, LANES), 1) < HEAD_DIM

    def pair(i, carry):
        here = pl.ds(pl.multiple_of(i * LANES, LANES), LANES)
        at = pl.ds(pl.multiple_of(low + i * LANES, LANES), LANES)
        found = []
        for half, mine in enumerate((first, jnp.logical_not(first))):
            for b in range(length // PASSAGE):
                lo, hi = band(b, length)
                block = slice(b * PASSAGE, (b + 1) * PASSAGE)
                q = queries[block, at]
                g = grad_contexts[block, here]
                zero = jnp.zeros_like(q)
                scores = nt(keys[lo:hi, at], jnp.where(mine, q, zero)) + bias[b, : hi - lo, :]
                probs = softmax_columns(scores)
                grad_probs = nt(values[lo:hi, at], jnp.where(mine, g, zero))
                inner = jnp.sum(grad_probs * probs, axis=0, keepdims=True)
                probs_t[half, lo:hi, block] = probs.astype(bf16)
                scores_t[half, lo:hi, block] = (probs * (grad_probs - inner)).astype(bf16)
            found.append(
                (
                    tn(scores_t[half], keys[:, at]),
                    nn(scores_t[half], queries[:, at]),
                    nn(probs_t[half], grad_contexts[:, here]),
                )
            )
        dq, dk, dv = (jnp.where(first_all, a, b) for a, b in zip(*found))
        grad_queries[:, here] = (dq * scale).astype(bf16)
        grad_keys[:, here] = dk.astype(bf16)
        grad_values[:, here] = dv.astype(bf16)
        return carry

    lax.fori_loop(0, across // LANES, pair, 0)
    grads = (
        lambda: tn(grad_queries[...], tokens[...]),
        lambda: tn(grad_keys[...], tokens[...]),
        lambda: tn(grad_values[...], tokens[...]),
        lambda: tn(contexts[:, low : low + across], grad_attended[...]),
    )
    grads = [make().astype(bf16).reshape(quarters, 2, rows, width) for make in grads]
    query_sum = column_sum(grad_queries[...].astype(f32))
    value_sum = column_sum(grad_values[...].astype(f32))
    for r in range(quarters):
        put_slots(index, r, [grads[d // 2][r, d % 2] for d in range(GROUP)], 0, keep, send)
        cols = slice(r * w, (r + 1) * w)
        last = jnp.concatenate(
            [query_sum[:, cols], value_sum[:, cols], jnp.zeros((1, width - 2 * w), f32)], axis=1
        )
        at = places[part * quarters + r]
        lines = [unit_sums[at : at + 1, :]]
        lines += [sums[i : i + 1, :] for sums in (sums_one, sums_two) for i in range(3)]
        lines = [jnp.broadcast_to(line, (EXTRA, width)).astype(bf16) for line in lines + [last]]
        put_slots(index, r, lines, rows, keep, send)


def input_backward(q0, k0, v0, q1, k1, v1, grad_one, weights, out):
    half = q0.shape[1]
    total = grad_one[...]
    for m, (left, right) in enumerate(((q0, q1), (k0, k1), (v0, v1))):
        total += nn(left[...], weights[m, :half]) + nn(right[...], weights[m, half:])
    out[...] = total.astype(bf16)


def finish_ffn(places_of, index_ref, four, other, out):
    rows = four.shape[1]
    for s, place in enumerate(places_of(index_ref[0])):
        at = pl.multiple_of(place * rows, rows)
        out[pl.ds(at, rows), :] = (other if s % 2 else four)[s // 2].astype(f32)


def finish_att(index_ref, four, other, gq, gk, gv, go, sums, whole):
    rows = four.shape[1] - EXTRA
    w = 2 * rows
    for s in range(GROUP):
        slot = (other if s % 2 else four)[s // 2].astype(f32)
        owner = index_ref[0] ^ s
        whole[pl.ds(pl.multiple_of(owner * rows, rows), rows), :] = slot[:rows]
        sums[pl.ds(pl.multiple_of(owner * EXTRA, EXTRA), EXTRA), :] = slot[rows:]
    for m, out in enumerate((gq, gk, gv, go)):
        out[...] = whole[m * w : (m + 1) * w, :]


def solution(mesh):
    n_dp, n_mp = mesh.shape["dp"], mesh.shape["mp"]
    if n_dp % GROUP or n_mp % 2:
        raise ValueError("mesh")

    def rotate(array, step):
        return lax.ppermute(array, "mp", [(i, (i + step) % n_mp) for i in range(n_mp)])

    def swap(array, bits):
        return lax.ppermute(array, "dp", [(i, i ^ bits) for i in range(n_dp)])

    def plane_swap(array):
        return [array, swap(array, 2), swap(array, 4), swap(array, 6)]

    def add(left, right):
        return (left.astype(f32) + right.astype(f32)).astype(bf16)

    def tie(*arrays):
        return lax.optimization_barrier(arrays)

    def after(array, *others):
        return tie(array, *others)[0]

    def first_axis(bits):
        go = slice(1, None, 2) if bits == 2 else slice(2, None)
        stay = slice(0, None, 2) if bits == 2 else slice(0, 2)
        return go, stay

    def plane_first(keep, got, bits):
        go, stay = first_axis(bits)
        return add(keep[go], got[go]), add(keep[stay], got[stay])

    def line_moves(parts, order):
        found = {r: rotate(parts[i], -r) if r else parts[i] for i, r in enumerate(order)}
        return [found[r] for r in range(n_mp)]

    def line_total(moved):
        moved = [array.astype(f32) for array in moved]
        total = sum(moved[0::2][1:], moved[0]) + sum(moved[1::2][1:], moved[1])
        if n_dp > GROUP:
            groups = [[i + GROUP * k for k in range(n_dp // GROUP)] for i in range(GROUP)]
            total = lax.psum(total, "dp", axis_index_groups=groups)
        return total.astype(bf16)

    def shards(
        tokens,
        segment_ids,
        query_weight,
        query_bias,
        key_weight,
        value_weight,
        value_bias,
        output_weight,
        output_bias,
        first_gain,
        first_shift,
        up_weight,
        up_bias,
        down_weight,
        down_bias,
        second_gain,
        second_shift,
        cotangent,
    ):
        length, width = tokens.shape
        w = query_weight.shape[1]
        units = up_weight.shape[1]
        rows = width // GROUP
        blocks = length // PASSAGE
        half, part = GROUP // 2, units // GROUP
        shape = jax.ShapeDtypeStruct
        place = lax.axis_index("mp")
        within = lax.axis_index("dp") % GROUP
        index = within.astype(jnp.int32).reshape(1)
        seg_row = lax.dynamic_slice_in_dim(segment_ids, place, 1, 0)
        seg_col = seg_row.reshape(length, 1)

        def slot(array, at, size):
            return lax.dynamic_slice_in_dim(array, at * size, size, 0)

        owns = [query_weight.T, key_weight.T, value_weight.T, output_weight]
        piece, owns = call(
            first_piece,
            "first_piece",
            [shape((rows + EXTRA, width), bf16), shape((4 * w, width), bf16)],
            [index, *owns, query_bias, value_bias, up_bias],
            "s" + "h" * 7,
            [
                pltpu.VMEM((w,), bf16),
                pltpu.VMEM((w,), bf16),
                pltpu.VMEM((units,), bf16),
                pltpu.SemaphoreType.DMA((7,)),
            ],
        )
        biases = [piece] + [rotate(piece, r) for r in range(1, n_mp)]
        order = [r for r in range(n_mp) if r != n_mp // 2] + [n_mp // 2]
        ffn_biases = [biases[r] for r in order]
        att_line = jnp.stack([g[:rows] for g in biases[1:]])
        by_x, by_y = within & 3, ((within >> 1) & 2) | (within & 1)
        piece = jnp.concatenate(
            [
                slot(down_weight, by_x, part),
                slot(up_weight, within, rows),
                slot(down_weight, 4 + by_y, part),
            ]
        )
        piece, att_line = tie(piece, att_line)
        ffn_line = [rotate(piece, r) for r in order[1:]]

        def plane_mixed(line):
            left = jnp.stack([g[: part + rows] for g in line])
            right = jnp.stack([g[part:] for g in line])
            corner = swap(jnp.stack([g[part : part + rows] for g in line]), 6)
            return left, swap(left, 2), swap(right, 4), corner, right[:, rows:]

        def slots_mixed(pieces):
            left, from_x, from_y, corner, own = pieces
            return jnp.stack([left, from_x, from_y, jnp.concatenate([corner, own], axis=1)])

        att_four = [att_line] + [swap(att_line, b) for b in (2, 4, 6)]
        att_four, ffn_line[:-1] = tie(att_four, ffn_line[:-1])
        att_four = jnp.stack(att_four)
        att_other = swap(att_four, 1)
        ffn_four = plane_mixed(ffn_line[:-1])
        tok_low = shape((length, width), bf16)
        tok_wide = shape((length, width), f32)
        queries, keys, values, contexts, normal, inverse, weights, wo = call(
            att_forward,
            "att_forward",
            [tok_low] * 4
            + [
                tok_wide,
                shape((length, 1), f32),
                shape((3, n_mp * w, width), bf16),
                shape((n_mp * w, width), bf16),
            ],
            [
                index,
                tokens,
                owns,
                att_four,
                att_other,
                *biases,
                output_bias,
                seg_row,
                seg_col,
            ],
            "s" + "v" * 11,
            [
                pltpu.VMEM((blocks, 3 * PASSAGE, PASSAGE), f32),
                pltpu.VMEM((2, length, length), bf16),
                pltpu.VMEM((8, width), f32),
                pltpu.VMEM((length, width), f32),
            ],
        )
        normal, ffn_four, ffn_line[-1] = tie(normal, ffn_four, ffn_line[-1])
        ffn_four = slots_mixed(ffn_four)
        ffn_other = swap(ffn_four, 1)
        last_four = plane_mixed(ffn_line[-1:])
        inner = (n_mp - 1) * units
        hidden_low = shape((length, inner), bf16)
        activated, slope, low_t, mixed, up, down = call(
            ffn_first,
            "ffn_first",
            [
                hidden_low,
                hidden_low,
                shape((width, length), bf16),
                tok_wide,
                shape((width, inner), bf16),
                shape((inner, width), bf16),
            ],
            [
                index,
                normal,
                first_gain,
                first_shift,
                down_bias,
                *ffn_biases[:-1],
                up_weight,
                down_weight,
                ffn_four,
                ffn_other,
            ],
            "s" + "v" * 11,
        )
        activated, last_four = tie(activated, last_four)
        last_four = slots_mixed(last_four)
        last_other = swap(last_four, 1)
        pieces = shape((half, n_mp, part, width), bf16)
        (
            output,
            grad_mixed,
            grad_two,
            sums_two,
            slope_last,
            up_last,
            down_last,
            keep_down,
            send_down,
        ) = call(
            ffn_last,
            "ffn_last",
            [
                tok_low,
                tok_low,
                tok_wide,
                shape((8, width), f32),
                shape((length, units), bf16),
                shape((width, units), bf16),
                shape((units, width), bf16),
                pieces,
                pieces,
            ],
            [
                index,
                normal,
                cotangent,
                first_gain,
                first_shift,
                second_gain,
                second_shift,
                ffn_biases[-1],
                activated,
                mixed,
                last_four,
                last_other,
            ],
            "s" + "v" * 11,
            [pltpu.VMEM((length, units), bf16), pltpu.VMEM((length, width), f32)],
        )
        got_down = swap(send_down, 1)
        hidden, low_sums = call(
            ffn_slopes,
            "ffn_slopes",
            [shape((length, n_mp * units), bf16), shape((8, units), f32)],
            [grad_mixed, slope, slope_last, down, down_last],
            "v" * 5,
        )
        hidden, got_down = tie(hidden, got_down)
        leave_x, leave_y = add(keep_down[1], got_down[1]), add(keep_down[3], got_down[3])
        stay_x, stay_y = add(keep_down[0], got_down[0]), add(keep_down[2], got_down[2])
        hidden, leave_x, leave_y = tie(hidden, leave_x, leave_y)
        come_x, come_y = swap(leave_x, 2), swap(leave_y, 4)
        pieces = shape((half, n_mp, rows, units), bf16)
        keep_up, send_up = call(
            ffn_grads, "ffn_grads", [pieces, pieces], [index, hidden, low_t], "svv"
        )
        hidden, keep_up, send_up = tie(hidden, keep_up, send_up)
        got_up = swap(send_up, 1)
        grad_one, grad_attended, sums_one = call(
            ffn_norm,
            "ffn_norm",
            [tok_wide, tok_low, shape((8, width), f32)],
            [hidden, grad_two, normal, inverse, first_gain, up, up_last],
            "v" * 7,
            [pltpu.VMEM((length, width), f32)],
        )
        grad_attended, sums_one, got_up = tie(grad_attended, sums_one, got_up)
        cut = units // 2
        left, right = slice(0, cut), slice(cut, None)

        def plane_halves(keep, got):
            leaves = add(keep[1::2, ..., left], got[1::2, ..., left])
            leaves_r = add(keep[2:, ..., right], got[2:, ..., right])
            stays = add(keep[0::2, ..., left], got[0::2, ..., left])
            stays_r = add(keep[:2, ..., right], got[:2, ..., right])
            return leaves, leaves_r, stays, stays_r

        leave_l, leave_r, stay_l, stay_r = plane_halves(keep_up, got_up)
        grad_attended, leave_l, leave_r = tie(grad_attended, leave_l, leave_r)
        come_l, come_r = swap(leave_l, 2), swap(leave_r, 4)
        halves = n_mp // 2
        across = halves * w
        pieces = shape((half, halves, rows + EXTRA, width), bf16)
        places = [order.index(r) for r in range(n_mp)]

        def attention(which, grad_attended):
            return call(
                functools.partial(att_backward, which, places),
                "att_backward",
                [shape((length, across), bf16)] * 3 + [pieces] * 2,
                [
                    index,
                    queries,
                    keys,
                    values,
                    contexts,
                    grad_attended,
                    tokens,
                    wo,
                    seg_row,
                    seg_col,
                    low_sums,
                    sums_one,
                    sums_two,
                ],
                "s" + "v" * 12,
                [
                    pltpu.VMEM((length, across), bf16),
                    pltpu.VMEM((blocks, 3 * PASSAGE, PASSAGE), f32),
                    pltpu.VMEM((2, length, length), bf16),
                    pltpu.VMEM((2, length, length), bf16),
                ],
            )

        q0, k0, v0, keep_0, send_0 = attention(0, grad_attended)
        come_x, come_y, q0, k0, v0, keep_0, send_0 = tie(
            come_x, come_y, q0, k0, v0, keep_0, send_0
        )
        got_0 = swap(send_0, 1)
        parts_x, parts_y = add(stay_x, come_x), add(stay_y, come_y)
        grad_attended, parts_x, got_0 = tie(grad_attended, parts_x, got_0)
        line_x = line_moves(parts_x, order)
        q1, k1, v1, keep_1, send_1 = attention(1, grad_attended)
        q1, k1, v1, keep_1, send_1, come_l, come_r, line_x[1:], parts_y = tie(
            q1, k1, v1, keep_1, send_1, come_l, come_r, line_x[1:], parts_y
        )
        got_1 = swap(send_1, 1)
        line_y = line_moves(parts_y, order)
        now_l, now_r = add(stay_l, come_l), add(stay_r, come_r)
        come_l, come_r = swap(now_l[1], 4), swap(now_r[1], 2)
        keep_att = jnp.concatenate([keep_0, keep_1], axis=1)
        got_att = jnp.concatenate([got_0, got_1], axis=1)
        leave_left, leave_right, stay_left, stay_right = plane_halves(keep_att, got_att)
        come_l, come_r, leave_left, leave_right = tie(come_l, come_r, leave_left, leave_right)
        come_left, come_right = swap(leave_left, 2), swap(leave_right, 4)
        up_parts = jnp.concatenate([add(now_l[0], come_l), add(now_r[0], come_r)], axis=-1)
        up_parts, line_y = tie(up_parts, line_y)
        up_line = line_moves(up_parts, order)
        down_x, down_y = line_total(line_x), line_total(line_y)
        come_left, come_right, up_line[1:3], down_x, down_y = tie(
            come_left, come_right, up_line[1:3], down_x, down_y
        )
        left_now, right_now = add(stay_left, come_left), add(stay_right, come_right)
        come_left, come_right = swap(left_now[1], 4), swap(right_now[1], 2)
        come_x, come_y = swap(down_x, 4), swap(down_y, 2)
        up_line[3:], come_left, come_right, come_x, come_y = tie(
            up_line[3:], come_left, come_right, come_x, come_y
        )
        att_parts = jnp.concatenate(
            [add(left_now[0], come_left), add(right_now[0], come_right)], axis=-1
        )
        att_line = line_moves(att_parts, range(n_mp))
        down_x, down_y = add(down_x, come_x), add(down_y, come_y)
        come_x, come_y = swap(down_x, 2), swap(down_y, 4)
        up_total = line_total(up_line)
        (grad_tokens,) = call(
            input_backward,
            "input_backward",
            [tok_low],
            [q0, k0, v0, q1, k1, v1, grad_one, weights],
            "v" * 8,
        )
        att_line[1], come_x, come_y, up_total, grad_tokens = tie(
            att_line[1], come_x, come_y, up_total, grad_tokens
        )
        up_four = plane_swap(up_total)
        down_four = [down_x, come_x, down_y, come_y]
        att_line[2:], up_four = tie(att_line[2:], up_four)
        att_four = plane_swap(line_total(att_line))
        down_four, up_four = jnp.stack(down_four), jnp.stack(up_four)
        (grad_down,) = call(
            functools.partial(finish_ffn, places_by_axis),
            "finish_down",
            [shape((units, width), f32)],
            [index, down_four, swap(down_four, 1)],
            "svv",
        )
        (grad_up,) = call(
            functools.partial(finish_ffn, eighths),
            "finish_up",
            [shape((width, units), f32)],
            [index, up_four, swap(up_four, 1)],
            "svv",
        )
        att_four, grad_down, grad_up = tie(att_four, grad_down, grad_up)
        att_four = jnp.stack(att_four)
        att_other = swap(att_four, 1)
        grad_query, grad_key, grad_value, grad_output, sums = call(
            finish_att,
            "finish_att",
            [shape((w, width), f32)] * 4 + [shape((GROUP * EXTRA, width), f32)],
            [index, att_four, att_other],
            "svv",
            [pltpu.VMEM((4 * w, width), f32)],
        )
        return (
            output,
            grad_tokens,
            grad_query.T,
            sums[(GROUP - 1) * EXTRA, :w],
            grad_key.T,
            grad_value.T,
            sums[(GROUP - 1) * EXTRA, w : 2 * w],
            grad_output,
            sums[EXTRA],
            sums[2 * EXTRA],
            sums[3 * EXTRA],
            grad_up,
            sums[0],
            grad_down,
            sums[4 * EXTRA],
            sums[5 * EXTRA],
            sums[6 * EXTRA],
        )

    everywhere, rows, columns, units = P(), P(("dp", "mp"), None), P(None, "mp"), P("mp")
    in_specs = (
        rows,
        P("dp", None),
        columns,
        units,
        columns,
        columns,
        units,
        P("mp", None),
        everywhere,
        everywhere,
        everywhere,
        columns,
        units,
        P("mp", None),
        everywhere,
        everywhere,
        everywhere,
        rows,
    )
    out_specs = (
        rows,
        rows,
        columns,
        units,
        columns,
        columns,
        units,
        P("mp", None),
        everywhere,
        everywhere,
        everywhere,
        columns,
        units,
        P("mp", None),
        everywhere,
        everywhere,
        everywhere,
    )
    return jax.shard_map(shards, mesh=mesh, in_specs=in_specs, out_specs=out_specs, check_vma=False)
```

```python
import functools
import math

import jax
import jax.numpy as jnp
from jax import lax
from jax.experimental import pallas as pl
from jax.experimental.pallas import tpu as pltpu
from jax.sharding import PartitionSpec as P

HEAD_DIM = 64
PASSAGE = 128
GROUP = 8
EXTRA = 8
LANES = 128
CHUNK = 128
SCOPED = {
    "first_piece": 60,
    "att_forward": 7,
    "ffn_first": 5,
    "ffn_last": 10,
    "ffn_slopes": 8,
    "ffn_grads": 5,
    "ffn_norm": 7,
    "att_backward": 11,
    "input_backward": 4,
    "finish_down": 4,
    "finish_up": 4,
    "finish_att": 6,
}
epsilon = 1e-05
bf16 = jnp.bfloat16
f32 = jnp.float32


def nn(left, right):
    return lax.dot_general(left, right, (((1,), (0,)), ((), ())), preferred_element_type=f32)


def nt(left, right):
    return lax.dot_general(left, right, (((1,), (1,)), ((), ())), preferred_element_type=f32)


def tn(left, right):
    return lax.dot_general(left, right, (((0,), (0,)), ((), ())), preferred_element_type=f32)


def call(body, name, outs, args, spaces, scratch=(), out_spaces=None):
    def spec(kind):
        if kind == "s":
            return pl.BlockSpec(memory_space=pltpu.SMEM)
        if kind == "h":
            return pl.BlockSpec(memory_space=pltpu.HBM)
        return pl.BlockSpec(memory_space=pltpu.VMEM)

    out_spaces = out_spaces or "v" * len(outs)
    def size(array):
        return math.prod(array.shape) * jnp.dtype(array.dtype).itemsize

    every = list(zip(args, spaces)) + list(zip(outs, out_spaces))
    moved = sum(size(array) for array, kind in every)
    return pl.pallas_call(
        body,
        name=name,
        out_shape=tuple(outs),
        in_specs=[spec(k) for k in spaces],
        out_specs=tuple(spec(k) for k in out_spaces),
        scratch_shapes=list(scratch),
        compiler_params=pltpu.CompilerParams(vmem_limit_bytes=SCOPED[name] << 20),
        cost_estimate=pl.CostEstimate(flops=0, bytes_accessed=moved // 64, transcendentals=0),
    )(*args)


def vector(ref):
    return ref[...].astype(f32).reshape(1, ref.shape[0])


def places_by_axis(index):
    x, y = index & 3, ((index >> 1) & 2) | (index & 1)
    return [x, x ^ 1, x ^ 2, x ^ 3, 4 + y, 4 + (y ^ 1), 4 + (y ^ 2), 4 + (y ^ 3)]


def eighths(index):
    return [index ^ s for s in range(GROUP)]


def places_gathered(index):
    places = places_by_axis(index)
    return places[:4] + places[6:] + places[4:6]


def place_slots(four, other, r, down_rows, rows, places, dest, base, columns):
    for s in range(GROUP):
        low = rows if (s < GROUP // 2) != down_rows else 0
        at = pl.multiple_of(base + places[s] * rows, rows)
        dest[pl.ds(at, rows), columns] = (other if s % 2 else four)[s // 2, r, low : low + rows]


def put_slots(index, r, rows, low, keep, send, by_axis=False):
    size = rows[0].shape[0]
    x, y = index & 3, ((index >> 1) & 2) | (index & 1)
    for odd in range(2):

        @pl.when((index & 1) == odd)
        def _():
            for d in range(GROUP):
                dest = send if (d ^ odd) & 1 else keep
                spot = (index ^ d) >> 1
                if by_axis:
                    spot = (x ^ d) >> 1 if d < 4 else 2 + ((y ^ (d - 4)) >> 1)
                dest[spot, r, low : low + size] = rows[d]


def normalize(total):
    centred = total - jnp.mean(total, axis=-1, keepdims=True)
    inverse = lax.rsqrt(jnp.mean(centred * centred, axis=-1, keepdims=True) + epsilon)
    return centred * inverse, inverse


def norm_backward(grad_out, normal, inverse, norm_gain):
    scaled = grad_out * norm_gain
    return inverse * (
        scaled
        - jnp.mean(scaled, axis=-1, keepdims=True)
        - normal * jnp.mean(scaled * normal, axis=-1, keepdims=True)
    )


def column_sum(array):
    return jnp.sum(array, axis=0, keepdims=True)


def folded(array):
    return jnp.sum(array.reshape(-1, 8, array.shape[1]), axis=0)


def by_rows(length, body, sums, width):
    def step(i, totals):
        found = body(pl.ds(pl.multiple_of(i * CHUNK, CHUNK), CHUNK))
        return tuple(t + folded(f) for t, f in zip(totals, found))

    zeros = tuple(jnp.zeros((8, width), f32) for _ in range(sums))
    totals = lax.fori_loop(0, length // CHUNK, step, zeros, unroll=1)
    return tuple(column_sum(t) for t in totals)


def band(block, length):
    return max(0, (block - 1) * PASSAGE), min(length, (block + 2) * PASSAGE)


def clear_outside(array, length):
    for b in range(length // PASSAGE):
        lo, hi = band(b, length)
        block = slice(b * PASSAGE, (b + 1) * PASSAGE)
        for low, high in ((0, lo), (hi, length)):
            if high > low:
                shape = (array.shape[0], high - low, PASSAGE)
                array[:, low:high, block] = jnp.zeros(shape, array.dtype)


def fill_bias(bias, seg_row, seg_col, length):
    for b in range(length // PASSAGE):
        lo, hi = band(b, length)
        same = seg_col[lo:hi, :] == seg_row[:, b * PASSAGE : (b + 1) * PASSAGE]
        bias[b, : hi - lo, :] = jnp.where(same, 0.0, -1e30)


def softmax_columns(scores):
    expo = jnp.exp(scores - jnp.max(scores, axis=0, keepdims=True))
    return expo * (1.0 / jnp.sum(expo, axis=0, keepdims=True))


def first_piece(
    index_ref, own_q, own_k, own_v, own_o, query_bias, value_bias, up_bias, out, owns,
    query_row, value_row, up_row, sems,
):
    w = own_q.shape[0]
    rows = w // 2
    small = [
        pltpu.make_async_copy(own, owns.at[pl.ds(m * w, w)], sems.at[3 + m])
        for m, own in enumerate((own_q, own_k, own_v, own_o))
    ]
    small += [
        pltpu.make_async_copy(query_bias, query_row, sems.at[0]),
        pltpu.make_async_copy(value_bias, value_row, sems.at[1]),
        pltpu.make_async_copy(up_bias, up_row, sems.at[2]),
    ]
    for copy in small:
        copy.start()
    for copy in small:
        copy.wait()
    out[:rows, :] = owns[pl.ds(pl.multiple_of(index_ref[0] * rows, rows), rows), :]
    out[rows:, :] = jnp.zeros((EXTRA, out.shape[1]), bf16)
    out[rows : rows + 1, :w] = vector(query_row).astype(bf16)
    out[rows : rows + 1, w : 2 * w] = vector(value_row).astype(bf16)
    out[rows + 1 : rows + 2, :] = vector(up_row).astype(bf16)


def att_forward(
    index_ref, tokens, owns, four, other, bias_0, bias_1, bias_2, bias_3,
    output_bias, seg_row, seg_col,
    queries, keys, values, contexts, normal, inverse, weights, wo,
    bias, probs_t, row, attended,
):
    length, width = tokens.shape
    w = owns.shape[0] // 4
    quarters = width // w
    rows = four.shape[2]
    index = index_ref[0]
    for m in range(3):
        weights[m, :w, :] = owns[m * w : (m + 1) * w, :]
    wo[:w, :] = owns[3 * w :, :]
    for r in range(1, quarters):
        for s in range(GROUP):
            owner = index ^ s
            at = pl.multiple_of(r * w + (owner & 1) * rows, rows)
            source = other if s % 2 else four

            @pl.when(owner < 6)
            def _():
                weights[owner >> 1, pl.ds(at, rows), :] = source[s // 2, r - 1]

            @pl.when(owner >= 6)
            def _():
                wo[pl.ds(at, rows), :] = source[s // 2, r - 1]

    fill_bias(bias, seg_row, seg_col, length)
    clear_outside(probs_t, length)
    for r, source in enumerate((bias_0, bias_1, bias_2, bias_3)):
        for i in range(2):
            piece = source[rows : rows + 1, i * w : (i + 1) * w].astype(f32)
            row[i : i + 1, r * w : (r + 1) * w] = piece
    low = (nt(tokens[...], weights[0]) + row[0:1, :]).astype(bf16)
    queries[...] = (low.astype(f32) * (HEAD_DIM**-0.5)).astype(bf16)
    keys[...] = nt(tokens[...], weights[1]).astype(bf16)
    values[...] = (nt(tokens[...], weights[2]) + row[1:2, :]).astype(bf16)
    lane = lax.broadcasted_iota(jnp.int32, (PASSAGE, LANES), 1) // HEAD_DIM
    lane_all = lax.broadcasted_iota(jnp.int32, (length, LANES), 1) // HEAD_DIM

    def head(i, carry):
        half = i & 1
        at = pl.ds(pl.multiple_of((i >> 1) * LANES, LANES), LANES)
        for b in range(length // PASSAGE):
            lo, hi = band(b, length)
            block = slice(b * PASSAGE, (b + 1) * PASSAGE)
            q = queries[block, at]
            masked = jnp.where(lane == half, q, jnp.zeros_like(q))
            scores = nt(keys[lo:hi, at], masked) + bias[b, : hi - lo, :]
            probs_t[0, lo:hi, block] = softmax_columns(scores).astype(bf16)
        found = tn(probs_t[0], values[:, at]).astype(bf16)
        contexts[:, at] = jnp.where(lane_all == half, found, contexts[:, at])
        return carry

    lax.fori_loop(0, width // HEAD_DIM, head, 0)
    attended[...] = nn(contexts[...], wo[...]) + vector(output_bias)

    def norm(rows):
        n, r = normalize(tokens[rows, :].astype(f32) + attended[rows, :])
        normal[rows, :] = n
        inverse[rows, :] = r
        return ()

    by_rows(length, norm, 0, width)


def gelu_rows(hidden, activated, slope, columns):
    def step(i, carry):
        rows = pl.ds(pl.multiple_of(i * CHUNK, CHUNK), CHUNK)
        value = hidden[rows, :]
        cumulative = 0.5 * (1.0 + lax.erf(value * 0.7071067811865476))
        density = jnp.exp(-0.5 * value * value) * 0.3989422804014327
        activated[rows, columns] = (value * cumulative).astype(bf16)
        slope[rows, columns] = (cumulative + value * density).astype(bf16)
        return carry

    lax.fori_loop(0, hidden.shape[0] // CHUNK, step, 0)


def each(count, body):
    def step(r, carry):
        body(r)
        return carry

    lax.fori_loop(0, count, step, 0)


def columns_of(r, size):
    return pl.ds(pl.multiple_of(r * size, LANES), size)


def ffn_first(
    index_ref, normal, gain, shift, down_bias, bias_0, bias_1, bias_2, own_up, own_down, four, other,
    activated, slope, low_t, mixed, up, down,
    hidden, lines, low_rows,
):
    units = own_up.shape[1]
    rows = four.shape[2] // 2
    quarters = four.shape[1] + 1
    biases = (bias_0, bias_1, bias_2)
    up_places, down_places = eighths(index_ref[0]), places_gathered(index_ref[0])
    normed = normal[...] * vector(gain) + vector(shift)
    low = normed.astype(bf16)
    low_t[...] = low.T
    low_rows[...] = low
    mixed[...] = normed + vector(down_bias)
    for r in range(quarters):
        mine = slice(r * units, (r + 1) * units)
        if r == 0:
            up[:, mine] = own_up[...]
            down[mine, :] = own_down[...]
        else:
            place_slots(four, other, r - 1, False, rows, up_places, up, 0, mine)
            place_slots(four, other, r - 1, True, rows, down_places, down, r * units, slice(None))
        at = biases[r].shape[0] - EXTRA + 1
        lines[r, :, :] = jnp.broadcast_to(biases[r][at : at + 1, :].astype(f32), lines.shape[1:])

    def quarter(r):
        mine = columns_of(r, units)
        hidden[...] = nn(low_rows[...], up[:, mine]) + lines[r, 0:1, :]
        gelu_rows(hidden, activated, slope, mine)

    each(quarters, quarter)
    mixed[...] += nn(activated[...], down[...])


def ffn_last(
    index_ref, normal, cotangent, gain, shift, second_gain, second_shift, bias, activated, mixed,
    four, other,
    output, grad_mixed, grad_two, sums, slope, up, down, keep, send,
    own, total,
):
    length, width = normal.shape
    units = up.shape[1]
    rows = four.shape[2] // 2
    index = index_ref[0]
    place_slots(four, other, 0, False, rows, eighths(index), up, 0, slice(None))
    place_slots(four, other, 0, True, rows, places_gathered(index), down, 0, slice(None))
    low = (normal[...] * vector(gain) + vector(shift)).astype(bf16)
    at = bias.shape[0] - EXTRA + 1
    total[...] = nn(low, up[...]) + bias[at : at + 1, :].astype(f32)
    gelu_rows(total, own, slope, slice(None))
    total[...] = mixed[...] + nn(own[...], down[...])
    out_gain, out_shift = vector(second_gain), vector(second_shift)

    def norm(rows):
        n, inverse = normalize(total[rows, :])
        output[rows, :] = (n * out_gain + out_shift).astype(bf16)
        grad_out = cotangent[rows, :].astype(f32)
        two = norm_backward(grad_out, n, inverse, out_gain)
        grad_two[rows, :] = two
        low = two.astype(bf16)
        grad_mixed[rows, :] = low
        return low.astype(f32), grad_out * n, grad_out

    sums[...] = jnp.zeros_like(sums)
    for i, found in enumerate(by_rows(length, norm, 3, width)):
        sums[i : i + 1, :] = found

    def put(r, left):
        grad = tn(left, grad_mixed[...]).astype(bf16)
        put_slots(index, r, grad.reshape(GROUP, -1, width), 0, keep, send, True)

    each(keep.shape[1] - 1, lambda r: put(r, activated[:, columns_of(r, units)]))
    put(keep.shape[1] - 1, own[...])


def ffn_slopes(grad_mixed, slope, slope_last, down, down_last, hidden, sums):
    units = down_last.shape[0]
    sums[...] = jnp.zeros_like(sums)

    def quarter(r, weight, factor):
        low = (nt(grad_mixed[...], weight) * factor.astype(f32)).astype(bf16)
        hidden[:, columns_of(r, units)] = low
        sums[pl.ds(r, 1), :] = column_sum(low.astype(f32))

    def inner(r):
        mine = columns_of(r, units)
        quarter(r, down[mine, :], slope[:, mine])

    each(down.shape[0] // units, inner)
    quarter(down.shape[0] // units, down_last[...], slope_last[...])


def ffn_grads(index_ref, hidden, low_t, keep, send):
    units = keep.shape[3]

    def quarter(r):
        grad = nn(low_t[...], hidden[:, columns_of(r, units)]).astype(bf16)
        put_slots(index_ref[0], r, grad.reshape(GROUP, -1, units), 0, keep, send)

    each(keep.shape[1], quarter)


def ffn_norm(
    hidden, grad_two, normal, inverse, gain_ref, up, up_last,
    grad_one, grad_attended, sums,
    total,
):
    length, width = normal.shape
    inner = up.shape[1]
    total[...] = nt(hidden[:, :inner], up[...]) + grad_two[...]
    total[...] += nt(hidden[:, inner:], up_last[...])
    gain = vector(gain_ref)

    def norm(at):
        grad_normed = total[at, :]
        n = normal[at, :]
        one = norm_backward(grad_normed, n, inverse[at, :], gain)
        grad_one[at, :] = one
        low = one.astype(bf16)
        grad_attended[at, :] = low
        return low.astype(f32), grad_normed * n, grad_normed

    sums[...] = jnp.zeros_like(sums)
    for i, found in enumerate(by_rows(length, norm, 3, width)):
        sums[i : i + 1, :] = found


def att_backward(
    part, places, index_ref, queries, keys, values, contexts, grad_attended, tokens, wo,
    seg_row, seg_col, unit_sums, sums_one, sums_two,
    grad_queries, grad_keys, grad_values, keep, send,
    grad_contexts, bias, probs_t, scores_t,
):
    length, width = tokens.shape
    quarters, rows = keep.shape[1], keep.shape[2] - EXTRA
    w = 2 * rows
    across = quarters * w
    index = index_ref[0]
    scale = HEAD_DIM**-0.5
    fill_bias(bias, seg_row, seg_col, length)
    clear_outside(probs_t, length)
    clear_outside(scores_t, length)
    low = part * across
    grad_contexts[...] = nt(grad_attended[...], wo[low : low + across, :]).astype(bf16)
    lane = lax.broadcasted_iota(jnp.int32, (PASSAGE, LANES), 1) // HEAD_DIM
    lane_all = lax.broadcasted_iota(jnp.int32, (length, LANES), 1) // HEAD_DIM

    def head(i, carry):
        half = i & 1
        here = pl.ds(pl.multiple_of((i >> 1) * LANES, LANES), LANES)
        at = pl.ds(pl.multiple_of(low + (i >> 1) * LANES, LANES), LANES)
        mine = lane == half
        for b in range(length // PASSAGE):
            lo, hi = band(b, length)
            block = slice(b * PASSAGE, (b + 1) * PASSAGE)
            q = queries[block, at]
            g = grad_contexts[block, here]
            zero = jnp.zeros_like(q)
            scores = nt(keys[lo:hi, at], jnp.where(mine, q, zero)) + bias[b, : hi - lo, :]
            probs = softmax_columns(scores)
            grad_probs = nt(values[lo:hi, at], jnp.where(mine, g, zero))
            inner = jnp.sum(grad_probs * probs, axis=0, keepdims=True)
            probs_t[0, lo:hi, block] = probs.astype(bf16)
            scores_t[0, lo:hi, block] = (probs * (grad_probs - inner)).astype(bf16)
        mine = lane_all == half
        for out, found in (
            (grad_queries, tn(scores_t[0], keys[:, at]) * scale),
            (grad_keys, nn(scores_t[0], queries[:, at])),
            (grad_values, nn(probs_t[0], grad_contexts[:, here])),
        ):
            out[:, here] = jnp.where(mine, found.astype(bf16), out[:, here])
        return carry

    lax.fori_loop(0, across // HEAD_DIM, head, 0)
    grads = (
        lambda: tn(grad_queries[...], tokens[...]),
        lambda: tn(grad_keys[...], tokens[...]),
        lambda: tn(grad_values[...], tokens[...]),
        lambda: tn(contexts[:, low : low + across], grad_attended[...]),
    )
    grads = [make().astype(bf16).reshape(quarters, 2, rows, width) for make in grads]
    query_sum = column_sum(grad_queries[...].astype(f32))
    value_sum = column_sum(grad_values[...].astype(f32))
    for r in range(quarters):
        put_slots(index, r, [grads[d // 2][r, d % 2] for d in range(GROUP)], 0, keep, send)
        cols = slice(r * w, (r + 1) * w)
        last = jnp.concatenate(
            [query_sum[:, cols], value_sum[:, cols], jnp.zeros((1, width - 2 * w), f32)], axis=1
        )
        at = places[part * quarters + r]
        lines = [unit_sums[at : at + 1, :]]
        lines += [sums[i : i + 1, :] for sums in (sums_one, sums_two) for i in range(3)]
        lines = [jnp.broadcast_to(line, (EXTRA, width)).astype(bf16) for line in lines + [last]]
        put_slots(index, r, lines, rows, keep, send)


def input_backward(q0, k0, v0, q1, k1, v1, grad_one, weights, out):
    half = q0.shape[1]
    total = grad_one[...]
    for m, (left, right) in enumerate(((q0, q1), (k0, k1), (v0, v1))):
        total += nn(left[...], weights[m, :half]) + nn(right[...], weights[m, half:])
    out[...] = total.astype(bf16)


def finish_ffn(places_of, index_ref, four, other, out):
    rows = four.shape[1]
    for s, place in enumerate(places_of(index_ref[0])):
        at = pl.multiple_of(place * rows, rows)
        out[pl.ds(at, rows), :] = (other if s % 2 else four)[s // 2].astype(f32)


def finish_att(index_ref, four, other, gq, gk, gv, go, sums, whole):
    rows = four.shape[1] - EXTRA
    w = 2 * rows
    for s in range(GROUP):
        slot = (other if s % 2 else four)[s // 2].astype(f32)
        owner = index_ref[0] ^ s
        whole[pl.ds(pl.multiple_of(owner * rows, rows), rows), :] = slot[:rows]
        sums[pl.ds(pl.multiple_of(owner * EXTRA, EXTRA), EXTRA), :] = slot[rows:]
    for m, out in enumerate((gq, gk, gv, go)):
        out[...] = whole[m * w : (m + 1) * w, :]


def solution(mesh):
    n_dp, n_mp = mesh.shape["dp"], mesh.shape["mp"]
    if n_dp % GROUP or n_mp % 2:
        raise ValueError("mesh")

    def rotate(array, step):
        return lax.ppermute(array, "mp", [(i, (i + step) % n_mp) for i in range(n_mp)])

    def swap(array, bits):
        return lax.ppermute(array, "dp", [(i, i ^ bits) for i in range(n_dp)])

    def plane_swap(array):
        return [array, swap(array, 2), swap(array, 4), swap(array, 6)]

    def add(left, right):
        return (left.astype(f32) + right.astype(f32)).astype(bf16)

    def tie(*arrays):
        return lax.optimization_barrier(arrays)

    def after(array, *others):
        return tie(array, *others)[0]

    def first_axis(bits):
        go = slice(1, None, 2) if bits == 2 else slice(2, None)
        stay = slice(0, None, 2) if bits == 2 else slice(0, 2)
        return go, stay

    def plane_first(keep, got, bits):
        go, stay = first_axis(bits)
        return add(keep[go], got[go]), add(keep[stay], got[stay])

    def line_moves(parts, order):
        found = {r: rotate(parts[i], -r) if r else parts[i] for i, r in enumerate(order)}
        return [found[r] for r in range(n_mp)]

    def line_total(moved):
        moved = [array.astype(f32) for array in moved]
        total = sum(moved[0::2][1:], moved[0]) + sum(moved[1::2][1:], moved[1])
        if n_dp > GROUP:
            groups = [[i + GROUP * k for k in range(n_dp // GROUP)] for i in range(GROUP)]
            total = lax.psum(total, "dp", axis_index_groups=groups)
        return total.astype(bf16)

    def shards(
        tokens,
        segment_ids,
        query_weight,
        query_bias,
        key_weight,
        value_weight,
        value_bias,
        output_weight,
        output_bias,
        first_gain,
        first_shift,
        up_weight,
        up_bias,
        down_weight,
        down_bias,
        second_gain,
        second_shift,
        cotangent,
    ):
        length, width = tokens.shape
        w = query_weight.shape[1]
        units = up_weight.shape[1]
        rows = width // GROUP
        blocks = length // PASSAGE
        half, part = GROUP // 2, units // GROUP
        shape = jax.ShapeDtypeStruct
        place = lax.axis_index("mp")
        within = lax.axis_index("dp") % GROUP
        index = within.astype(jnp.int32).reshape(1)
        seg_row = lax.dynamic_slice_in_dim(segment_ids, place, 1, 0)
        seg_col = seg_row.reshape(length, 1)

        def slot(array, at, size):
            return lax.dynamic_slice_in_dim(array, at * size, size, 0)

        owns = [query_weight.T, key_weight.T, value_weight.T, output_weight]
        piece, owns = call(
            first_piece,
            "first_piece",
            [shape((rows + EXTRA, width), bf16), shape((4 * w, width), bf16)],
            [index, *owns, query_bias, value_bias, up_bias],
            "s" + "h" * 7,
            [
                pltpu.VMEM((w,), bf16),
                pltpu.VMEM((w,), bf16),
                pltpu.VMEM((units,), bf16),
                pltpu.SemaphoreType.DMA((7,)),
            ],
        )
        biases = [piece] + [rotate(piece, r) for r in range(1, n_mp)]
        order = [r for r in range(n_mp) if r != n_mp // 2] + [n_mp // 2]
        ffn_biases = [biases[r] for r in order]
        att_line = jnp.stack([g[:rows] for g in biases[1:]])
        by_x, by_y = within & 3, ((within >> 1) & 2) | (within & 1)
        piece = jnp.concatenate(
            [
                slot(down_weight, by_x, part),
                slot(up_weight, within, rows),
                slot(down_weight, 4 + by_y, part),
            ]
        )
        piece, att_line = tie(piece, att_line)
        ffn_line = [rotate(piece, r) for r in order[1:]]

        def plane_mixed(line):
            left = jnp.stack([g[: part + rows] for g in line])
            right = jnp.stack([g[part:] for g in line])
            corner = swap(jnp.stack([g[part : part + rows] for g in line]), 6)
            return left, swap(left, 2), swap(right, 4), corner, right[:, rows:]

        def slots_mixed(pieces):
            left, from_x, from_y, corner, own = pieces
            return jnp.stack([left, from_x, from_y, jnp.concatenate([corner, own], axis=1)])

        att_four = [att_line] + [swap(att_line, b) for b in (2, 4, 6)]
        att_four, ffn_line[:-1] = tie(att_four, ffn_line[:-1])
        att_four = jnp.stack(att_four)
        att_other = swap(att_four, 1)
        ffn_four = plane_mixed(ffn_line[:-1])
        tok_low = shape((length, width), bf16)
        tok_wide = shape((length, width), f32)
        queries, keys, values, contexts, normal, inverse, weights, wo = call(
            att_forward,
            "att_forward",
            [tok_low] * 4
            + [
                tok_wide,
                shape((length, 1), f32),
                shape((3, n_mp * w, width), bf16),
                shape((n_mp * w, width), bf16),
            ],
            [
                index,
                tokens,
                owns,
                att_four,
                att_other,
                *biases,
                output_bias,
                seg_row,
                seg_col,
            ],
            "s" + "v" * 11,
            [
                pltpu.VMEM((blocks, 3 * PASSAGE, PASSAGE), f32),
                pltpu.VMEM((1, length, length), bf16),
                pltpu.VMEM((8, width), f32),
                pltpu.VMEM((length, width), f32),
            ],
        )
        normal, ffn_four, ffn_line[-1] = tie(normal, ffn_four, ffn_line[-1])
        ffn_four = slots_mixed(ffn_four)
        ffn_other = swap(ffn_four, 1)
        last_four = plane_mixed(ffn_line[-1:])
        inner = (n_mp - 1) * units
        hidden_low = shape((length, inner), bf16)
        activated, slope, low_t, mixed, up, down = call(
            ffn_first,
            "ffn_first",
            [
                hidden_low,
                hidden_low,
                shape((width, length), bf16),
                tok_wide,
                shape((width, inner), bf16),
                shape((inner, width), bf16),
            ],
            [
                index,
                normal,
                first_gain,
                first_shift,
                down_bias,
                *ffn_biases[:-1],
                up_weight,
                down_weight,
                ffn_four,
                ffn_other,
            ],
            "s" + "v" * 11,
            [
                pltpu.VMEM((length, units), f32),
                pltpu.VMEM((n_mp, 8, units), f32),
                pltpu.VMEM((length, width), bf16),
            ],
        )
        activated, last_four = tie(activated, last_four)
        last_four = slots_mixed(last_four)
        last_other = swap(last_four, 1)
        pieces = shape((half, n_mp, part, width), bf16)
        (
            output,
            grad_mixed,
            grad_two,
            sums_two,
            slope_last,
            up_last,
            down_last,
            keep_down,
            send_down,
        ) = call(
            ffn_last,
            "ffn_last",
            [
                tok_low,
                tok_low,
                tok_wide,
                shape((8, width), f32),
                shape((length, units), bf16),
                shape((width, units), bf16),
                shape((units, width), bf16),
                pieces,
                pieces,
            ],
            [
                index,
                normal,
                cotangent,
                first_gain,
                first_shift,
                second_gain,
                second_shift,
                ffn_biases[-1],
                activated,
                mixed,
                last_four,
                last_other,
            ],
            "s" + "v" * 11,
            [pltpu.VMEM((length, units), bf16), pltpu.VMEM((length, width), f32)],
        )
        got_down = swap(send_down, 1)
        hidden, low_sums = call(
            ffn_slopes,
            "ffn_slopes",
            [shape((length, n_mp * units), bf16), shape((8, units), f32)],
            [grad_mixed, slope, slope_last, down, down_last],
            "v" * 5,
        )
        hidden, got_down = tie(hidden, got_down)
        leave_x, leave_y = add(keep_down[1], got_down[1]), add(keep_down[3], got_down[3])
        stay_x, stay_y = add(keep_down[0], got_down[0]), add(keep_down[2], got_down[2])
        hidden, leave_x, leave_y = tie(hidden, leave_x, leave_y)
        come_x, come_y = swap(leave_x, 2), swap(leave_y, 4)
        pieces = shape((half, n_mp, rows, units), bf16)
        keep_up, send_up = call(
            ffn_grads, "ffn_grads", [pieces, pieces], [index, hidden, low_t], "svv"
        )
        hidden, keep_up, send_up = tie(hidden, keep_up, send_up)
        got_up = swap(send_up, 1)
        grad_one, grad_attended, sums_one = call(
            ffn_norm,
            "ffn_norm",
            [tok_wide, tok_low, shape((8, width), f32)],
            [hidden, grad_two, normal, inverse, first_gain, up, up_last],
            "v" * 7,
            [pltpu.VMEM((length, width), f32)],
        )
        grad_attended, sums_one, got_up = tie(grad_attended, sums_one, got_up)
        cut = units // 2
        left, right = slice(0, cut), slice(cut, None)

        def plane_halves(keep, got):
            leaves = add(keep[1::2, ..., left], got[1::2, ..., left])
            leaves_r = add(keep[2:, ..., right], got[2:, ..., right])
            stays = add(keep[0::2, ..., left], got[0::2, ..., left])
            stays_r = add(keep[:2, ..., right], got[:2, ..., right])
            return leaves, leaves_r, stays, stays_r

        leave_l, leave_r, stay_l, stay_r = plane_halves(keep_up, got_up)
        grad_attended, leave_l, leave_r = tie(grad_attended, leave_l, leave_r)
        come_l, come_r = swap(leave_l, 2), swap(leave_r, 4)
        halves = n_mp // 2
        across = halves * w
        pieces = shape((half, halves, rows + EXTRA, width), bf16)
        places = [order.index(r) for r in range(n_mp)]

        def attention(which, grad_attended):
            return call(
                functools.partial(att_backward, which, places),
                "att_backward",
                [shape((length, across), bf16)] * 3 + [pieces] * 2,
                [
                    index,
                    queries,
                    keys,
                    values,
                    contexts,
                    grad_attended,
                    tokens,
                    wo,
                    seg_row,
                    seg_col,
                    low_sums,
                    sums_one,
                    sums_two,
                ],
                "s" + "v" * 12,
                [
                    pltpu.VMEM((length, across), bf16),
                    pltpu.VMEM((blocks, 3 * PASSAGE, PASSAGE), f32),
                    pltpu.VMEM((1, length, length), bf16),
                    pltpu.VMEM((1, length, length), bf16),
                ],
            )

        q0, k0, v0, keep_0, send_0 = attention(0, grad_attended)
        come_x, come_y, q0, k0, v0, keep_0, send_0 = tie(
            come_x, come_y, q0, k0, v0, keep_0, send_0
        )
        got_0 = swap(send_0, 1)
        parts_x, parts_y = add(stay_x, come_x), add(stay_y, come_y)
        grad_attended, parts_x, got_0 = tie(grad_attended, parts_x, got_0)
        line_x = line_moves(parts_x, order)
        q1, k1, v1, keep_1, send_1 = attention(1, grad_attended)
        q1, k1, v1, keep_1, send_1, come_l, come_r, line_x[1:], parts_y = tie(
            q1, k1, v1, keep_1, send_1, come_l, come_r, line_x[1:], parts_y
        )
        got_1 = swap(send_1, 1)
        line_y = line_moves(parts_y, order)
        now_l, now_r = add(stay_l, come_l), add(stay_r, come_r)
        come_l, come_r = swap(now_l[1], 4), swap(now_r[1], 2)
        keep_att = jnp.concatenate([keep_0, keep_1], axis=1)
        got_att = jnp.concatenate([got_0, got_1], axis=1)
        leave_left, leave_right, stay_left, stay_right = plane_halves(keep_att, got_att)
        come_l, come_r, leave_left, leave_right = tie(come_l, come_r, leave_left, leave_right)
        come_left, come_right = swap(leave_left, 2), swap(leave_right, 4)
        up_parts = jnp.concatenate([add(now_l[0], come_l), add(now_r[0], come_r)], axis=-1)
        up_parts, line_y = tie(up_parts, line_y)
        up_line = line_moves(up_parts, order)
        down_x, down_y = line_total(line_x), line_total(line_y)
        come_left, come_right, up_line[1:3], down_x, down_y = tie(
            come_left, come_right, up_line[1:3], down_x, down_y
        )
        left_now, right_now = add(stay_left, come_left), add(stay_right, come_right)
        come_left, come_right = swap(left_now[1], 4), swap(right_now[1], 2)
        come_x, come_y = swap(down_x, 4), swap(down_y, 2)
        up_line[3:], come_left, come_right, come_x, come_y = tie(
            up_line[3:], come_left, come_right, come_x, come_y
        )
        att_parts = jnp.concatenate(
            [add(left_now[0], come_left), add(right_now[0], come_right)], axis=-1
        )
        att_line = line_moves(att_parts, range(n_mp))
        down_x, down_y = add(down_x, come_x), add(down_y, come_y)
        come_x, come_y = swap(down_x, 2), swap(down_y, 4)
        up_total = line_total(up_line)
        (grad_tokens,) = call(
            input_backward,
            "input_backward",
            [tok_low],
            [q0, k0, v0, q1, k1, v1, grad_one, weights],
            "v" * 8,
        )
        att_line[1], come_x, come_y, up_total, grad_tokens = tie(
            att_line[1], come_x, come_y, up_total, grad_tokens
        )
        up_four = plane_swap(up_total)
        down_four = [down_x, come_x, down_y, come_y]
        att_line[2:], up_four = tie(att_line[2:], up_four)
        att_four = plane_swap(line_total(att_line))
        down_four, up_four = jnp.stack(down_four), jnp.stack(up_four)
        (grad_down,) = call(
            functools.partial(finish_ffn, places_by_axis),
            "finish_down",
            [shape((units, width), f32)],
            [index, down_four, swap(down_four, 1)],
            "svv",
        )
        (grad_up,) = call(
            functools.partial(finish_ffn, eighths),
            "finish_up",
            [shape((width, units), f32)],
            [index, up_four, swap(up_four, 1)],
            "svv",
        )
        att_four, grad_down, grad_up = tie(att_four, grad_down, grad_up)
        att_four = jnp.stack(att_four)
        att_other = swap(att_four, 1)
        grad_query, grad_key, grad_value, grad_output, sums = call(
            finish_att,
            "finish_att",
            [shape((w, width), f32)] * 4 + [shape((GROUP * EXTRA, width), f32)],
            [index, att_four, att_other],
            "svv",
            [pltpu.VMEM((4 * w, width), f32)],
        )
        return (
            output,
            grad_tokens,
            grad_query.T,
            sums[(GROUP - 1) * EXTRA, :w],
            grad_key.T,
            grad_value.T,
            sums[(GROUP - 1) * EXTRA, w : 2 * w],
            grad_output,
            sums[EXTRA],
            sums[2 * EXTRA],
            sums[3 * EXTRA],
            grad_up,
            sums[0],
            grad_down,
            sums[4 * EXTRA],
            sums[5 * EXTRA],
            sums[6 * EXTRA],
        )

    everywhere, rows, columns, units = P(), P(("dp", "mp"), None), P(None, "mp"), P("mp")
    in_specs = (
        rows,
        P("dp", None),
        columns,
        units,
        columns,
        columns,
        units,
        P("mp", None),
        everywhere,
        everywhere,
        everywhere,
        columns,
        units,
        P("mp", None),
        everywhere,
        everywhere,
        everywhere,
        rows,
    )
    out_specs = (
        rows,
        rows,
        columns,
        units,
        columns,
        columns,
        units,
        P("mp", None),
        everywhere,
        everywhere,
        everywhere,
        columns,
        units,
        P("mp", None),
        everywhere,
        everywhere,
        everywhere,
    )
    return jax.shard_map(shards, mesh=mesh, in_specs=in_specs, out_specs=out_specs, check_vma=False)
```

```python
import functools
import math

import jax
import jax.numpy as jnp
from jax import lax
from jax.experimental import pallas as pl
from jax.experimental.pallas import tpu as pltpu
from jax.sharding import PartitionSpec as P

HEAD_DIM = 64
PASSAGE = 128
GROUP = 8
EXTRA = 8
LANES = 128
CHUNK = 128
SCOPED = {
    "first_piece": 60,
    "att_forward": 7,
    "ffn_first": 5,
    "ffn_last": 10,
    "ffn_slopes": 8,
    "ffn_grads": 5,
    "ffn_norm": 7,
    "att_backward": 11,
    "input_backward": 4,
    "finish_down": 4,
    "finish_up": 4,
    "finish_att": 6,
}
epsilon = 1e-05
bf16 = jnp.bfloat16
f32 = jnp.float32


def nn(left, right):
    return lax.dot_general(left, right, (((1,), (0,)), ((), ())), preferred_element_type=f32)


def nt(left, right):
    return lax.dot_general(left, right, (((1,), (1,)), ((), ())), preferred_element_type=f32)


def tn(left, right):
    return lax.dot_general(left, right, (((0,), (0,)), ((), ())), preferred_element_type=f32)


def call(body, name, outs, args, spaces, scratch=(), out_spaces=None):
    def spec(kind):
        if kind == "s":
            return pl.BlockSpec(memory_space=pltpu.SMEM)
        if kind == "h":
            return pl.BlockSpec(memory_space=pltpu.HBM)
        return pl.BlockSpec(memory_space=pltpu.VMEM)

    out_spaces = out_spaces or "v" * len(outs)
    def size(array):
        return math.prod(array.shape) * jnp.dtype(array.dtype).itemsize

    every = list(zip(args, spaces)) + list(zip(outs, out_spaces))
    moved = sum(size(array) for array, kind in every)
    return pl.pallas_call(
        body,
        name=name,
        out_shape=tuple(outs),
        in_specs=[spec(k) for k in spaces],
        out_specs=tuple(spec(k) for k in out_spaces),
        scratch_shapes=list(scratch),
        compiler_params=pltpu.CompilerParams(vmem_limit_bytes=SCOPED[name] << 20),
        cost_estimate=pl.CostEstimate(flops=0, bytes_accessed=moved // 64, transcendentals=0),
    )(*args)


def vector(ref):
    return ref[...].astype(f32).reshape(1, ref.shape[0])


def places_by_axis(index):
    x, y = index & 3, ((index >> 1) & 2) | (index & 1)
    return [x, x ^ 1, x ^ 2, x ^ 3, 4 + y, 4 + (y ^ 1), 4 + (y ^ 2), 4 + (y ^ 3)]


def eighths(index):
    return [index ^ s for s in range(GROUP)]


def places_gathered(index):
    places = places_by_axis(index)
    return places[:4] + places[6:] + places[4:6]


def place_slots(pieces, others, r, down_rows, rows, places, dest, base, columns):
    upper, lower = slice(0, rows), slice(rows, 2 * rows)
    sources = ((0, upper), (1, upper), (2, lower), (4, lower))
    if not down_rows:
        sources = ((0, lower), (1, lower), (2, upper), (3, upper))
    for s in range(GROUP):
        piece, part = sources[s // 2]
        at = pl.multiple_of(base + places[s] * rows, rows)
        dest[pl.ds(at, rows), columns] = (others if s % 2 else pieces)[piece][r, part]


def put_slots(index, r, rows, low, keep, send, by_axis=False):
    size = rows[0].shape[0]
    x, y = index & 3, ((index >> 1) & 2) | (index & 1)
    for odd in range(2):

        @pl.when((index & 1) == odd)
        def _():
            for d in range(GROUP):
                dest = send if (d ^ odd) & 1 else keep
                spot = (index ^ d) >> 1
                if by_axis:
                    spot = (x ^ d) >> 1 if d < 4 else 2 + ((y ^ (d - 4)) >> 1)
                dest[spot, r, low : low + size] = rows[d]


def normalize(total):
    centred = total - jnp.mean(total, axis=-1, keepdims=True)
    inverse = lax.rsqrt(jnp.mean(centred * centred, axis=-1, keepdims=True) + epsilon)
    return centred * inverse, inverse


def norm_backward(grad_out, normal, inverse, norm_gain):
    scaled = grad_out * norm_gain
    return inverse * (
        scaled
        - jnp.mean(scaled, axis=-1, keepdims=True)
        - normal * jnp.mean(scaled * normal, axis=-1, keepdims=True)
    )


def column_sum(array):
    return jnp.sum(array, axis=0, keepdims=True)


def folded(array):
    return jnp.sum(array.reshape(-1, 8, array.shape[1]), axis=0)


def by_rows(length, body, sums, width):
    def step(i, totals):
        found = body(pl.ds(pl.multiple_of(i * CHUNK, CHUNK), CHUNK))
        return tuple(t + folded(f) for t, f in zip(totals, found))

    zeros = tuple(jnp.zeros((8, width), f32) for _ in range(sums))
    totals = lax.fori_loop(0, length // CHUNK, step, zeros, unroll=1)
    return tuple(column_sum(t) for t in totals)


def band(block, length):
    return max(0, (block - 1) * PASSAGE), min(length, (block + 2) * PASSAGE)


def clear_outside(array, length):
    for b in range(length // PASSAGE):
        lo, hi = band(b, length)
        block = slice(b * PASSAGE, (b + 1) * PASSAGE)
        for low, high in ((0, lo), (hi, length)):
            if high > low:
                shape = (array.shape[0], high - low, PASSAGE)
                array[:, low:high, block] = jnp.zeros(shape, array.dtype)


def fill_bias(bias, seg_row, seg_col, length):
    for b in range(length // PASSAGE):
        lo, hi = band(b, length)
        same = seg_col[lo:hi, :] == seg_row[:, b * PASSAGE : (b + 1) * PASSAGE]
        bias[b, : hi - lo, :] = jnp.where(same, 0.0, -1e30)


def softmax_columns(scores):
    expo = jnp.exp(scores - jnp.max(scores, axis=0, keepdims=True))
    return expo * (1.0 / jnp.sum(expo, axis=0, keepdims=True))


def first_piece(
    index_ref, own_q, own_k, own_v, own_o, query_bias, value_bias, up_bias, out, owns,
    query_row, value_row, up_row, sems,
):
    w = own_q.shape[0]
    rows = w // 2
    small = [
        pltpu.make_async_copy(own, owns.at[pl.ds(m * w, w)], sems.at[3 + m])
        for m, own in enumerate((own_q, own_k, own_v, own_o))
    ]
    small += [
        pltpu.make_async_copy(query_bias, query_row, sems.at[0]),
        pltpu.make_async_copy(value_bias, value_row, sems.at[1]),
        pltpu.make_async_copy(up_bias, up_row, sems.at[2]),
    ]
    for copy in small:
        copy.start()
    for copy in small:
        copy.wait()
    out[:rows, :] = owns[pl.ds(pl.multiple_of(index_ref[0] * rows, rows), rows), :]
    out[rows:, :] = jnp.zeros((EXTRA, out.shape[1]), bf16)
    out[rows : rows + 1, :w] = vector(query_row).astype(bf16)
    out[rows : rows + 1, w : 2 * w] = vector(value_row).astype(bf16)
    out[rows + 1 : rows + 2, :] = vector(up_row).astype(bf16)


def att_forward(
    index_ref, tokens, owns, four, other, bias_0, bias_1, bias_2, bias_3,
    output_bias, seg_row, seg_col,
    queries, keys, values, contexts, normal, inverse, weights, wo,
    bias, probs_t, row, attended,
):
    length, width = tokens.shape
    w = owns.shape[0] // 4
    quarters = width // w
    rows = four.shape[2]
    index = index_ref[0]
    for m in range(3):
        weights[m, :w, :] = owns[m * w : (m + 1) * w, :]
    wo[:w, :] = owns[3 * w :, :]
    for r in range(1, quarters):
        for s in range(GROUP):
            owner = index ^ s
            at = pl.multiple_of(r * w + (owner & 1) * rows, rows)
            source = other if s % 2 else four

            @pl.when(owner < 6)
            def _():
                weights[owner >> 1, pl.ds(at, rows), :] = source[s // 2, r - 1]

            @pl.when(owner >= 6)
            def _():
                wo[pl.ds(at, rows), :] = source[s // 2, r - 1]

    fill_bias(bias, seg_row, seg_col, length)
    clear_outside(probs_t, length)
    for r, source in enumerate((bias_0, bias_1, bias_2, bias_3)):
        for i in range(2):
            piece = source[rows : rows + 1, i * w : (i + 1) * w].astype(f32)
            row[i : i + 1, r * w : (r + 1) * w] = piece
    low = (nt(tokens[...], weights[0]) + row[0:1, :]).astype(bf16)
    queries[...] = (low.astype(f32) * (HEAD_DIM**-0.5)).astype(bf16)
    keys[...] = nt(tokens[...], weights[1]).astype(bf16)
    values[...] = (nt(tokens[...], weights[2]) + row[1:2, :]).astype(bf16)
    first = lax.broadcasted_iota(jnp.int32, (PASSAGE, LANES), 1) < HEAD_DIM
    first_all = lax.broadcasted_iota(jnp.int32, (length, LANES), 1) < HEAD_DIM

    def pair(i, carry):
        at = pl.ds(pl.multiple_of(i * LANES, LANES), LANES)
        for half, mine in enumerate((first, jnp.logical_not(first))):
            for b in range(length // PASSAGE):
                lo, hi = band(b, length)
                block = slice(b * PASSAGE, (b + 1) * PASSAGE)
                q = queries[block, at]
                masked = jnp.where(mine, q, jnp.zeros_like(q))
                scores = nt(keys[lo:hi, at], masked) + bias[b, : hi - lo, :]
                probs_t[half, lo:hi, block] = softmax_columns(scores).astype(bf16)
        found = [tn(probs_t[half], values[:, at]) for half in range(2)]
        contexts[:, at] = jnp.where(first_all, *found).astype(bf16)
        return carry

    lax.fori_loop(0, width // LANES, pair, 0)
    attended[...] = nn(contexts[...], wo[...]) + vector(output_bias)

    def norm(rows):
        n, r = normalize(tokens[rows, :].astype(f32) + attended[rows, :])
        normal[rows, :] = n
        inverse[rows, :] = r
        return ()

    by_rows(length, norm, 0, width)


def gelu_rows(hidden, activated, slope, columns):
    def step(i, carry):
        rows = pl.ds(pl.multiple_of(i * CHUNK, CHUNK), CHUNK)
        value = hidden[rows, :]
        cumulative = 0.5 * (1.0 + lax.erf(value * 0.7071067811865476))
        density = jnp.exp(-0.5 * value * value) * 0.3989422804014327
        activated[rows, columns] = (value * cumulative).astype(bf16)
        slope[rows, columns] = (cumulative + value * density).astype(bf16)
        return carry

    lax.fori_loop(0, hidden.shape[0] // CHUNK, step, 0)


def each(count, body):
    def step(r, carry):
        body(r)
        return carry

    lax.fori_loop(0, count, step, 0)


def columns_of(r, size):
    return pl.ds(pl.multiple_of(r * size, LANES), size)


def ffn_first(
    index_ref, normal, gain, shift, down_bias, bias_0, bias_1, bias_2, own_up, own_down,
    left, from_x, from_y, corner, right, left_o, from_x_o, from_y_o, corner_o, right_o,
    activated, slope, low_t, mixed, up, down,
    hidden, lines, low_rows,
):
    units = own_up.shape[1]
    four = (left, from_x, from_y, corner, right)
    other = (left_o, from_x_o, from_y_o, corner_o, right_o)
    rows = corner.shape[1]
    quarters = corner.shape[0] + 1
    biases = (bias_0, bias_1, bias_2)
    up_places, down_places = eighths(index_ref[0]), places_gathered(index_ref[0])
    normed = normal[...] * vector(gain) + vector(shift)
    low = normed.astype(bf16)
    low_t[...] = low.T
    low_rows[...] = low
    mixed[...] = normed + vector(down_bias)
    for r in range(quarters):
        mine = slice(r * units, (r + 1) * units)
        if r == 0:
            up[:, mine] = own_up[...]
            down[mine, :] = own_down[...]
        else:
            place_slots(four, other, r - 1, False, rows, up_places, up, 0, mine)
            place_slots(four, other, r - 1, True, rows, down_places, down, r * units, slice(None))
        at = biases[r].shape[0] - EXTRA + 1
        lines[r, :, :] = jnp.broadcast_to(biases[r][at : at + 1, :].astype(f32), lines.shape[1:])

    def quarter(r):
        mine = columns_of(r, units)
        hidden[...] = nn(low_rows[...], up[:, mine]) + lines[r, 0:1, :]
        gelu_rows(hidden, activated, slope, mine)

    each(quarters, quarter)
    mixed[...] += nn(activated[...], down[...])


def ffn_last(
    index_ref, normal, cotangent, gain, shift, second_gain, second_shift, bias, activated, mixed,
    left, from_x, from_y, corner, right, left_o, from_x_o, from_y_o, corner_o, right_o,
    output, grad_mixed, grad_two, sums, slope, up, down, keep, send,
    own, total,
):
    length, width = normal.shape
    units = up.shape[1]
    four = (left, from_x, from_y, corner, right)
    other = (left_o, from_x_o, from_y_o, corner_o, right_o)
    rows = corner.shape[1]
    index = index_ref[0]
    place_slots(four, other, 0, False, rows, eighths(index), up, 0, slice(None))
    place_slots(four, other, 0, True, rows, places_gathered(index), down, 0, slice(None))
    low = (normal[...] * vector(gain) + vector(shift)).astype(bf16)
    at = bias.shape[0] - EXTRA + 1
    total[...] = nn(low, up[...]) + bias[at : at + 1, :].astype(f32)
    gelu_rows(total, own, slope, slice(None))
    total[...] = mixed[...] + nn(own[...], down[...])
    out_gain, out_shift = vector(second_gain), vector(second_shift)

    def norm(rows):
        n, inverse = normalize(total[rows, :])
        output[rows, :] = (n * out_gain + out_shift).astype(bf16)
        grad_out = cotangent[rows, :].astype(f32)
        two = norm_backward(grad_out, n, inverse, out_gain)
        grad_two[rows, :] = two
        low = two.astype(bf16)
        grad_mixed[rows, :] = low
        return low.astype(f32), grad_out * n, grad_out

    sums[...] = jnp.zeros_like(sums)
    for i, found in enumerate(by_rows(length, norm, 3, width)):
        sums[i : i + 1, :] = found

    def put(r, left):
        grad = tn(left, grad_mixed[...]).astype(bf16)
        put_slots(index, r, grad.reshape(GROUP, -1, width), 0, keep, send, True)

    each(keep.shape[1] - 1, lambda r: put(r, activated[:, columns_of(r, units)]))
    put(keep.shape[1] - 1, own[...])


def ffn_slopes(grad_mixed, slope, slope_last, down, down_last, hidden, sums):
    units = down_last.shape[0]
    sums[...] = jnp.zeros_like(sums)

    def quarter(r, weight, factor):
        low = (nt(grad_mixed[...], weight) * factor.astype(f32)).astype(bf16)
        hidden[:, columns_of(r, units)] = low
        sums[pl.ds(r, 1), :] = column_sum(low.astype(f32))

    def inner(r):
        mine = columns_of(r, units)
        quarter(r, down[mine, :], slope[:, mine])

    each(down.shape[0] // units, inner)
    quarter(down.shape[0] // units, down_last[...], slope_last[...])


def ffn_grads(index_ref, hidden, low_t, keep, send):
    units = keep.shape[3]

    def quarter(r):
        grad = nn(low_t[...], hidden[:, columns_of(r, units)]).astype(bf16)
        put_slots(index_ref[0], r, grad.reshape(GROUP, -1, units), 0, keep, send)

    each(keep.shape[1], quarter)


def ffn_norm(
    hidden, grad_two, normal, inverse, gain_ref, up, up_last,
    grad_one, grad_attended, sums,
    total,
):
    length, width = normal.shape
    inner = up.shape[1]
    total[...] = nt(hidden[:, :inner], up[...]) + grad_two[...]
    total[...] += nt(hidden[:, inner:], up_last[...])
    gain = vector(gain_ref)

    def norm(at):
        grad_normed = total[at, :]
        n = normal[at, :]
        one = norm_backward(grad_normed, n, inverse[at, :], gain)
        grad_one[at, :] = one
        low = one.astype(bf16)
        grad_attended[at, :] = low
        return low.astype(f32), grad_normed * n, grad_normed

    sums[...] = jnp.zeros_like(sums)
    for i, found in enumerate(by_rows(length, norm, 3, width)):
        sums[i : i + 1, :] = found


def att_backward(
    part, places, index_ref, queries, keys, values, contexts, grad_attended, tokens, wo,
    seg_row, seg_col, unit_sums, sums_one, sums_two,
    grad_queries, grad_keys, grad_values, keep, send,
    grad_contexts, bias, probs_t, scores_t,
):
    length, width = tokens.shape
    quarters, rows = keep.shape[1], keep.shape[2] - EXTRA
    w = 2 * rows
    across = quarters * w
    index = index_ref[0]
    scale = HEAD_DIM**-0.5
    fill_bias(bias, seg_row, seg_col, length)
    clear_outside(probs_t, length)
    clear_outside(scores_t, length)
    low = part * across
    grad_contexts[...] = nt(grad_attended[...], wo[low : low + across, :]).astype(bf16)
    lane = lax.broadcasted_iota(jnp.int32, (PASSAGE, LANES), 1) // HEAD_DIM
    lane_all = lax.broadcasted_iota(jnp.int32, (length, LANES), 1) // HEAD_DIM

    def head(i, carry):
        half = i & 1
        here = pl.ds(pl.multiple_of((i >> 1) * LANES, LANES), LANES)
        at = pl.ds(pl.multiple_of(low + (i >> 1) * LANES, LANES), LANES)
        mine = lane == half
        for b in range(length // PASSAGE):
            lo, hi = band(b, length)
            block = slice(b * PASSAGE, (b + 1) * PASSAGE)
            q = queries[block, at]
            g = grad_contexts[block, here]
            zero = jnp.zeros_like(q)
            scores = nt(keys[lo:hi, at], jnp.where(mine, q, zero)) + bias[b, : hi - lo, :]
            probs = softmax_columns(scores)
            grad_probs = nt(values[lo:hi, at], jnp.where(mine, g, zero))
            inner = jnp.sum(grad_probs * probs, axis=0, keepdims=True)
            probs_t[0, lo:hi, block] = probs.astype(bf16)
            scores_t[0, lo:hi, block] = (probs * (grad_probs - inner)).astype(bf16)
        mine = lane_all == half
        for out, found in (
            (grad_queries, tn(scores_t[0], keys[:, at]) * scale),
            (grad_keys, nn(scores_t[0], queries[:, at])),
            (grad_values, nn(probs_t[0], grad_contexts[:, here])),
        ):
            out[:, here] = jnp.where(mine, found.astype(bf16), out[:, here])
        return carry

    lax.fori_loop(0, across // HEAD_DIM, head, 0)
    grads = (
        lambda: tn(grad_queries[...], tokens[...]),
        lambda: tn(grad_keys[...], tokens[...]),
        lambda: tn(grad_values[...], tokens[...]),
        lambda: tn(contexts[:, low : low + across], grad_attended[...]),
    )
    grads = [make().astype(bf16).reshape(quarters, 2, rows, width) for make in grads]
    query_sum = column_sum(grad_queries[...].astype(f32))
    value_sum = column_sum(grad_values[...].astype(f32))
    for r in range(quarters):
        put_slots(index, r, [grads[d // 2][r, d % 2] for d in range(GROUP)], 0, keep, send)
        cols = slice(r * w, (r + 1) * w)
        last = jnp.concatenate(
            [query_sum[:, cols], value_sum[:, cols], jnp.zeros((1, width - 2 * w), f32)], axis=1
        )
        at = places[part * quarters + r]
        lines = [unit_sums[at : at + 1, :]]
        lines += [sums[i : i + 1, :] for sums in (sums_one, sums_two) for i in range(3)]
        lines = [jnp.broadcast_to(line, (EXTRA, width)).astype(bf16) for line in lines + [last]]
        put_slots(index, r, lines, rows, keep, send)


def input_backward(q0, k0, v0, q1, k1, v1, grad_one, weights, out):
    half = q0.shape[1]
    total = grad_one[...]
    for m, (left, right) in enumerate(((q0, q1), (k0, k1), (v0, v1))):
        total += nn(left[...], weights[m, :half]) + nn(right[...], weights[m, half:])
    out[...] = total.astype(bf16)


def finish_ffn(places_of, index_ref, four, other, out):
    rows = four.shape[1]
    for s, place in enumerate(places_of(index_ref[0])):
        at = pl.multiple_of(place * rows, rows)
        out[pl.ds(at, rows), :] = (other if s % 2 else four)[s // 2].astype(f32)


def finish_att(index_ref, four, other, gq, gk, gv, go, sums, whole):
    rows = four.shape[1] - EXTRA
    w = 2 * rows
    for s in range(GROUP):
        slot = (other if s % 2 else four)[s // 2].astype(f32)
        owner = index_ref[0] ^ s
        whole[pl.ds(pl.multiple_of(owner * rows, rows), rows), :] = slot[:rows]
        sums[pl.ds(pl.multiple_of(owner * EXTRA, EXTRA), EXTRA), :] = slot[rows:]
    for m, out in enumerate((gq, gk, gv, go)):
        out[...] = whole[m * w : (m + 1) * w, :]


def solution(mesh):
    n_dp, n_mp = mesh.shape["dp"], mesh.shape["mp"]
    if n_dp % GROUP or n_mp % 2:
        raise ValueError("mesh")

    def rotate(array, step):
        return lax.ppermute(array, "mp", [(i, (i + step) % n_mp) for i in range(n_mp)])

    def swap(array, bits):
        return lax.ppermute(array, "dp", [(i, i ^ bits) for i in range(n_dp)])

    def plane_swap(array):
        return [array, swap(array, 2), swap(array, 4), swap(array, 6)]

    def add(left, right):
        return (left.astype(f32) + right.astype(f32)).astype(bf16)

    def tie(*arrays):
        return lax.optimization_barrier(arrays)

    def after(array, *others):
        return tie(array, *others)[0]

    def first_axis(bits):
        go = slice(1, None, 2) if bits == 2 else slice(2, None)
        stay = slice(0, None, 2) if bits == 2 else slice(0, 2)
        return go, stay

    def plane_first(keep, got, bits):
        go, stay = first_axis(bits)
        return add(keep[go], got[go]), add(keep[stay], got[stay])

    def line_moves(parts, order):
        found = {r: rotate(parts[i], -r) if r else parts[i] for i, r in enumerate(order)}
        return [found[r] for r in range(n_mp)]

    def line_total(moved):
        moved = [array.astype(f32) for array in moved]
        total = sum(moved[0::2][1:], moved[0]) + sum(moved[1::2][1:], moved[1])
        if n_dp > GROUP:
            groups = [[i + GROUP * k for k in range(n_dp // GROUP)] for i in range(GROUP)]
            total = lax.psum(total, "dp", axis_index_groups=groups)
        return total.astype(bf16)

    def shards(
        tokens,
        segment_ids,
        query_weight,
        query_bias,
        key_weight,
        value_weight,
        value_bias,
        output_weight,
        output_bias,
        first_gain,
        first_shift,
        up_weight,
        up_bias,
        down_weight,
        down_bias,
        second_gain,
        second_shift,
        cotangent,
    ):
        length, width = tokens.shape
        w = query_weight.shape[1]
        units = up_weight.shape[1]
        rows = width // GROUP
        blocks = length // PASSAGE
        half, part = GROUP // 2, units // GROUP
        shape = jax.ShapeDtypeStruct
        place = lax.axis_index("mp")
        within = lax.axis_index("dp") % GROUP
        index = within.astype(jnp.int32).reshape(1)
        seg_row = lax.dynamic_slice_in_dim(segment_ids, place, 1, 0)
        seg_col = seg_row.reshape(length, 1)

        def slot(array, at, size):
            return lax.dynamic_slice_in_dim(array, at * size, size, 0)

        owns = [query_weight.T, key_weight.T, value_weight.T, output_weight]
        piece, owns = call(
            first_piece,
            "first_piece",
            [shape((rows + EXTRA, width), bf16), shape((4 * w, width), bf16)],
            [index, *owns, query_bias, value_bias, up_bias],
            "s" + "h" * 7,
            [
                pltpu.VMEM((w,), bf16),
                pltpu.VMEM((w,), bf16),
                pltpu.VMEM((units,), bf16),
                pltpu.SemaphoreType.DMA((7,)),
            ],
        )
        biases = [piece] + [rotate(piece, r) for r in range(1, n_mp)]
        order = [r for r in range(n_mp) if r != n_mp // 2] + [n_mp // 2]
        ffn_biases = [biases[r] for r in order]
        att_line = jnp.stack([g[:rows] for g in biases[1:]])
        by_x, by_y = within & 3, ((within >> 1) & 2) | (within & 1)
        piece = jnp.concatenate(
            [
                slot(down_weight, by_x, part),
                slot(up_weight, within, rows),
                slot(down_weight, 4 + by_y, part),
            ]
        )
        piece, att_line = tie(piece, att_line)
        ffn_line = [rotate(piece, r) for r in order[1:]]

        def plane_mixed(line):
            left = jnp.stack([g[: part + rows] for g in line])
            right = jnp.stack([g[part:] for g in line])
            corner = swap(jnp.stack([g[part : part + rows] for g in line]), 6)
            return left, swap(left, 2), swap(right, 4), corner, right

        att_four = [att_line] + [swap(att_line, b) for b in (2, 4, 6)]
        att_four, ffn_line[:-1] = tie(att_four, ffn_line[:-1])
        att_four = jnp.stack(att_four)
        att_other = swap(att_four, 1)
        ffn_four = plane_mixed(ffn_line[:-1])
        tok_low = shape((length, width), bf16)
        tok_wide = shape((length, width), f32)
        queries, keys, values, contexts, normal, inverse, weights, wo = call(
            att_forward,
            "att_forward",
            [tok_low] * 4
            + [
                tok_wide,
                shape((length, 1), f32),
                shape((3, n_mp * w, width), bf16),
                shape((n_mp * w, width), bf16),
            ],
            [
                index,
                tokens,
                owns,
                att_four,
                att_other,
                *biases,
                output_bias,
                seg_row,
                seg_col,
            ],
            "s" + "v" * 11,
            [
                pltpu.VMEM((blocks, 3 * PASSAGE, PASSAGE), f32),
                pltpu.VMEM((2, length, length), bf16),
                pltpu.VMEM((8, width), f32),
                pltpu.VMEM((length, width), f32),
            ],
        )
        normal, ffn_four, ffn_line[-1] = tie(normal, ffn_four, ffn_line[-1])
        ffn_other = [swap(array, 1) for array in ffn_four]
        last_four = plane_mixed(ffn_line[-1:])
        inner = (n_mp - 1) * units
        hidden_low = shape((length, inner), bf16)
        activated, slope, low_t, mixed, up, down = call(
            ffn_first,
            "ffn_first",
            [
                hidden_low,
                hidden_low,
                shape((width, length), bf16),
                tok_wide,
                shape((width, inner), bf16),
                shape((inner, width), bf16),
            ],
            [
                index,
                normal,
                first_gain,
                first_shift,
                down_bias,
                *ffn_biases[:-1],
                up_weight,
                down_weight,
                *ffn_four,
                *ffn_other,
            ],
            "s" + "v" * 19,
            [
                pltpu.VMEM((length, units), f32),
                pltpu.VMEM((n_mp, 8, units), f32),
                pltpu.VMEM((length, width), bf16),
            ],
        )
        activated, last_four = tie(activated, last_four)
        last_other = [swap(array, 1) for array in last_four]
        pieces = shape((half, n_mp, part, width), bf16)
        (
            output,
            grad_mixed,
            grad_two,
            sums_two,
            slope_last,
            up_last,
            down_last,
            keep_down,
            send_down,
        ) = call(
            ffn_last,
            "ffn_last",
            [
                tok_low,
                tok_low,
                tok_wide,
                shape((8, width), f32),
                shape((length, units), bf16),
                shape((width, units), bf16),
                shape((units, width), bf16),
                pieces,
                pieces,
            ],
            [
                index,
                normal,
                cotangent,
                first_gain,
                first_shift,
                second_gain,
                second_shift,
                ffn_biases[-1],
                activated,
                mixed,
                *last_four,
                *last_other,
            ],
            "s" + "v" * 19,
            [pltpu.VMEM((length, units), bf16), pltpu.VMEM((length, width), f32)],
        )
        got_down = swap(send_down, 1)
        hidden, low_sums = call(
            ffn_slopes,
            "ffn_slopes",
            [shape((length, n_mp * units), bf16), shape((8, units), f32)],
            [grad_mixed, slope, slope_last, down, down_last],
            "v" * 5,
        )
        hidden, got_down = tie(hidden, got_down)
        leave_x, leave_y = add(keep_down[1], got_down[1]), add(keep_down[3], got_down[3])
        stay_x, stay_y = add(keep_down[0], got_down[0]), add(keep_down[2], got_down[2])
        hidden, leave_x, leave_y = tie(hidden, leave_x, leave_y)
        come_x, come_y = swap(leave_x, 2), swap(leave_y, 4)
        pieces = shape((half, n_mp, rows, units), bf16)
        keep_up, send_up = call(
            ffn_grads, "ffn_grads", [pieces, pieces], [index, hidden, low_t], "svv"
        )
        hidden, keep_up, send_up = tie(hidden, keep_up, send_up)
        got_up = swap(send_up, 1)
        grad_one, grad_attended, sums_one = call(
            ffn_norm,
            "ffn_norm",
            [tok_wide, tok_low, shape((8, width), f32)],
            [hidden, grad_two, normal, inverse, first_gain, up, up_last],
            "v" * 7,
            [pltpu.VMEM((length, width), f32)],
        )
        grad_attended, sums_one, got_up = tie(grad_attended, sums_one, got_up)
        cut = units // 2
        left, right = slice(0, cut), slice(cut, None)

        def plane_halves(keep, got):
            leaves = add(keep[1::2, ..., left], got[1::2, ..., left])
            leaves_r = add(keep[2:, ..., right], got[2:, ..., right])
            stays = add(keep[0::2, ..., left], got[0::2, ..., left])
            stays_r = add(keep[:2, ..., right], got[:2, ..., right])
            return leaves, leaves_r, stays, stays_r

        leave_l, leave_r, stay_l, stay_r = plane_halves(keep_up, got_up)
        grad_attended, leave_l, leave_r = tie(grad_attended, leave_l, leave_r)
        come_l, come_r = swap(leave_l, 2), swap(leave_r, 4)
        halves = n_mp // 2
        across = halves * w
        pieces = shape((half, halves, rows + EXTRA, width), bf16)
        places = [order.index(r) for r in range(n_mp)]

        def attention(which, grad_attended):
            return call(
                functools.partial(att_backward, which, places),
                "att_backward",
                [shape((length, across), bf16)] * 3 + [pieces] * 2,
                [
                    index,
                    queries,
                    keys,
                    values,
                    contexts,
                    grad_attended,
                    tokens,
                    wo,
                    seg_row,
                    seg_col,
                    low_sums,
                    sums_one,
                    sums_two,
                ],
                "s" + "v" * 12,
                [
                    pltpu.VMEM((length, across), bf16),
                    pltpu.VMEM((blocks, 3 * PASSAGE, PASSAGE), f32),
                    pltpu.VMEM((1, length, length), bf16),
                    pltpu.VMEM((1, length, length), bf16),
                ],
            )

        q0, k0, v0, keep_0, send_0 = attention(0, grad_attended)
        come_x, come_y, q0, k0, v0, keep_0, send_0 = tie(
            come_x, come_y, q0, k0, v0, keep_0, send_0
        )
        got_0 = swap(send_0, 1)
        parts_x, parts_y = add(stay_x, come_x), add(stay_y, come_y)
        grad_attended, parts_x, got_0 = tie(grad_attended, parts_x, got_0)
        line_x = line_moves(parts_x, order)
        q1, k1, v1, keep_1, send_1 = attention(1, grad_attended)
        q1, k1, v1, keep_1, send_1, come_l, come_r, line_x[1:], parts_y = tie(
            q1, k1, v1, keep_1, send_1, come_l, come_r, line_x[1:], parts_y
        )
        got_1 = swap(send_1, 1)
        line_y = line_moves(parts_y, order)
        now_l, now_r = add(stay_l, come_l), add(stay_r, come_r)
        come_l, come_r = swap(now_l[1], 4), swap(now_r[1], 2)
        keep_att = jnp.concatenate([keep_0, keep_1], axis=1)
        got_att = jnp.concatenate([got_0, got_1], axis=1)
        leave_left, leave_right, stay_left, stay_right = plane_halves(keep_att, got_att)
        come_l, come_r, leave_left, leave_right = tie(come_l, come_r, leave_left, leave_right)
        come_left, come_right = swap(leave_left, 2), swap(leave_right, 4)
        up_parts = jnp.concatenate([add(now_l[0], come_l), add(now_r[0], come_r)], axis=-1)
        up_parts, line_y = tie(up_parts, line_y)
        up_line = line_moves(up_parts, order)
        down_x, down_y = line_total(line_x), line_total(line_y)
        come_left, come_right, up_line[1:3], down_x, down_y = tie(
            come_left, come_right, up_line[1:3], down_x, down_y
        )
        left_now, right_now = add(stay_left, come_left), add(stay_right, come_right)
        come_left, come_right = swap(left_now[1], 4), swap(right_now[1], 2)
        up_line[3:], come_left, come_right, down_x, down_y = tie(
            up_line[3:], come_left, come_right, down_x, down_y
        )
        come_x, come_y = swap(down_x, 4), swap(down_y, 2)
        att_parts = jnp.concatenate(
            [add(left_now[0], come_left), add(right_now[0], come_right)], axis=-1
        )
        att_line = line_moves(att_parts, range(n_mp))
        down_x, down_y = add(down_x, come_x), add(down_y, come_y)
        come_x, come_y = swap(down_x, 2), swap(down_y, 4)
        up_total = line_total(up_line)
        (grad_tokens,) = call(
            input_backward,
            "input_backward",
            [tok_low],
            [q0, k0, v0, q1, k1, v1, grad_one, weights],
            "v" * 8,
        )
        att_line[1], come_x, come_y, up_total, grad_tokens = tie(
            att_line[1], come_x, come_y, up_total, grad_tokens
        )
        up_four = plane_swap(up_total)
        down_four = [down_x, come_x, down_y, come_y]
        att_line[2:], up_four = tie(att_line[2:], up_four)
        att_four = plane_swap(line_total(att_line))
        down_four, up_four = jnp.stack(down_four), jnp.stack(up_four)
        (grad_down,) = call(
            functools.partial(finish_ffn, places_by_axis),
            "finish_down",
            [shape((units, width), f32)],
            [index, down_four, swap(down_four, 1)],
            "svv",
        )
        (grad_up,) = call(
            functools.partial(finish_ffn, eighths),
            "finish_up",
            [shape((width, units), f32)],
            [index, up_four, swap(up_four, 1)],
            "svv",
        )
        att_four, grad_down, grad_up = tie(att_four, grad_down, grad_up)
        att_four = jnp.stack(att_four)
        att_other = swap(att_four, 1)
        grad_query, grad_key, grad_value, grad_output, sums = call(
            finish_att,
            "finish_att",
            [shape((w, width), f32)] * 4 + [shape((GROUP * EXTRA, width), f32)],
            [index, att_four, att_other],
            "svv",
            [pltpu.VMEM((4 * w, width), f32)],
        )
        return (
            output,
            grad_tokens,
            grad_query.T,
            sums[(GROUP - 1) * EXTRA, :w],
            grad_key.T,
            grad_value.T,
            sums[(GROUP - 1) * EXTRA, w : 2 * w],
            grad_output,
            sums[EXTRA],
            sums[2 * EXTRA],
            sums[3 * EXTRA],
            grad_up,
            sums[0],
            grad_down,
            sums[4 * EXTRA],
            sums[5 * EXTRA],
            sums[6 * EXTRA],
        )

    everywhere, rows, columns, units = P(), P(("dp", "mp"), None), P(None, "mp"), P("mp")
    in_specs = (
        rows,
        P("dp", None),
        columns,
        units,
        columns,
        columns,
        units,
        P("mp", None),
        everywhere,
        everywhere,
        everywhere,
        columns,
        units,
        P("mp", None),
        everywhere,
        everywhere,
        everywhere,
        rows,
    )
    out_specs = (
        rows,
        rows,
        columns,
        units,
        columns,
        columns,
        units,
        P("mp", None),
        everywhere,
        everywhere,
        everywhere,
        columns,
        units,
        P("mp", None),
        everywhere,
        everywhere,
        everywhere,
    )
    return jax.shard_map(shards, mesh=mesh, in_specs=in_specs, out_specs=out_specs, check_vma=False)
```

```python
import functools
import math

import jax
import jax.numpy as jnp
from jax import lax
from jax.experimental import pallas as pl
from jax.experimental.pallas import tpu as pltpu
from jax.sharding import PartitionSpec as P

HEAD_DIM = 64
PASSAGE = 128
GROUP = 8
EXTRA = 8
LANES = 128
CHUNK = 128
SCOPED = {
    "first_piece": 60,
    "att_forward": 7,
    "ffn_first": 5,
    "ffn_last": 10,
    "ffn_slopes": 8,
    "ffn_grads": 5,
    "ffn_norm": 7,
    "att_backward": 11,
    "input_backward": 4,
    "finish_down": 4,
    "finish_up": 4,
    "finish_att": 6,
}
epsilon = 1e-05
bf16 = jnp.bfloat16
f32 = jnp.float32


def nn(left, right):
    return lax.dot_general(left, right, (((1,), (0,)), ((), ())), preferred_element_type=f32)


def nt(left, right):
    return lax.dot_general(left, right, (((1,), (1,)), ((), ())), preferred_element_type=f32)


def tn(left, right):
    return lax.dot_general(left, right, (((0,), (0,)), ((), ())), preferred_element_type=f32)


def call(body, name, outs, args, spaces, scratch=(), out_spaces=None):
    def spec(kind):
        if kind == "s":
            return pl.BlockSpec(memory_space=pltpu.SMEM)
        if kind == "h":
            return pl.BlockSpec(memory_space=pltpu.HBM)
        return pl.BlockSpec(memory_space=pltpu.VMEM)

    out_spaces = out_spaces or "v" * len(outs)
    def size(array):
        return math.prod(array.shape) * jnp.dtype(array.dtype).itemsize

    every = list(zip(args, spaces)) + list(zip(outs, out_spaces))
    moved = sum(size(array) for array, kind in every)
    return pl.pallas_call(
        body,
        name=name,
        out_shape=tuple(outs),
        in_specs=[spec(k) for k in spaces],
        out_specs=tuple(spec(k) for k in out_spaces),
        scratch_shapes=list(scratch),
        compiler_params=pltpu.CompilerParams(vmem_limit_bytes=SCOPED[name] << 20),
        cost_estimate=pl.CostEstimate(flops=0, bytes_accessed=moved // 64, transcendentals=0),
    )(*args)


def vector(ref):
    return ref[...].astype(f32).reshape(1, ref.shape[0])


def places_by_axis(index):
    x, y = index & 3, ((index >> 1) & 2) | (index & 1)
    return [x, x ^ 1, x ^ 2, x ^ 3, 4 + y, 4 + (y ^ 1), 4 + (y ^ 2), 4 + (y ^ 3)]


def eighths(index):
    return [index ^ s for s in range(GROUP)]


def places_gathered(index):
    places = places_by_axis(index)
    return places[:4] + places[6:] + places[4:6]


def place_slots(pieces, others, r, down_rows, rows, places, dest, base, columns):
    upper, lower = slice(0, rows), slice(rows, 2 * rows)
    sources = ((0, upper), (1, upper), (2, lower), (4, lower))
    if not down_rows:
        sources = ((0, lower), (1, lower), (2, upper), (3, upper))
    for s in range(GROUP):
        piece, part = sources[s // 2]
        at = pl.multiple_of(base + places[s] * rows, rows)
        dest[pl.ds(at, rows), columns] = (others if s % 2 else pieces)[piece][r, part]


def put_slots(index, r, rows, low, keep, send, by_axis=False):
    size = rows[0].shape[0]
    x, y = index & 3, ((index >> 1) & 2) | (index & 1)
    for odd in range(2):

        @pl.when((index & 1) == odd)
        def _():
            for d in range(GROUP):
                dest = send if (d ^ odd) & 1 else keep
                spot = (index ^ d) >> 1
                if by_axis:
                    spot = (x ^ d) >> 1 if d < 4 else 2 + ((y ^ (d - 4)) >> 1)
                dest[spot, r, low : low + size] = rows[d]


def normalize(total):
    centred = total - jnp.mean(total, axis=-1, keepdims=True)
    inverse = lax.rsqrt(jnp.mean(centred * centred, axis=-1, keepdims=True) + epsilon)
    return centred * inverse, inverse


def norm_backward(grad_out, normal, inverse, norm_gain):
    scaled = grad_out * norm_gain
    return inverse * (
        scaled
        - jnp.mean(scaled, axis=-1, keepdims=True)
        - normal * jnp.mean(scaled * normal, axis=-1, keepdims=True)
    )


def column_sum(array):
    return jnp.sum(array, axis=0, keepdims=True)


def folded(array):
    return jnp.sum(array.reshape(-1, 8, array.shape[1]), axis=0)


def by_rows(length, body, sums, width):
    def step(i, totals):
        found = body(pl.ds(pl.multiple_of(i * CHUNK, CHUNK), CHUNK))
        return tuple(t + folded(f) for t, f in zip(totals, found))

    zeros = tuple(jnp.zeros((8, width), f32) for _ in range(sums))
    totals = lax.fori_loop(0, length // CHUNK, step, zeros, unroll=1)
    return tuple(column_sum(t) for t in totals)


def band(block, length):
    return max(0, (block - 1) * PASSAGE), min(length, (block + 2) * PASSAGE)


def clear_outside(array, length):
    for b in range(length // PASSAGE):
        lo, hi = band(b, length)
        block = slice(b * PASSAGE, (b + 1) * PASSAGE)
        for low, high in ((0, lo), (hi, length)):
            if high > low:
                shape = (array.shape[0], high - low, PASSAGE)
                array[:, low:high, block] = jnp.zeros(shape, array.dtype)


def fill_bias(bias, seg_row, seg_col, length):
    for b in range(length // PASSAGE):
        lo, hi = band(b, length)
        same = seg_col[lo:hi, :] == seg_row[:, b * PASSAGE : (b + 1) * PASSAGE]
        bias[b, : hi - lo, :] = jnp.where(same, 0.0, -1e30)


def softmax_columns(scores):
    expo = jnp.exp(scores - jnp.max(scores, axis=0, keepdims=True))
    return expo * (1.0 / jnp.sum(expo, axis=0, keepdims=True))


def first_piece(
    index_ref, own_q, own_k, own_v, own_o, query_bias, value_bias, up_bias, out, owns,
    query_row, value_row, up_row, sems,
):
    w = own_q.shape[0]
    rows = w // 2
    small = [
        pltpu.make_async_copy(own, owns.at[pl.ds(m * w, w)], sems.at[3 + m])
        for m, own in enumerate((own_q, own_k, own_v, own_o))
    ]
    small += [
        pltpu.make_async_copy(query_bias, query_row, sems.at[0]),
        pltpu.make_async_copy(value_bias, value_row, sems.at[1]),
        pltpu.make_async_copy(up_bias, up_row, sems.at[2]),
    ]
    for copy in small:
        copy.start()
    for copy in small:
        copy.wait()
    out[:rows, :] = owns[pl.ds(pl.multiple_of(index_ref[0] * rows, rows), rows), :]
    out[rows:, :] = jnp.zeros((EXTRA, out.shape[1]), bf16)
    out[rows : rows + 1, :w] = vector(query_row).astype(bf16)
    out[rows : rows + 1, w : 2 * w] = vector(value_row).astype(bf16)
    out[rows + 1 : rows + 2, :] = vector(up_row).astype(bf16)


def att_forward(
    index_ref, tokens, owns, four, other, bias_0, bias_1, bias_2, bias_3,
    output_bias, seg_row, seg_col,
    queries, keys, values, contexts, normal, inverse, weights, wo,
    bias, probs_t, row, attended,
):
    length, width = tokens.shape
    w = owns.shape[0] // 4
    quarters = width // w
    rows = four.shape[2]
    index = index_ref[0]
    for m in range(3):
        weights[m, :w, :] = owns[m * w : (m + 1) * w, :]
    wo[:w, :] = owns[3 * w :, :]
    for r in range(1, quarters):
        for s in range(GROUP):
            owner = index ^ s
            at = pl.multiple_of(r * w + (owner & 1) * rows, rows)
            source = other if s % 2 else four

            @pl.when(owner < 6)
            def _():
                weights[owner >> 1, pl.ds(at, rows), :] = source[s // 2, r - 1]

            @pl.when(owner >= 6)
            def _():
                wo[pl.ds(at, rows), :] = source[s // 2, r - 1]

    fill_bias(bias, seg_row, seg_col, length)
    clear_outside(probs_t, length)
    for r, source in enumerate((bias_0, bias_1, bias_2, bias_3)):
        for i in range(2):
            piece = source[rows : rows + 1, i * w : (i + 1) * w].astype(f32)
            row[i : i + 1, r * w : (r + 1) * w] = piece
    low = (nt(tokens[...], weights[0]) + row[0:1, :]).astype(bf16)
    queries[...] = (low.astype(f32) * (HEAD_DIM**-0.5)).astype(bf16)
    keys[...] = nt(tokens[...], weights[1]).astype(bf16)
    values[...] = (nt(tokens[...], weights[2]) + row[1:2, :]).astype(bf16)
    first = lax.broadcasted_iota(jnp.int32, (PASSAGE, LANES), 1) < HEAD_DIM
    first_all = lax.broadcasted_iota(jnp.int32, (length, LANES), 1) < HEAD_DIM

    def pair(i, carry):
        at = pl.ds(pl.multiple_of(i * LANES, LANES), LANES)
        for half, mine in enumerate((first, jnp.logical_not(first))):
            for b in range(length // PASSAGE):
                lo, hi = band(b, length)
                block = slice(b * PASSAGE, (b + 1) * PASSAGE)
                q = queries[block, at]
                masked = jnp.where(mine, q, jnp.zeros_like(q))
                scores = nt(keys[lo:hi, at], masked) + bias[b, : hi - lo, :]
                probs_t[half, lo:hi, block] = softmax_columns(scores).astype(bf16)
        found = [tn(probs_t[half], values[:, at]) for half in range(2)]
        contexts[:, at] = jnp.where(first_all, *found).astype(bf16)
        return carry

    lax.fori_loop(0, width // LANES, pair, 0)
    attended[...] = nn(contexts[...], wo[...]) + vector(output_bias)

    def norm(rows):
        n, r = normalize(tokens[rows, :].astype(f32) + attended[rows, :])
        normal[rows, :] = n
        inverse[rows, :] = r
        return ()

    by_rows(length, norm, 0, width)


def gelu_rows(hidden, activated, slope, columns):
    def step(i, carry):
        rows = pl.ds(pl.multiple_of(i * CHUNK, CHUNK), CHUNK)
        value = hidden[rows, :]
        cumulative = 0.5 * (1.0 + lax.erf(value * 0.7071067811865476))
        density = jnp.exp(-0.5 * value * value) * 0.3989422804014327
        activated[rows, columns] = (value * cumulative).astype(bf16)
        slope[rows, columns] = (cumulative + value * density).astype(bf16)
        return carry

    lax.fori_loop(0, hidden.shape[0] // CHUNK, step, 0)


def each(count, body):
    def step(r, carry):
        body(r)
        return carry

    lax.fori_loop(0, count, step, 0)


def columns_of(r, size):
    return pl.ds(pl.multiple_of(r * size, LANES), size)


def ffn_first(
    index_ref, normal, gain, shift, down_bias, bias_0, bias_1, bias_2, own_up, own_down,
    left, from_x, from_y, corner, right, left_o, from_x_o, from_y_o, corner_o, right_o,
    activated, slope, low_t, mixed, up, down,
    hidden, lines, low_rows,
):
    units = own_up.shape[1]
    four = (left, from_x, from_y, corner, right)
    other = (left_o, from_x_o, from_y_o, corner_o, right_o)
    rows = corner.shape[1]
    quarters = corner.shape[0] + 1
    biases = (bias_0, bias_1, bias_2)
    up_places, down_places = eighths(index_ref[0]), places_gathered(index_ref[0])
    normed = normal[...] * vector(gain) + vector(shift)
    low = normed.astype(bf16)
    low_t[...] = low.T
    low_rows[...] = low
    mixed[...] = normed + vector(down_bias)
    for r in range(quarters):
        mine = slice(r * units, (r + 1) * units)
        if r == 0:
            up[:, mine] = own_up[...]
            down[mine, :] = own_down[...]
        else:
            place_slots(four, other, r - 1, False, rows, up_places, up, 0, mine)
            place_slots(four, other, r - 1, True, rows, down_places, down, r * units, slice(None))
        at = biases[r].shape[0] - EXTRA + 1
        lines[r, :, :] = jnp.broadcast_to(biases[r][at : at + 1, :].astype(f32), lines.shape[1:])

    def quarter(r):
        mine = columns_of(r, units)
        hidden[...] = nn(low_rows[...], up[:, mine]) + lines[r, 0:1, :]
        gelu_rows(hidden, activated, slope, mine)

    each(quarters, quarter)
    mixed[...] += nn(activated[...], down[...])


def ffn_last(
    index_ref, normal, cotangent, gain, shift, second_gain, second_shift, bias, activated, mixed,
    left, from_x, from_y, corner, right, left_o, from_x_o, from_y_o, corner_o, right_o,
    output, grad_mixed, grad_two, sums, slope, up, down, keep, send,
    own, total,
):
    length, width = normal.shape
    units = up.shape[1]
    four = (left, from_x, from_y, corner, right)
    other = (left_o, from_x_o, from_y_o, corner_o, right_o)
    rows = corner.shape[1]
    index = index_ref[0]
    place_slots(four, other, 0, False, rows, eighths(index), up, 0, slice(None))
    place_slots(four, other, 0, True, rows, places_gathered(index), down, 0, slice(None))
    low = (normal[...] * vector(gain) + vector(shift)).astype(bf16)
    at = bias.shape[0] - EXTRA + 1
    total[...] = nn(low, up[...]) + bias[at : at + 1, :].astype(f32)
    gelu_rows(total, own, slope, slice(None))
    total[...] = mixed[...] + nn(own[...], down[...])
    out_gain, out_shift = vector(second_gain), vector(second_shift)

    def norm(rows):
        n, inverse = normalize(total[rows, :])
        output[rows, :] = (n * out_gain + out_shift).astype(bf16)
        grad_out = cotangent[rows, :].astype(f32)
        two = norm_backward(grad_out, n, inverse, out_gain)
        grad_two[rows, :] = two
        low = two.astype(bf16)
        grad_mixed[rows, :] = low
        return low.astype(f32), grad_out * n, grad_out

    sums[...] = jnp.zeros_like(sums)
    for i, found in enumerate(by_rows(length, norm, 3, width)):
        sums[i : i + 1, :] = found

    def put(r, left):
        grad = tn(left, grad_mixed[...]).astype(bf16)
        put_slots(index, r, grad.reshape(GROUP, -1, width), 0, keep, send, True)

    each(keep.shape[1] - 1, lambda r: put(r, activated[:, columns_of(r, units)]))
    put(keep.shape[1] - 1, own[...])


def ffn_slopes(grad_mixed, slope, slope_last, down, down_last, hidden, sums):
    units = down_last.shape[0]
    sums[...] = jnp.zeros_like(sums)

    def quarter(r, weight, factor):
        low = (nt(grad_mixed[...], weight) * factor.astype(f32)).astype(bf16)
        hidden[:, columns_of(r, units)] = low
        sums[pl.ds(r, 1), :] = column_sum(low.astype(f32))

    def inner(r):
        mine = columns_of(r, units)
        quarter(r, down[mine, :], slope[:, mine])

    each(down.shape[0] // units, inner)
    quarter(down.shape[0] // units, down_last[...], slope_last[...])


def ffn_grads(index_ref, hidden, low_t, keep, send):
    units = keep.shape[3]

    def quarter(r):
        grad = nn(low_t[...], hidden[:, columns_of(r, units)]).astype(bf16)
        put_slots(index_ref[0], r, grad.reshape(GROUP, -1, units), 0, keep, send)

    each(keep.shape[1], quarter)


def ffn_norm(
    hidden, grad_two, normal, inverse, gain_ref, up, up_last,
    grad_one, grad_attended, sums,
    total,
):
    length, width = normal.shape
    inner = up.shape[1]
    total[...] = nt(hidden[:, :inner], up[...]) + grad_two[...]
    total[...] += nt(hidden[:, inner:], up_last[...])
    gain = vector(gain_ref)

    def norm(at):
        grad_normed = total[at, :]
        n = normal[at, :]
        one = norm_backward(grad_normed, n, inverse[at, :], gain)
        grad_one[at, :] = one
        low = one.astype(bf16)
        grad_attended[at, :] = low
        return low.astype(f32), grad_normed * n, grad_normed

    sums[...] = jnp.zeros_like(sums)
    for i, found in enumerate(by_rows(length, norm, 3, width)):
        sums[i : i + 1, :] = found


def att_backward(
    part, places, index_ref, queries, keys, values, contexts, grad_attended, tokens, wo,
    seg_row, seg_col, unit_sums, sums_one, sums_two,
    grad_queries, grad_keys, grad_values, keep, send,
    grad_contexts, bias, probs_t, scores_t,
):
    length, width = tokens.shape
    quarters, rows = keep.shape[1], keep.shape[2] - EXTRA
    w = 2 * rows
    across = quarters * w
    index = index_ref[0]
    scale = HEAD_DIM**-0.5
    fill_bias(bias, seg_row, seg_col, length)
    clear_outside(probs_t, length)
    clear_outside(scores_t, length)
    low = part * across
    grad_contexts[...] = nt(grad_attended[...], wo[low : low + across, :]).astype(bf16)
    lane = lax.broadcasted_iota(jnp.int32, (PASSAGE, LANES), 1) // HEAD_DIM
    lane_all = lax.broadcasted_iota(jnp.int32, (length, LANES), 1) // HEAD_DIM

    def head(i, carry):
        half = i & 1
        here = pl.ds(pl.multiple_of((i >> 1) * LANES, LANES), LANES)
        at = pl.ds(pl.multiple_of(low + (i >> 1) * LANES, LANES), LANES)
        mine = lane == half
        for b in range(length // PASSAGE):
            lo, hi = band(b, length)
            block = slice(b * PASSAGE, (b + 1) * PASSAGE)
            q = queries[block, at]
            g = grad_contexts[block, here]
            zero = jnp.zeros_like(q)
            scores = nt(keys[lo:hi, at], jnp.where(mine, q, zero)) + bias[b, : hi - lo, :]
            probs = softmax_columns(scores)
            grad_probs = nt(values[lo:hi, at], jnp.where(mine, g, zero))
            inner = jnp.sum(grad_probs * probs, axis=0, keepdims=True)
            probs_t[0, lo:hi, block] = probs.astype(bf16)
            scores_t[0, lo:hi, block] = (probs * (grad_probs - inner)).astype(bf16)
        mine = lane_all == half
        for out, found in (
            (grad_queries, tn(scores_t[0], keys[:, at]) * scale),
            (grad_keys, nn(scores_t[0], queries[:, at])),
            (grad_values, nn(probs_t[0], grad_contexts[:, here])),
        ):
            out[:, here] = jnp.where(mine, found.astype(bf16), out[:, here])
        return carry

    lax.fori_loop(0, across // HEAD_DIM, head, 0)
    grads = (
        lambda: tn(grad_queries[...], tokens[...]),
        lambda: tn(grad_keys[...], tokens[...]),
        lambda: tn(grad_values[...], tokens[...]),
        lambda: tn(contexts[:, low : low + across], grad_attended[...]),
    )
    grads = [make().astype(bf16).reshape(quarters, 2, rows, width) for make in grads]
    query_sum = column_sum(grad_queries[...].astype(f32))
    value_sum = column_sum(grad_values[...].astype(f32))
    for r in range(quarters):
        put_slots(index, r, [grads[d // 2][r, d % 2] for d in range(GROUP)], 0, keep, send)
        cols = slice(r * w, (r + 1) * w)
        last = jnp.concatenate(
            [query_sum[:, cols], value_sum[:, cols], jnp.zeros((1, width - 2 * w), f32)], axis=1
        )
        at = places[part * quarters + r]
        lines = [unit_sums[at : at + 1, :]]
        lines += [sums[i : i + 1, :] for sums in (sums_one, sums_two) for i in range(3)]
        lines = [jnp.broadcast_to(line, (EXTRA, width)).astype(bf16) for line in lines + [last]]
        put_slots(index, r, lines, rows, keep, send)


def input_backward(q0, k0, v0, q1, k1, v1, grad_one, weights, out):
    half = q0.shape[1]
    total = grad_one[...]
    for m, (left, right) in enumerate(((q0, q1), (k0, k1), (v0, v1))):
        total += nn(left[...], weights[m, :half]) + nn(right[...], weights[m, half:])
    out[...] = total.astype(bf16)


def finish_ffn(places_of, index_ref, four, other, out):
    rows = four.shape[1]
    for s, place in enumerate(places_of(index_ref[0])):
        at = pl.multiple_of(place * rows, rows)
        out[pl.ds(at, rows), :] = (other if s % 2 else four)[s // 2].astype(f32)


def finish_att(index_ref, four, other, gq, gk, gv, go, query_sum, value_sum, *rest):
    sums, whole = rest[:-2], rest[-1]
    lines = rest[-2]
    rows = four.shape[1] - EXTRA
    w = 2 * rows
    for s in range(GROUP):
        slot = (other if s % 2 else four)[s // 2].astype(f32)
        owner = index_ref[0] ^ s
        whole[pl.ds(pl.multiple_of(owner * rows, rows), rows), :] = slot[:rows]
        lines[pl.ds(pl.multiple_of(owner * EXTRA, EXTRA), EXTRA), :] = slot[rows:]
    for m, out in enumerate((gq, gk, gv, go)):
        out[...] = whole[m * w : (m + 1) * w, :]
    for j, out in enumerate(sums):
        out[...] = lines[j * EXTRA, :]
    last = len(sums) * EXTRA
    query_sum[...] = lines[last, :w]
    value_sum[...] = lines[last, w : 2 * w]


def solution(mesh):
    n_dp, n_mp = mesh.shape["dp"], mesh.shape["mp"]
    if n_dp % GROUP or n_mp % 2:
        raise ValueError("mesh")

    def rotate(array, step):
        return lax.ppermute(array, "mp", [(i, (i + step) % n_mp) for i in range(n_mp)])

    def swap(array, bits):
        return lax.ppermute(array, "dp", [(i, i ^ bits) for i in range(n_dp)])

    def plane_swap(array):
        return [array, swap(array, 2), swap(array, 4), swap(array, 6)]

    def add(left, right):
        return (left.astype(f32) + right.astype(f32)).astype(bf16)

    def tie(*arrays):
        return lax.optimization_barrier(arrays)

    def after(array, *others):
        return tie(array, *others)[0]

    def first_axis(bits):
        go = slice(1, None, 2) if bits == 2 else slice(2, None)
        stay = slice(0, None, 2) if bits == 2 else slice(0, 2)
        return go, stay

    def plane_first(keep, got, bits):
        go, stay = first_axis(bits)
        return add(keep[go], got[go]), add(keep[stay], got[stay])

    def line_moves(parts, order):
        found = {r: rotate(parts[i], -r) if r else parts[i] for i, r in enumerate(order)}
        return [found[r] for r in range(n_mp)]

    def line_total(moved):
        moved = [array.astype(f32) for array in moved]
        total = sum(moved[0::2][1:], moved[0]) + sum(moved[1::2][1:], moved[1])
        if n_dp > GROUP:
            groups = [[i + GROUP * k for k in range(n_dp // GROUP)] for i in range(GROUP)]
            total = lax.psum(total, "dp", axis_index_groups=groups)
        return total.astype(bf16)

    def shards(
        tokens,
        segment_ids,
        query_weight,
        query_bias,
        key_weight,
        value_weight,
        value_bias,
        output_weight,
        output_bias,
        first_gain,
        first_shift,
        up_weight,
        up_bias,
        down_weight,
        down_bias,
        second_gain,
        second_shift,
        cotangent,
    ):
        length, width = tokens.shape
        w = query_weight.shape[1]
        units = up_weight.shape[1]
        rows = width // GROUP
        blocks = length // PASSAGE
        half, part = GROUP // 2, units // GROUP
        shape = jax.ShapeDtypeStruct
        place = lax.axis_index("mp")
        within = lax.axis_index("dp") % GROUP
        index = within.astype(jnp.int32).reshape(1)
        seg_row = lax.dynamic_slice_in_dim(segment_ids, place, 1, 0)
        seg_col = seg_row.reshape(length, 1)

        def slot(array, at, size):
            return lax.dynamic_slice_in_dim(array, at * size, size, 0)

        owns = [query_weight.T, key_weight.T, value_weight.T, output_weight]
        piece, owns = call(
            first_piece,
            "first_piece",
            [shape((rows + EXTRA, width), bf16), shape((4 * w, width), bf16)],
            [index, *owns, query_bias, value_bias, up_bias],
            "s" + "h" * 7,
            [
                pltpu.VMEM((w,), bf16),
                pltpu.VMEM((w,), bf16),
                pltpu.VMEM((units,), bf16),
                pltpu.SemaphoreType.DMA((7,)),
            ],
        )
        biases = [piece] + [rotate(piece, r) for r in range(1, n_mp)]
        order = [r for r in range(n_mp) if r != n_mp // 2] + [n_mp // 2]
        ffn_biases = [biases[r] for r in order]
        att_line = jnp.stack([g[:rows] for g in biases[1:]])
        by_x, by_y = within & 3, ((within >> 1) & 2) | (within & 1)
        piece = jnp.concatenate(
            [
                slot(down_weight, by_x, part),
                slot(up_weight, within, rows),
                slot(down_weight, 4 + by_y, part),
            ]
        )
        piece, att_line = tie(piece, att_line)
        ffn_line = [rotate(piece, r) for r in order[1:]]

        def plane_mixed(line):
            left = jnp.stack([g[: part + rows] for g in line])
            right = jnp.stack([g[part:] for g in line])
            corner = swap(jnp.stack([g[part : part + rows] for g in line]), 6)
            return left, swap(left, 2), swap(right, 4), corner, right

        att_four = [att_line] + [swap(att_line, b) for b in (2, 4, 6)]
        att_four, ffn_line[:-1] = tie(att_four, ffn_line[:-1])
        att_four = jnp.stack(att_four)
        att_other = swap(att_four, 1)
        ffn_four = plane_mixed(ffn_line[:-1])
        tok_low = shape((length, width), bf16)
        tok_wide = shape((length, width), f32)
        queries, keys, values, contexts, normal, inverse, weights, wo = call(
            att_forward,
            "att_forward",
            [tok_low] * 4
            + [
                tok_wide,
                shape((length, 1), f32),
                shape((3, n_mp * w, width), bf16),
                shape((n_mp * w, width), bf16),
            ],
            [
                index,
                tokens,
                owns,
                att_four,
                att_other,
                *biases,
                output_bias,
                seg_row,
                seg_col,
            ],
            "s" + "v" * 11,
            [
                pltpu.VMEM((blocks, 3 * PASSAGE, PASSAGE), f32),
                pltpu.VMEM((2, length, length), bf16),
                pltpu.VMEM((8, width), f32),
                pltpu.VMEM((length, width), f32),
            ],
        )
        normal, ffn_four, ffn_line[-1] = tie(normal, ffn_four, ffn_line[-1])
        ffn_other = [swap(array, 1) for array in ffn_four]
        last_four = plane_mixed(ffn_line[-1:])
        inner = (n_mp - 1) * units
        hidden_low = shape((length, inner), bf16)
        activated, slope, low_t, mixed, up, down = call(
            ffn_first,
            "ffn_first",
            [
                hidden_low,
                hidden_low,
                shape((width, length), bf16),
                tok_wide,
                shape((width, inner), bf16),
                shape((inner, width), bf16),
            ],
            [
                index,
                normal,
                first_gain,
                first_shift,
                down_bias,
                *ffn_biases[:-1],
                up_weight,
                down_weight,
                *ffn_four,
                *ffn_other,
            ],
            "s" + "v" * 19,
            [
                pltpu.VMEM((length, units), f32),
                pltpu.VMEM((n_mp, 8, units), f32),
                pltpu.VMEM((length, width), bf16),
            ],
        )
        activated, last_four = tie(activated, last_four)
        last_other = [swap(array, 1) for array in last_four]
        pieces = shape((half, n_mp, part, width), bf16)
        (
            output,
            grad_mixed,
            grad_two,
            sums_two,
            slope_last,
            up_last,
            down_last,
            keep_down,
            send_down,
        ) = call(
            ffn_last,
            "ffn_last",
            [
                tok_low,
                tok_low,
                tok_wide,
                shape((8, width), f32),
                shape((length, units), bf16),
                shape((width, units), bf16),
                shape((units, width), bf16),
                pieces,
                pieces,
            ],
            [
                index,
                normal,
                cotangent,
                first_gain,
                first_shift,
                second_gain,
                second_shift,
                ffn_biases[-1],
                activated,
                mixed,
                *last_four,
                *last_other,
            ],
            "s" + "v" * 19,
            [pltpu.VMEM((length, units), bf16), pltpu.VMEM((length, width), f32)],
        )
        got_down = swap(send_down, 1)
        hidden, low_sums = call(
            ffn_slopes,
            "ffn_slopes",
            [shape((length, n_mp * units), bf16), shape((8, units), f32)],
            [grad_mixed, slope, slope_last, down, down_last],
            "v" * 5,
        )
        hidden, got_down = tie(hidden, got_down)
        leave_x, leave_y = add(keep_down[1], got_down[1]), add(keep_down[3], got_down[3])
        stay_x, stay_y = add(keep_down[0], got_down[0]), add(keep_down[2], got_down[2])
        hidden, leave_x, leave_y = tie(hidden, leave_x, leave_y)
        come_x, come_y = swap(leave_x, 2), swap(leave_y, 4)
        pieces = shape((half, n_mp, rows, units), bf16)
        keep_up, send_up = call(
            ffn_grads, "ffn_grads", [pieces, pieces], [index, hidden, low_t], "svv"
        )
        hidden, keep_up, send_up = tie(hidden, keep_up, send_up)
        got_up = swap(send_up, 1)
        grad_one, grad_attended, sums_one = call(
            ffn_norm,
            "ffn_norm",
            [tok_wide, tok_low, shape((8, width), f32)],
            [hidden, grad_two, normal, inverse, first_gain, up, up_last],
            "v" * 7,
            [pltpu.VMEM((length, width), f32)],
        )
        grad_attended, sums_one, got_up = tie(grad_attended, sums_one, got_up)
        cut = units // 2
        left, right = slice(0, cut), slice(cut, None)

        def plane_halves(keep, got):
            leaves = add(keep[1::2, ..., left], got[1::2, ..., left])
            leaves_r = add(keep[2:, ..., right], got[2:, ..., right])
            stays = add(keep[0::2, ..., left], got[0::2, ..., left])
            stays_r = add(keep[:2, ..., right], got[:2, ..., right])
            return leaves, leaves_r, stays, stays_r

        leave_l, leave_r, stay_l, stay_r = plane_halves(keep_up, got_up)
        grad_attended, leave_l, leave_r = tie(grad_attended, leave_l, leave_r)
        come_l, come_r = swap(leave_l, 2), swap(leave_r, 4)
        halves = n_mp // 2
        across = halves * w
        pieces = shape((half, halves, rows + EXTRA, width), bf16)
        places = [order.index(r) for r in range(n_mp)]

        def attention(which, grad_attended):
            return call(
                functools.partial(att_backward, which, places),
                "att_backward",
                [shape((length, across), bf16)] * 3 + [pieces] * 2,
                [
                    index,
                    queries,
                    keys,
                    values,
                    contexts,
                    grad_attended,
                    tokens,
                    wo,
                    seg_row,
                    seg_col,
                    low_sums,
                    sums_one,
                    sums_two,
                ],
                "s" + "v" * 12,
                [
                    pltpu.VMEM((length, across), bf16),
                    pltpu.VMEM((blocks, 3 * PASSAGE, PASSAGE), f32),
                    pltpu.VMEM((1, length, length), bf16),
                    pltpu.VMEM((1, length, length), bf16),
                ],
            )

        q0, k0, v0, keep_0, send_0 = attention(0, grad_attended)
        come_x, come_y, q0, k0, v0, keep_0, send_0 = tie(
            come_x, come_y, q0, k0, v0, keep_0, send_0
        )
        got_0 = swap(send_0, 1)
        parts_x, parts_y = add(stay_x, come_x), add(stay_y, come_y)
        grad_attended, parts_x, got_0 = tie(grad_attended, parts_x, got_0)
        line_x = line_moves(parts_x, order)
        q1, k1, v1, keep_1, send_1 = attention(1, grad_attended)
        q1, k1, v1, keep_1, send_1, come_l, come_r, line_x[1:], parts_y = tie(
            q1, k1, v1, keep_1, send_1, come_l, come_r, line_x[1:], parts_y
        )
        got_1 = swap(send_1, 1)
        line_y = line_moves(parts_y, order)
        now_l, now_r = add(stay_l, come_l), add(stay_r, come_r)
        come_l, come_r = swap(now_l[1], 4), swap(now_r[1], 2)
        keep_att = jnp.concatenate([keep_0, keep_1], axis=1)
        got_att = jnp.concatenate([got_0, got_1], axis=1)
        leave_left, leave_right, stay_left, stay_right = plane_halves(keep_att, got_att)
        come_l, come_r, leave_left, leave_right = tie(come_l, come_r, leave_left, leave_right)
        come_left, come_right = swap(leave_left, 2), swap(leave_right, 4)
        up_parts = jnp.concatenate([add(now_l[0], come_l), add(now_r[0], come_r)], axis=-1)
        up_parts, line_y = tie(up_parts, line_y)
        up_line = line_moves(up_parts, order)
        down_x, down_y = line_total(line_x), line_total(line_y)
        come_left, come_right, up_line[1:3], down_x, down_y = tie(
            come_left, come_right, up_line[1:3], down_x, down_y
        )
        left_now, right_now = add(stay_left, come_left), add(stay_right, come_right)
        come_left, come_right = swap(left_now[1], 4), swap(right_now[1], 2)
        up_line[3:], come_left, come_right, down_x, down_y = tie(
            up_line[3:], come_left, come_right, down_x, down_y
        )
        come_x, come_y = swap(down_x, 4), swap(down_y, 2)
        att_parts = jnp.concatenate(
            [add(left_now[0], come_left), add(right_now[0], come_right)], axis=-1
        )
        att_line = line_moves(att_parts, range(n_mp))
        down_x, down_y = add(down_x, come_x), add(down_y, come_y)
        come_x, come_y = swap(down_x, 2), swap(down_y, 4)
        up_total = line_total(up_line)
        (grad_tokens,) = call(
            input_backward,
            "input_backward",
            [tok_low],
            [q0, k0, v0, q1, k1, v1, grad_one, weights],
            "v" * 8,
        )
        att_line[1], come_x, come_y, up_total, grad_tokens = tie(
            att_line[1], come_x, come_y, up_total, grad_tokens
        )
        up_four = plane_swap(up_total)
        down_four = [down_x, come_x, down_y, come_y]
        att_line[2:], up_four = tie(att_line[2:], up_four)
        att_four = plane_swap(line_total(att_line))
        down_four, up_four = jnp.stack(down_four), jnp.stack(up_four)
        (grad_down,) = call(
            functools.partial(finish_ffn, places_by_axis),
            "finish_down",
            [shape((units, width), f32)],
            [index, down_four, swap(down_four, 1)],
            "svv",
        )
        (grad_up,) = call(
            functools.partial(finish_ffn, eighths),
            "finish_up",
            [shape((width, units), f32)],
            [index, up_four, swap(up_four, 1)],
            "svv",
        )
        att_four, grad_down, grad_up = tie(att_four, grad_down, grad_up)
        att_four = jnp.stack(att_four)
        att_other = swap(att_four, 1)
        grad_query, grad_key, grad_value, grad_output, query_sum, value_sum, *sums = call(
            finish_att,
            "finish_att",
            [shape((w, width), f32)] * 4
            + [shape((w,), f32)] * 2
            + [shape((width,), f32)] * (GROUP - 1),
            [index, att_four, att_other],
            "svv",
            [pltpu.VMEM((GROUP * EXTRA, width), f32), pltpu.VMEM((4 * w, width), f32)],
        )
        return (
            output,
            grad_tokens,
            grad_query.T,
            query_sum,
            grad_key.T,
            grad_value.T,
            value_sum,
            grad_output,
            sums[1],
            sums[2],
            sums[3],
            grad_up,
            sums[0],
            grad_down,
            sums[4],
            sums[5],
            sums[6],
        )

    everywhere, rows, columns, units = P(), P(("dp", "mp"), None), P(None, "mp"), P("mp")
    in_specs = (
        rows,
        P("dp", None),
        columns,
        units,
        columns,
        columns,
        units,
        P("mp", None),
        everywhere,
        everywhere,
        everywhere,
        columns,
        units,
        P("mp", None),
        everywhere,
        everywhere,
        everywhere,
        rows,
    )
    out_specs = (
        rows,
        rows,
        columns,
        units,
        columns,
        columns,
        units,
        P("mp", None),
        everywhere,
        everywhere,
        everywhere,
        columns,
        units,
        P("mp", None),
        everywhere,
        everywhere,
        everywhere,
    )
    return jax.shard_map(shards, mesh=mesh, in_specs=in_specs, out_specs=out_specs, check_vma=False)
```

```python
import functools
import math

import jax
import jax.numpy as jnp
from jax import lax
from jax.experimental import pallas as pl
from jax.experimental.pallas import tpu as pltpu
from jax.sharding import PartitionSpec as P

HEAD_DIM = 64
PASSAGE = 128
GROUP = 8
EXTRA = 8
LANES = 128
CHUNK = 128
SCOPED = {
    "first_piece": 60,
    "att_forward": 7,
    "ffn_first": 5,
    "ffn_last": 10,
    "ffn_slopes": 8,
    "ffn_grads": 5,
    "ffn_norm": 7,
    "att_backward": 11,
    "input_backward": 4,
    "finish_down": 4,
    "finish_up": 4,
    "finish_att": 6,
}
epsilon = 1e-05
bf16 = jnp.bfloat16
f32 = jnp.float32


def nn(left, right):
    return lax.dot_general(left, right, (((1,), (0,)), ((), ())), preferred_element_type=f32)


def nt(left, right):
    return lax.dot_general(left, right, (((1,), (1,)), ((), ())), preferred_element_type=f32)


def tn(left, right):
    return lax.dot_general(left, right, (((0,), (0,)), ((), ())), preferred_element_type=f32)


def call(body, name, outs, args, spaces, scratch=(), out_spaces=None):
    def spec(kind):
        if kind == "s":
            return pl.BlockSpec(memory_space=pltpu.SMEM)
        if kind == "h":
            return pl.BlockSpec(memory_space=pltpu.HBM)
        return pl.BlockSpec(memory_space=pltpu.VMEM)

    out_spaces = out_spaces or "v" * len(outs)
    def size(array):
        return math.prod(array.shape) * jnp.dtype(array.dtype).itemsize

    every = list(zip(args, spaces)) + list(zip(outs, out_spaces))
    moved = sum(size(array) for array, kind in every)
    return pl.pallas_call(
        body,
        name=name,
        out_shape=tuple(outs),
        in_specs=[spec(k) for k in spaces],
        out_specs=tuple(spec(k) for k in out_spaces),
        scratch_shapes=list(scratch),
        compiler_params=pltpu.CompilerParams(vmem_limit_bytes=SCOPED[name] << 20),
        cost_estimate=pl.CostEstimate(flops=0, bytes_accessed=moved // 64, transcendentals=0),
    )(*args)


def vector(ref):
    return ref[...].astype(f32).reshape(1, ref.shape[0])


def places_by_axis(index):
    x, y = index & 3, ((index >> 1) & 2) | (index & 1)
    return [x, x ^ 1, x ^ 2, x ^ 3, 4 + y, 4 + (y ^ 1), 4 + (y ^ 2), 4 + (y ^ 3)]


def eighths(index):
    return [index ^ s for s in range(GROUP)]


def places_gathered(index):
    places = places_by_axis(index)
    return places[:4] + places[6:] + places[4:6]


def place_slots(pieces, others, r, down_rows, rows, places, dest, base, columns):
    upper, lower = slice(0, rows), slice(rows, 2 * rows)
    sources = ((0, upper), (1, upper), (2, lower), (4, lower))
    if not down_rows:
        sources = ((0, lower), (1, lower), (2, upper), (3, upper))
    for s in range(GROUP):
        piece, part = sources[s // 2]
        at = pl.multiple_of(base + places[s] * rows, rows)
        dest[pl.ds(at, rows), columns] = (others if s % 2 else pieces)[piece][r, part]


def put_slots(index, r, rows, low, keep, send, by_axis=False):
    size = rows[0].shape[0]
    x, y = index & 3, ((index >> 1) & 2) | (index & 1)
    for odd in range(2):

        @pl.when((index & 1) == odd)
        def _():
            for d in range(GROUP):
                dest = send if (d ^ odd) & 1 else keep
                spot = (index ^ d) >> 1
                if by_axis:
                    spot = (x ^ d) >> 1 if d < 4 else 2 + ((y ^ (d - 4)) >> 1)
                dest[spot, r, low : low + size] = rows[d]


def normalize(total):
    centred = total - jnp.mean(total, axis=-1, keepdims=True)
    inverse = lax.rsqrt(jnp.mean(centred * centred, axis=-1, keepdims=True) + epsilon)
    return centred * inverse, inverse


def norm_backward(grad_out, normal, inverse, norm_gain):
    scaled = grad_out * norm_gain
    return inverse * (
        scaled
        - jnp.mean(scaled, axis=-1, keepdims=True)
        - normal * jnp.mean(scaled * normal, axis=-1, keepdims=True)
    )


def column_sum(array):
    return jnp.sum(array, axis=0, keepdims=True)


def folded(array):
    return jnp.sum(array.reshape(-1, 8, array.shape[1]), axis=0)


def by_rows(length, body, sums, width):
    def step(i, totals):
        found = body(pl.ds(pl.multiple_of(i * CHUNK, CHUNK), CHUNK))
        return tuple(t + folded(f) for t, f in zip(totals, found))

    zeros = tuple(jnp.zeros((8, width), f32) for _ in range(sums))
    totals = lax.fori_loop(0, length // CHUNK, step, zeros, unroll=1)
    return tuple(column_sum(t) for t in totals)


def band(block, length):
    return max(0, (block - 1) * PASSAGE), min(length, (block + 2) * PASSAGE)


def clear_outside(array, length):
    for b in range(length // PASSAGE):
        lo, hi = band(b, length)
        block = slice(b * PASSAGE, (b + 1) * PASSAGE)
        for low, high in ((0, lo), (hi, length)):
            if high > low:
                shape = (array.shape[0], high - low, PASSAGE)
                array[:, low:high, block] = jnp.zeros(shape, array.dtype)


def fill_bias(bias, seg_row, seg_col, length):
    for b in range(length // PASSAGE):
        lo, hi = band(b, length)
        same = seg_col[lo:hi, :] == seg_row[:, b * PASSAGE : (b + 1) * PASSAGE]
        bias[b, : hi - lo, :] = jnp.where(same, 0.0, -1e30)


def softmax_columns(scores):
    expo = jnp.exp(scores - jnp.max(scores, axis=0, keepdims=True))
    return expo * (1.0 / jnp.sum(expo, axis=0, keepdims=True))


def first_piece(
    index_ref, own_q, own_k, own_v, own_o, query_bias, value_bias, up_bias, out, owns,
    query_row, value_row, up_row, sems,
):
    w = own_q.shape[0]
    rows = w // 2
    small = [
        pltpu.make_async_copy(own, owns.at[pl.ds(m * w, w)], sems.at[3 + m])
        for m, own in enumerate((own_q, own_k, own_v, own_o))
    ]
    small += [
        pltpu.make_async_copy(query_bias, query_row, sems.at[0]),
        pltpu.make_async_copy(value_bias, value_row, sems.at[1]),
        pltpu.make_async_copy(up_bias, up_row, sems.at[2]),
    ]
    for copy in small:
        copy.start()
    for copy in small:
        copy.wait()
    out[:rows, :] = owns[pl.ds(pl.multiple_of(index_ref[0] * rows, rows), rows), :]
    out[rows:, :] = jnp.zeros((EXTRA, out.shape[1]), bf16)
    out[rows : rows + 1, :w] = vector(query_row).astype(bf16)
    out[rows : rows + 1, w : 2 * w] = vector(value_row).astype(bf16)
    out[rows + 1 : rows + 2, :] = vector(up_row).astype(bf16)


def att_forward(
    index_ref, tokens, owns, four, other, bias_0, bias_1, bias_2, bias_3,
    output_bias, seg_row, seg_col,
    queries, keys, values, contexts, normal, inverse, weights, wo,
    bias, probs_t, row, attended,
):
    length, width = tokens.shape
    w = owns.shape[0] // 4
    quarters = width // w
    rows = four.shape[2]
    index = index_ref[0]
    for m in range(3):
        weights[m, :w, :] = owns[m * w : (m + 1) * w, :]
    wo[:w, :] = owns[3 * w :, :]
    for r in range(1, quarters):
        for s in range(GROUP):
            owner = index ^ s
            at = pl.multiple_of(r * w + (owner & 1) * rows, rows)
            source = other if s % 2 else four

            @pl.when(owner < 6)
            def _():
                weights[owner >> 1, pl.ds(at, rows), :] = source[s // 2, r - 1]

            @pl.when(owner >= 6)
            def _():
                wo[pl.ds(at, rows), :] = source[s // 2, r - 1]

    fill_bias(bias, seg_row, seg_col, length)
    clear_outside(probs_t, length)
    for r, source in enumerate((bias_0, bias_1, bias_2, bias_3)):
        for i in range(2):
            piece = source[rows : rows + 1, i * w : (i + 1) * w].astype(f32)
            row[i : i + 1, r * w : (r + 1) * w] = piece
    low = (nt(tokens[...], weights[0]) + row[0:1, :]).astype(bf16)
    queries[...] = (low.astype(f32) * (HEAD_DIM**-0.5)).astype(bf16)
    keys[...] = nt(tokens[...], weights[1]).astype(bf16)
    values[...] = (nt(tokens[...], weights[2]) + row[1:2, :]).astype(bf16)
    first = lax.broadcasted_iota(jnp.int32, (PASSAGE, LANES), 1) < HEAD_DIM
    first_all = lax.broadcasted_iota(jnp.int32, (length, LANES), 1) < HEAD_DIM

    def pair(i, carry):
        at = pl.ds(pl.multiple_of(i * LANES, LANES), LANES)
        for half, mine in enumerate((first, jnp.logical_not(first))):
            for b in range(length // PASSAGE):
                lo, hi = band(b, length)
                block = slice(b * PASSAGE, (b + 1) * PASSAGE)
                q = queries[block, at]
                masked = jnp.where(mine, q, jnp.zeros_like(q))
                scores = nt(keys[lo:hi, at], masked) + bias[b, : hi - lo, :]
                probs_t[half, lo:hi, block] = softmax_columns(scores).astype(bf16)
        found = [tn(probs_t[half], values[:, at]) for half in range(2)]
        contexts[:, at] = jnp.where(first_all, *found).astype(bf16)
        return carry

    lax.fori_loop(0, width // LANES, pair, 0)
    attended[...] = nn(contexts[...], wo[...]) + vector(output_bias)

    def norm(rows):
        n, r = normalize(tokens[rows, :].astype(f32) + attended[rows, :])
        normal[rows, :] = n
        inverse[rows, :] = r
        return ()

    by_rows(length, norm, 0, width)


def gelu_rows(hidden, activated, slope, columns):
    def step(i, carry):
        rows = pl.ds(pl.multiple_of(i * CHUNK, CHUNK), CHUNK)
        value = hidden[rows, :]
        cumulative = 0.5 * (1.0 + lax.erf(value * 0.7071067811865476))
        density = jnp.exp(-0.5 * value * value) * 0.3989422804014327
        activated[rows, columns] = (value * cumulative).astype(bf16)
        slope[rows, columns] = (cumulative + value * density).astype(bf16)
        return carry

    lax.fori_loop(0, hidden.shape[0] // CHUNK, step, 0)


def each(count, body):
    def step(r, carry):
        body(r)
        return carry

    lax.fori_loop(0, count, step, 0)


def columns_of(r, size):
    return pl.ds(pl.multiple_of(r * size, LANES), size)


def ffn_first(
    index_ref, normal, gain, shift, down_bias, bias_0, bias_1, bias_2, own_up, own_down,
    left, from_x, from_y, corner, right, left_o, from_x_o, from_y_o, corner_o, right_o,
    activated, slope, low_t, mixed, up, down,
    hidden, lines, low_rows,
):
    units = own_up.shape[1]
    four = (left, from_x, from_y, corner, right)
    other = (left_o, from_x_o, from_y_o, corner_o, right_o)
    rows = corner.shape[1]
    quarters = corner.shape[0] + 1
    biases = (bias_0, bias_1, bias_2)
    up_places, down_places = eighths(index_ref[0]), places_gathered(index_ref[0])
    normed = normal[...] * vector(gain) + vector(shift)
    low = normed.astype(bf16)
    low_t[...] = low.T
    low_rows[...] = low
    mixed[...] = normed + vector(down_bias)
    for r in range(quarters):
        mine = slice(r * units, (r + 1) * units)
        if r == 0:
            up[:, mine] = own_up[...]
            down[mine, :] = own_down[...]
        else:
            place_slots(four, other, r - 1, False, rows, up_places, up, 0, mine)
            place_slots(four, other, r - 1, True, rows, down_places, down, r * units, slice(None))
        at = biases[r].shape[0] - EXTRA + 1
        lines[r, :, :] = jnp.broadcast_to(biases[r][at : at + 1, :].astype(f32), lines.shape[1:])

    def quarter(r):
        mine = columns_of(r, units)
        hidden[...] = nn(low_rows[...], up[:, mine]) + lines[r, 0:1, :]
        gelu_rows(hidden, activated, slope, mine)

    each(quarters, quarter)
    mixed[...] += nn(activated[...], down[...])


def ffn_last(
    index_ref, normal, cotangent, gain, shift, second_gain, second_shift, bias, activated, mixed,
    left, from_x, from_y, corner, right, left_o, from_x_o, from_y_o, corner_o, right_o,
    output, grad_mixed, grad_two, sums, slope, up, down, keep, send,
    own, total,
):
    length, width = normal.shape
    units = up.shape[1]
    four = (left, from_x, from_y, corner, right)
    other = (left_o, from_x_o, from_y_o, corner_o, right_o)
    rows = corner.shape[1]
    index = index_ref[0]
    place_slots(four, other, 0, False, rows, eighths(index), up, 0, slice(None))
    place_slots(four, other, 0, True, rows, places_gathered(index), down, 0, slice(None))
    low = (normal[...] * vector(gain) + vector(shift)).astype(bf16)
    at = bias.shape[0] - EXTRA + 1
    total[...] = nn(low, up[...]) + bias[at : at + 1, :].astype(f32)
    gelu_rows(total, own, slope, slice(None))
    total[...] = mixed[...] + nn(own[...], down[...])
    out_gain, out_shift = vector(second_gain), vector(second_shift)

    def norm(rows):
        n, inverse = normalize(total[rows, :])
        output[rows, :] = (n * out_gain + out_shift).astype(bf16)
        grad_out = cotangent[rows, :].astype(f32)
        two = norm_backward(grad_out, n, inverse, out_gain)
        grad_two[rows, :] = two
        low = two.astype(bf16)
        grad_mixed[rows, :] = low
        return low.astype(f32), grad_out * n, grad_out

    sums[...] = jnp.zeros_like(sums)
    for i, found in enumerate(by_rows(length, norm, 3, width)):
        sums[i : i + 1, :] = found

    def put(r, left):
        grad = tn(left, grad_mixed[...]).astype(bf16)
        put_slots(index, r, grad.reshape(GROUP, -1, width), 0, keep, send, True)

    each(keep.shape[1] - 1, lambda r: put(r, activated[:, columns_of(r, units)]))
    put(keep.shape[1] - 1, own[...])


def ffn_slopes(grad_mixed, slope, slope_last, down, down_last, hidden, sums):
    units = down_last.shape[0]
    sums[...] = jnp.zeros_like(sums)

    def quarter(r, weight, factor):
        low = (nt(grad_mixed[...], weight) * factor.astype(f32)).astype(bf16)
        hidden[:, columns_of(r, units)] = low
        sums[pl.ds(r, 1), :] = column_sum(low.astype(f32))

    def inner(r):
        mine = columns_of(r, units)
        quarter(r, down[mine, :], slope[:, mine])

    for r in range(down.shape[0] // units):
        inner(r)
    quarter(down.shape[0] // units, down_last[...], slope_last[...])


def ffn_grads(index_ref, hidden, low_t, keep, send):
    units = keep.shape[3]

    def quarter(r):
        grad = nn(low_t[...], hidden[:, columns_of(r, units)]).astype(bf16)
        put_slots(index_ref[0], r, grad.reshape(GROUP, -1, units), 0, keep, send)

    each(keep.shape[1], quarter)


def ffn_norm(
    hidden, grad_two, normal, inverse, gain_ref, up, up_last,
    grad_one, grad_attended, sums,
    total,
):
    length, width = normal.shape
    inner = up.shape[1]
    total[...] = nt(hidden[:, :inner], up[...]) + grad_two[...]
    total[...] += nt(hidden[:, inner:], up_last[...])
    gain = vector(gain_ref)

    def norm(at):
        grad_normed = total[at, :]
        n = normal[at, :]
        one = norm_backward(grad_normed, n, inverse[at, :], gain)
        grad_one[at, :] = one
        low = one.astype(bf16)
        grad_attended[at, :] = low
        return low.astype(f32), grad_normed * n, grad_normed

    sums[...] = jnp.zeros_like(sums)
    for i, found in enumerate(by_rows(length, norm, 3, width)):
        sums[i : i + 1, :] = found


def att_backward(
    part, places, index_ref, queries, keys, values, contexts, grad_attended, tokens, wo,
    seg_row, seg_col, unit_sums, sums_one, sums_two,
    grad_queries, grad_keys, grad_values, keep, send,
    grad_contexts, bias, probs_t, scores_t,
):
    length, width = tokens.shape
    quarters, rows = keep.shape[1], keep.shape[2] - EXTRA
    w = 2 * rows
    across = quarters * w
    index = index_ref[0]
    scale = HEAD_DIM**-0.5
    fill_bias(bias, seg_row, seg_col, length)
    clear_outside(probs_t, length)
    clear_outside(scores_t, length)
    low = part * across
    grad_contexts[...] = nt(grad_attended[...], wo[low : low + across, :]).astype(bf16)
    lane = lax.broadcasted_iota(jnp.int32, (PASSAGE, LANES), 1) // HEAD_DIM
    lane_all = lax.broadcasted_iota(jnp.int32, (length, LANES), 1) // HEAD_DIM

    def head(i, carry):
        half = i & 1
        here = pl.ds(pl.multiple_of((i >> 1) * LANES, LANES), LANES)
        at = pl.ds(pl.multiple_of(low + (i >> 1) * LANES, LANES), LANES)
        mine = lane == half
        for b in range(length // PASSAGE):
            lo, hi = band(b, length)
            block = slice(b * PASSAGE, (b + 1) * PASSAGE)
            q = queries[block, at]
            g = grad_contexts[block, here]
            zero = jnp.zeros_like(q)
            scores = nt(keys[lo:hi, at], jnp.where(mine, q, zero)) + bias[b, : hi - lo, :]
            probs = softmax_columns(scores)
            grad_probs = nt(values[lo:hi, at], jnp.where(mine, g, zero))
            inner = jnp.sum(grad_probs * probs, axis=0, keepdims=True)
            probs_t[0, lo:hi, block] = probs.astype(bf16)
            scores_t[0, lo:hi, block] = (probs * (grad_probs - inner)).astype(bf16)
        mine = lane_all == half
        for out, found in (
            (grad_queries, tn(scores_t[0], keys[:, at]) * scale),
            (grad_keys, nn(scores_t[0], queries[:, at])),
            (grad_values, nn(probs_t[0], grad_contexts[:, here])),
        ):
            out[:, here] = jnp.where(mine, found.astype(bf16), out[:, here])
        return carry

    lax.fori_loop(0, across // HEAD_DIM, head, 0)
    grads = (
        lambda: tn(grad_queries[...], tokens[...]),
        lambda: tn(grad_keys[...], tokens[...]),
        lambda: tn(grad_values[...], tokens[...]),
        lambda: tn(contexts[:, low : low + across], grad_attended[...]),
    )
    grads = [make().astype(bf16).reshape(quarters, 2, rows, width) for make in grads]
    query_sum = column_sum(grad_queries[...].astype(f32))
    value_sum = column_sum(grad_values[...].astype(f32))
    for r in range(quarters):
        put_slots(index, r, [grads[d // 2][r, d % 2] for d in range(GROUP)], 0, keep, send)
        cols = slice(r * w, (r + 1) * w)
        last = jnp.concatenate(
            [query_sum[:, cols], value_sum[:, cols], jnp.zeros((1, width - 2 * w), f32)], axis=1
        )
        at = places[part * quarters + r]
        lines = [unit_sums[at : at + 1, :]]
        lines += [sums[i : i + 1, :] for sums in (sums_one, sums_two) for i in range(3)]
        lines = [jnp.broadcast_to(line, (EXTRA, width)).astype(bf16) for line in lines + [last]]
        put_slots(index, r, lines, rows, keep, send)


def input_backward(q0, k0, v0, q1, k1, v1, grad_one, weights, out):
    half = q0.shape[1]
    total = grad_one[...]
    for m, (left, right) in enumerate(((q0, q1), (k0, k1), (v0, v1))):
        total += nn(left[...], weights[m, :half]) + nn(right[...], weights[m, half:])
    out[...] = total.astype(bf16)


def finish_ffn(places_of, index_ref, four, other, out):
    rows = four.shape[1]
    for s, place in enumerate(places_of(index_ref[0])):
        at = pl.multiple_of(place * rows, rows)
        out[pl.ds(at, rows), :] = (other if s % 2 else four)[s // 2].astype(f32)


def finish_att(index_ref, four, other, gq, gk, gv, go, query_sum, value_sum, *rest):
    sums, whole = rest[:-2], rest[-1]
    lines = rest[-2]
    rows = four.shape[1] - EXTRA
    w = 2 * rows
    for s in range(GROUP):
        slot = (other if s % 2 else four)[s // 2].astype(f32)
        owner = index_ref[0] ^ s
        whole[pl.ds(pl.multiple_of(owner * rows, rows), rows), :] = slot[:rows]
        lines[pl.ds(pl.multiple_of(owner * EXTRA, EXTRA), EXTRA), :] = slot[rows:]
    for m, out in enumerate((gq, gk, gv, go)):
        out[...] = whole[m * w : (m + 1) * w, :]
    for j, out in enumerate(sums):
        out[...] = lines[j * EXTRA, :]
    last = len(sums) * EXTRA
    query_sum[...] = lines[last, :w]
    value_sum[...] = lines[last, w : 2 * w]


def solution(mesh):
    n_dp, n_mp = mesh.shape["dp"], mesh.shape["mp"]
    if n_dp % GROUP or n_mp % 2:
        raise ValueError("mesh")

    def rotate(array, step):
        return lax.ppermute(array, "mp", [(i, (i + step) % n_mp) for i in range(n_mp)])

    def swap(array, bits):
        return lax.ppermute(array, "dp", [(i, i ^ bits) for i in range(n_dp)])

    def plane_swap(array):
        return [array, swap(array, 2), swap(array, 4), swap(array, 6)]

    def add(left, right):
        return (left.astype(f32) + right.astype(f32)).astype(bf16)

    def tie(*arrays):
        return lax.optimization_barrier(arrays)

    def after(array, *others):
        return tie(array, *others)[0]

    def first_axis(bits):
        go = slice(1, None, 2) if bits == 2 else slice(2, None)
        stay = slice(0, None, 2) if bits == 2 else slice(0, 2)
        return go, stay

    def plane_first(keep, got, bits):
        go, stay = first_axis(bits)
        return add(keep[go], got[go]), add(keep[stay], got[stay])

    def line_moves(parts, order):
        found = {r: rotate(parts[i], -r) if r else parts[i] for i, r in enumerate(order)}
        return [found[r] for r in range(n_mp)]

    def line_total(moved):
        moved = [array.astype(f32) for array in moved]
        total = sum(moved[0::2][1:], moved[0]) + sum(moved[1::2][1:], moved[1])
        if n_dp > GROUP:
            groups = [[i + GROUP * k for k in range(n_dp // GROUP)] for i in range(GROUP)]
            total = lax.psum(total, "dp", axis_index_groups=groups)
        return total.astype(bf16)

    def shards(
        tokens,
        segment_ids,
        query_weight,
        query_bias,
        key_weight,
        value_weight,
        value_bias,
        output_weight,
        output_bias,
        first_gain,
        first_shift,
        up_weight,
        up_bias,
        down_weight,
        down_bias,
        second_gain,
        second_shift,
        cotangent,
    ):
        length, width = tokens.shape
        w = query_weight.shape[1]
        units = up_weight.shape[1]
        rows = width // GROUP
        blocks = length // PASSAGE
        half, part = GROUP // 2, units // GROUP
        shape = jax.ShapeDtypeStruct
        place = lax.axis_index("mp")
        within = lax.axis_index("dp") % GROUP
        index = within.astype(jnp.int32).reshape(1)
        seg_row = lax.dynamic_slice_in_dim(segment_ids, place, 1, 0)
        seg_col = seg_row.reshape(length, 1)

        def slot(array, at, size):
            return lax.dynamic_slice_in_dim(array, at * size, size, 0)

        owns = [query_weight.T, key_weight.T, value_weight.T, output_weight]
        piece, owns = call(
            first_piece,
            "first_piece",
            [shape((rows + EXTRA, width), bf16), shape((4 * w, width), bf16)],
            [index, *owns, query_bias, value_bias, up_bias],
            "s" + "h" * 7,
            [
                pltpu.VMEM((w,), bf16),
                pltpu.VMEM((w,), bf16),
                pltpu.VMEM((units,), bf16),
                pltpu.SemaphoreType.DMA((7,)),
            ],
        )
        biases = [piece] + [rotate(piece, r) for r in range(1, n_mp)]
        order = [r for r in range(n_mp) if r != n_mp // 2] + [n_mp // 2]
        ffn_biases = [biases[r] for r in order]
        att_line = jnp.stack([g[:rows] for g in biases[1:]])
        by_x, by_y = within & 3, ((within >> 1) & 2) | (within & 1)
        piece = jnp.concatenate(
            [
                slot(down_weight, by_x, part),
                slot(up_weight, within, rows),
                slot(down_weight, 4 + by_y, part),
            ]
        )
        piece, att_line = tie(piece, att_line)
        ffn_line = [rotate(piece, r) for r in order[1:]]

        def plane_mixed(line):
            left = jnp.stack([g[: part + rows] for g in line])
            right = jnp.stack([g[part:] for g in line])
            corner = swap(jnp.stack([g[part : part + rows] for g in line]), 6)
            return left, swap(left, 2), swap(right, 4), corner, right

        att_four = [att_line] + [swap(att_line, b) for b in (2, 4, 6)]
        att_four, ffn_line[:-1] = tie(att_four, ffn_line[:-1])
        att_four = jnp.stack(att_four)
        att_other = swap(att_four, 1)
        ffn_four = plane_mixed(ffn_line[:-1])
        tok_low = shape((length, width), bf16)
        tok_wide = shape((length, width), f32)
        queries, keys, values, contexts, normal, inverse, weights, wo = call(
            att_forward,
            "att_forward",
            [tok_low] * 4
            + [
                tok_wide,
                shape((length, 1), f32),
                shape((3, n_mp * w, width), bf16),
                shape((n_mp * w, width), bf16),
            ],
            [
                index,
                tokens,
                owns,
                att_four,
                att_other,
                *biases,
                output_bias,
                seg_row,
                seg_col,
            ],
            "s" + "v" * 11,
            [
                pltpu.VMEM((blocks, 3 * PASSAGE, PASSAGE), f32),
                pltpu.VMEM((2, length, length), bf16),
                pltpu.VMEM((8, width), f32),
                pltpu.VMEM((length, width), f32),
            ],
        )
        normal, ffn_four, ffn_line[-1] = tie(normal, ffn_four, ffn_line[-1])
        ffn_other = [swap(array, 1) for array in ffn_four]
        last_four = plane_mixed(ffn_line[-1:])
        inner = (n_mp - 1) * units
        hidden_low = shape((length, inner), bf16)
        activated, slope, low_t, mixed, up, down = call(
            ffn_first,
            "ffn_first",
            [
                hidden_low,
                hidden_low,
                shape((width, length), bf16),
                tok_wide,
                shape((width, inner), bf16),
                shape((inner, width), bf16),
            ],
            [
                index,
                normal,
                first_gain,
                first_shift,
                down_bias,
                *ffn_biases[:-1],
                up_weight,
                down_weight,
                *ffn_four,
                *ffn_other,
            ],
            "s" + "v" * 19,
            [
                pltpu.VMEM((length, units), f32),
                pltpu.VMEM((n_mp, 8, units), f32),
                pltpu.VMEM((length, width), bf16),
            ],
        )
        activated, last_four = tie(activated, last_four)
        last_other = [swap(array, 1) for array in last_four]
        pieces = shape((half, n_mp, part, width), bf16)
        (
            output,
            grad_mixed,
            grad_two,
            sums_two,
            slope_last,
            up_last,
            down_last,
            keep_down,
            send_down,
        ) = call(
            ffn_last,
            "ffn_last",
            [
                tok_low,
                tok_low,
                tok_wide,
                shape((8, width), f32),
                shape((length, units), bf16),
                shape((width, units), bf16),
                shape((units, width), bf16),
                pieces,
                pieces,
            ],
            [
                index,
                normal,
                cotangent,
                first_gain,
                first_shift,
                second_gain,
                second_shift,
                ffn_biases[-1],
                activated,
                mixed,
                *last_four,
                *last_other,
            ],
            "s" + "v" * 19,
            [pltpu.VMEM((length, units), bf16), pltpu.VMEM((length, width), f32)],
        )
        got_down = swap(send_down, 1)
        hidden, low_sums = call(
            ffn_slopes,
            "ffn_slopes",
            [shape((length, n_mp * units), bf16), shape((8, units), f32)],
            [grad_mixed, slope, slope_last, down, down_last],
            "v" * 5,
        )
        hidden, got_down = tie(hidden, got_down)
        leave_x, leave_y = add(keep_down[1], got_down[1]), add(keep_down[3], got_down[3])
        stay_x, stay_y = add(keep_down[0], got_down[0]), add(keep_down[2], got_down[2])
        hidden, leave_x, leave_y = tie(hidden, leave_x, leave_y)
        come_x, come_y = swap(leave_x, 2), swap(leave_y, 4)
        pieces = shape((half, n_mp, rows, units), bf16)
        keep_up, send_up = call(
            ffn_grads, "ffn_grads", [pieces, pieces], [index, hidden, low_t], "svv"
        )
        hidden, keep_up, send_up = tie(hidden, keep_up, send_up)
        got_up = swap(send_up, 1)
        grad_one, grad_attended, sums_one = call(
            ffn_norm,
            "ffn_norm",
            [tok_wide, tok_low, shape((8, width), f32)],
            [hidden, grad_two, normal, inverse, first_gain, up, up_last],
            "v" * 7,
            [pltpu.VMEM((length, width), f32)],
        )
        grad_attended, sums_one, got_up = tie(grad_attended, sums_one, got_up)
        cut = units // 2
        left, right = slice(0, cut), slice(cut, None)

        def plane_halves(keep, got):
            leaves = add(keep[1::2, ..., left], got[1::2, ..., left])
            leaves_r = add(keep[2:, ..., right], got[2:, ..., right])
            stays = add(keep[0::2, ..., left], got[0::2, ..., left])
            stays_r = add(keep[:2, ..., right], got[:2, ..., right])
            return leaves, leaves_r, stays, stays_r

        leave_l, leave_r, stay_l, stay_r = plane_halves(keep_up, got_up)
        grad_attended, leave_l, leave_r = tie(grad_attended, leave_l, leave_r)
        come_l, come_r = swap(leave_l, 2), swap(leave_r, 4)
        halves = n_mp // 2
        across = halves * w
        pieces = shape((half, halves, rows + EXTRA, width), bf16)
        places = [order.index(r) for r in range(n_mp)]

        def attention(which, grad_attended):
            return call(
                functools.partial(att_backward, which, places),
                "att_backward",
                [shape((length, across), bf16)] * 3 + [pieces] * 2,
                [
                    index,
                    queries,
                    keys,
                    values,
                    contexts,
                    grad_attended,
                    tokens,
                    wo,
                    seg_row,
                    seg_col,
                    low_sums,
                    sums_one,
                    sums_two,
                ],
                "s" + "v" * 12,
                [
                    pltpu.VMEM((length, across), bf16),
                    pltpu.VMEM((blocks, 3 * PASSAGE, PASSAGE), f32),
                    pltpu.VMEM((1, length, length), bf16),
                    pltpu.VMEM((1, length, length), bf16),
                ],
            )

        q0, k0, v0, keep_0, send_0 = attention(0, grad_attended)
        come_x, come_y, q0, k0, v0, keep_0, send_0 = tie(
            come_x, come_y, q0, k0, v0, keep_0, send_0
        )
        got_0 = swap(send_0, 1)
        parts_x, parts_y = add(stay_x, come_x), add(stay_y, come_y)
        grad_attended, parts_x, got_0 = tie(grad_attended, parts_x, got_0)
        line_x = line_moves(parts_x, order)
        q1, k1, v1, keep_1, send_1 = attention(1, grad_attended)
        q1, k1, v1, keep_1, send_1, come_l, come_r, line_x[1:], parts_y = tie(
            q1, k1, v1, keep_1, send_1, come_l, come_r, line_x[1:], parts_y
        )
        got_1 = swap(send_1, 1)
        line_y = line_moves(parts_y, order)
        now_l, now_r = add(stay_l, come_l), add(stay_r, come_r)
        come_l, come_r = swap(now_l[1], 4), swap(now_r[1], 2)
        keep_att = jnp.concatenate([keep_0, keep_1], axis=1)
        got_att = jnp.concatenate([got_0, got_1], axis=1)
        leave_left, leave_right, stay_left, stay_right = plane_halves(keep_att, got_att)
        come_l, come_r, leave_left, leave_right = tie(come_l, come_r, leave_left, leave_right)
        come_left, come_right = swap(leave_left, 2), swap(leave_right, 4)
        up_parts = jnp.concatenate([add(now_l[0], come_l), add(now_r[0], come_r)], axis=-1)
        up_parts, line_y = tie(up_parts, line_y)
        up_line = line_moves(up_parts, order)
        down_x, down_y = line_total(line_x), line_total(line_y)
        come_left, come_right, up_line[1:3], down_x, down_y = tie(
            come_left, come_right, up_line[1:3], down_x, down_y
        )
        left_now, right_now = add(stay_left, come_left), add(stay_right, come_right)
        come_left, come_right = swap(left_now[1], 4), swap(right_now[1], 2)
        come_left, come_right, down_x, down_y = tie(come_left, come_right, down_x, down_y)
        come_x, come_y = swap(down_x, 4), swap(down_y, 2)
        att_parts = jnp.concatenate(
            [add(left_now[0], come_left), add(right_now[0], come_right)], axis=-1
        )
        att_line = line_moves(att_parts, range(n_mp))
        down_x, down_y = add(down_x, come_x), add(down_y, come_y)
        come_x, come_y = swap(down_x, 2), swap(down_y, 4)
        up_total = line_total(up_line)
        (grad_tokens,) = call(
            input_backward,
            "input_backward",
            [tok_low],
            [q0, k0, v0, q1, k1, v1, grad_one, weights],
            "v" * 8,
        )
        att_line[1], come_x, come_y, up_total, grad_tokens = tie(
            att_line[1], come_x, come_y, up_total, grad_tokens
        )
        up_four = plane_swap(up_total)
        down_four = [down_x, come_x, down_y, come_y]
        att_line[2:], up_four = tie(att_line[2:], up_four)
        att_four = plane_swap(line_total(att_line))
        down_four, up_four = jnp.stack(down_four), jnp.stack(up_four)
        (grad_down,) = call(
            functools.partial(finish_ffn, places_by_axis),
            "finish_down",
            [shape((units, width), f32)],
            [index, down_four, swap(down_four, 1)],
            "svv",
        )
        (grad_up,) = call(
            functools.partial(finish_ffn, eighths),
            "finish_up",
            [shape((width, units), f32)],
            [index, up_four, swap(up_four, 1)],
            "svv",
        )
        att_four, grad_down, grad_up = tie(att_four, grad_down, grad_up)
        att_four = jnp.stack(att_four)
        att_other = swap(att_four, 1)
        grad_query, grad_key, grad_value, grad_output, query_sum, value_sum, *sums = call(
            finish_att,
            "finish_att",
            [shape((w, width), f32)] * 4
            + [shape((w,), f32)] * 2
            + [shape((width,), f32)] * (GROUP - 1),
            [index, att_four, att_other],
            "svv",
            [pltpu.VMEM((GROUP * EXTRA, width), f32), pltpu.VMEM((4 * w, width), f32)],
        )
        return (
            output,
            grad_tokens,
            grad_query.T,
            query_sum,
            grad_key.T,
            grad_value.T,
            value_sum,
            grad_output,
            sums[1],
            sums[2],
            sums[3],
            grad_up,
            sums[0],
            grad_down,
            sums[4],
            sums[5],
            sums[6],
        )

    everywhere, rows, columns, units = P(), P(("dp", "mp"), None), P(None, "mp"), P("mp")
    in_specs = (
        rows,
        P("dp", None),
        columns,
        units,
        columns,
        columns,
        units,
        P("mp", None),
        everywhere,
        everywhere,
        everywhere,
        columns,
        units,
        P("mp", None),
        everywhere,
        everywhere,
        everywhere,
        rows,
    )
    out_specs = (
        rows,
        rows,
        columns,
        units,
        columns,
        columns,
        units,
        P("mp", None),
        everywhere,
        everywhere,
        everywhere,
        columns,
        units,
        P("mp", None),
        everywhere,
        everywhere,
        everywhere,
    )
    return jax.shard_map(shards, mesh=mesh, in_specs=in_specs, out_specs=out_specs, check_vma=False)
```
